256 devices in a mesh: seq: 4 (over y), head: 64 (over x, z, core).
Axes of the slice: x: 4, y: 4, z: 8, core: 2. Of those that a mesh axis runs over, the one named last changes fastest.
Arguments:
- pre_x: bfloat16 [4096, 8192], P('seq', 'head'), may hold values from -6 to 6
- pre_bc: bfloat16 [4096, 256], P('seq'), may hold values from -6 to 6
- conv_x: float32 [4, 8192], P(None, 'head'), may hold values from -3 to 3
- conv_bc: float32 [4, 256], replicated, may hold values from -3 to 3
- log_decay: float32 [128, 4096], P('head', 'seq'), may hold values from -1.5 to 0
- lengths: int32 [4], replicated, may hold values from 1 to 2048, 4096 in all
- grad_out: bfloat16 [4096, 8192], P('seq', 'head'), may hold values from -0.3125 to 0.3125
Outputs:
- grad_pre_x: float32 [4096, 8192], P('seq', 'head')
- grad_pre_bc: float32 [4096, 256], P(('seq', 'head'))
- grad_log_decay: float32 [128, 4096], P('head', 'seq')
The draws below stay inside these ranges and needn't reach their ends.
Inputs may be any that keep to these rules, and one draw needn't show every extreme that they name: `lengths`: the 4 counts sum to 4096.
All inputs are finite; a program needn't handle non-finite values.
Results may differ from the reference program's by a relative error of at most 0.0003.
Values may be sent and summed in bfloat16 or wider, within the bound.
A program may use at most 64 MiB of HBM per device.

```python
import math
import jax
import jax.numpy as jnp
import numpy as np
from jax import lax

HEAD_COUNT_TOTAL = 128
P_SIZE = 64
N = 128
K = 4
NOTES = 4
BLOCK = 256
PACKED_LENGTH = 4096
HP = 8192


def draw_log_decay(key, part):
    random_keys = jax.random.split(jax.random.fold_in(key, 7), 6)
    slow_share = 0.5
    slow = jax.random.uniform(random_keys[0], (HEAD_COUNT_TOTAL,)) < slow_share
    slow_rate = jnp.exp(jax.random.uniform(random_keys[1], (HEAD_COUNT_TOTAL,), jnp.float32, jnp.log(0.1), jnp.log(1.0))) / PACKED_LENGTH
    fast_rate = jnp.exp(jax.random.uniform(random_keys[2], (HEAD_COUNT_TOTAL,), jnp.float32, jnp.log(1.0 / 50.0), jnp.log(1.0 / 30.0)))
    decay_speed = jnp.where(slow, slow_rate, fast_rate)
    coarse_value = jnp.exp(jax.random.uniform(random_keys[3], (HEAD_COUNT_TOTAL, PACKED_LENGTH), jnp.float32, jnp.log(0.5), jnp.log(2.0)))
    cluster_locations = jax.random.randint(random_keys[4], (6,), 0, PACKED_LENGTH)
    cluster_loss = jax.random.uniform(random_keys[5], (HEAD_COUNT_TOTAL, 6), jnp.float32, 0.2, 0.5)
    locations = jnp.arange(PACKED_LENGTH)
    cluster_groups = jnp.zeros((HEAD_COUNT_TOTAL, PACKED_LENGTH), jnp.float32)
    for token_index in range(6):
        matched = (locations == cluster_locations[token_index]).astype(jnp.float32)
        cluster_groups = cluster_groups + jnp.log(1.0 - cluster_loss[:, token_index])[:, None] * matched[None, :]
    return (-(decay_speed[:, None] * coarse_value) + cluster_groups).astype(jnp.float32)


def strengthened(array, stream_key, source, target, blocks, factor):
    def block_of(position):
        return (jnp.arange(array.shape[position]) // (array.shape[position] // blocks)).reshape((-1,) + (1,) * (array.ndim - 1 - position))

    one_side = jax.random.permutation(stream_key, blocks)[block_of(target)]
    second = (block_of(target) + blocks // 2) % blocks
    return jnp.where((block_of(source) == one_side) | (block_of(source) == second), factor * array, array)


def level_of(stream_key, shape, shards, smallest, top_value):
    loudness, own = 1.0, jax.random.fold_in(stream_key, 6)
    for position, blocks in shards:
        heights = jnp.exp(jax.random.uniform(jax.random.fold_in(own, position), (blocks,), jnp.float32, smallest / len(shards), top_value / len(shards)))
        loudness = loudness * jnp.repeat(heights, shape[position] // blocks).reshape([-1 if axis == position else 1 for axis in range(len(shape))])
    return loudness


def profile(count, total, most, skew):
    weights = [(1 << 20) // math.isqrt(rank ** skew) + 1 for rank in range(2, count + 1)]
    spare, counts = total - most - (count - 1), [1] * (count - 1)
    while spare > 0:
        candidates = [i for i in range(count - 1) if counts[i] < most]
        whole, left = sum([weights[i] for i in candidates]), spare
        for i in candidates:
            addition = min(most - counts[i], max(1, left * weights[i] // whole), spare)
            counts[i] = counts[i] + addition
            spare = spare - addition
    return np.array([most] + counts)


def ragged(stream_key, number_of, total, most, slope):
    if number_of == 2:
        one = jax.random.randint(stream_key, (), max(1, total - most), min(most, total - 1) + 1)
        return jnp.stack([one, total - one])
    tallies = jnp.asarray(profile(number_of, total, most, slope), jnp.int32)
    couples = (number_of - 1) // 2
    donor, receiver = tallies[1:1 + 2 * couples:2], tallies[2:2 + 2 * couples:2]
    slack = jnp.minimum(donor - 1, most - receiver)
    moved = jax.random.randint(jax.random.fold_in(stream_key, 1), (couples,), 0, 1 << 20) % (slack + 1)
    tallies = tallies.at[1:1 + 2 * couples:2].set(donor - moved).at[2:2 + 2 * couples:2].set(receiver + moved)
    return tallies[jax.random.permutation(jax.random.fold_in(stream_key, 2), number_of)]


def normal_values(own_key, shape, scale, most, cuts=(), held_as=jnp.bfloat16):
    values = jax.random.normal(own_key, shape, jnp.float32) * scale
    if len(cuts) > 0:
        values = level_of(own_key, shape, cuts, -0.22, 0.18) * values
    return jnp.clip(values, min=-most, max=most).astype(held_as)


def bell_draw_with(stream_key, dims, spread, reach, cuts, heavy, held_as=jnp.bfloat16):
    values = spread * jax.random.normal(stream_key, dims, jnp.float32)
    if cuts:
        values = values * level_of(stream_key, dims, cuts, -0.22, 0.18)
    return jnp.clip(strengthened(values, jax.random.fold_in(stream_key, 3), *heavy), -reach, reach).astype(held_as)


def setup_inputs(seed: int = 0) -> dict:
    arg_keys = jax.random.split(jax.random.key(seed), 8)
    return {
        "pre_x": normal_values(arg_keys[0], (PACKED_LENGTH, HP), 1.0, 6.0, ((0, 4), (1, 64))),
        "pre_bc": normal_values(arg_keys[1], (PACKED_LENGTH, 2 * N), 1.0, 6.0, ((0, 4),)),
        "conv_x": normal_values(arg_keys[2], (K, HP), 0.5, 3.0, ((1, 64),), jnp.float32),
        "conv_bc": normal_values(arg_keys[3], (K, 2 * N), 0.5, 3.0, (), jnp.float32),
        "log_decay": draw_log_decay(jax.random.fold_in(arg_keys[7], 71), 0),
        "lengths": ragged(arg_keys[5], NOTES, PACKED_LENGTH, PACKED_LENGTH // 2, 2).astype(jnp.int32),
        "grad_out": bell_draw_with(arg_keys[6], (PACKED_LENGTH, HP), 0.02, 0.3125, ((0, 4), (1, 64)), (1, 0, 64, 4.0)),
    }


precise = lax.Precision.HIGHEST

def matmul(left, right):
    return jnp.dot(left, right, precision=precise, preferred_element_type=jnp.float32)

def note_index(positions, lengths):
    starts = jnp.cumsum(lengths) - lengths
    hits = (positions[:, None] >= starts[None, :]).astype(jnp.int32)
    return (lax.optimization_barrier(jnp.sum(hits, axis=1)) - 1).astype(jnp.int32)

def block_edges(log_block, note_block, note_before):
    cumul = jnp.cumsum(log_block)
    entry = jnp.exp(cumul) * (note_block == note_before)
    leave = jnp.exp(cumul[-1] - cumul) * (note_block == note_block[-1])
    through = jnp.exp(cumul[-1]) * (note_block[-1] == note_before)
    return (cumul, entry, leave, through)

def block_forward(state, x_block, b_block, c_block, log_block, note_block, note_before):
    cumul, entry, leave, through = block_edges(log_block, note_block, note_before)
    length = note_block.shape[0]
    lower = jnp.arange(length)[:, None] >= jnp.arange(length)[None, :]
    linked = lower & (note_block[:, None] == note_block[None, :])
    decay_matrix = jnp.exp(jnp.where(linked, cumul[:, None] - cumul[None, :], 0.0)) * linked
    scores = matmul(c_block, b_block.T) * decay_matrix
    output = matmul(scores, x_block) + entry[:, None] * matmul(c_block, state.T)
    updated = through * state + matmul((x_block * leave[:, None]).T, b_block)
    return (output, updated)

def head_forward(state, x_head, b_blocks, c_blocks, log_head, note_blocks, befores):

    def advance(carry, block):
        output, updated = block_forward(carry, *block)
        return (updated, output)
    final, outputs = lax.scan(advance, state, (x_head, b_blocks, c_blocks, log_head, note_blocks, befores))
    return (outputs, final)

def conv_forward(extended, weights, note_ext):
    width = weights.shape[0]
    count = extended.shape[0] - width + 1
    result = jnp.zeros((count, extended.shape[1]), jnp.float32)
    for k in range(width):
        linked = note_ext[k:k + count] == note_ext[width - 1:width - 1 + count]
        result = result + weights[k][None, :] * extended[k:k + count] * linked[:, None]
    return result

def reference(pre_x, pre_bc, conv_x, conv_bc, log_decay, lengths, grad_out):
    rim_width = K - 1
    note_ext = note_index(jnp.arange(-rim_width, PACKED_LENGTH).astype(jnp.int32), lengths)
    note_ids = note_ext[rim_width:]
    block_count = PACKED_LENGTH // BLOCK
    note_blocks = note_ids.reshape(block_count, BLOCK)
    befores = jnp.concatenate([jnp.full((1,), -1, jnp.int32), note_blocks[:-1, -1]])

    def forward(in_x, in_bc, log_rates):
        pad_x = jnp.zeros((rim_width, in_x.shape[1]), jnp.float32)
        pad_bc = jnp.zeros((rim_width, in_bc.shape[1]), jnp.float32)
        u_x = conv_forward(jnp.concatenate([pad_x, in_x]), conv_x, note_ext)
        u_bc = conv_forward(jnp.concatenate([pad_bc, in_bc]), conv_bc, note_ext)
        v_x = jax.nn.silu(u_x)
        v_bc = jax.nn.silu(u_bc)
        x_heads = v_x.reshape(block_count, BLOCK, HEAD_COUNT_TOTAL, P_SIZE).transpose(2, 0, 1, 3)
        b_blocks = v_bc[:, :N].reshape(block_count, BLOCK, N)
        c_blocks = v_bc[:, N:].reshape(block_count, BLOCK, N)
        log_blocks = log_rates.reshape(HEAD_COUNT_TOTAL, block_count, BLOCK)

        def one_head(paired):
            start_state = jnp.zeros((P_SIZE, N), jnp.float32)
            return head_forward(start_state, paired[0], b_blocks, c_blocks, paired[1], note_blocks, befores)[0]
        outputs = lax.map(jax.checkpoint(one_head), (x_heads, log_blocks))
        return outputs.transpose(1, 2, 0, 3).reshape(PACKED_LENGTH, HEAD_COUNT_TOTAL * P_SIZE)
    _, pull = jax.vjp(forward, pre_x.astype(jnp.float32), pre_bc.astype(jnp.float32), log_decay)
    grad_x, grad_bc, grad_log = pull(grad_out.astype(jnp.float32))
    return (grad_x, grad_bc, grad_log)
```

```python
import jax
import jax.numpy as jnp
from jax import lax
from jax.sharding import PartitionSpec as P

P_SIZE = 64
N = 128
K = 4
BLOCK = 256


precise = lax.Precision.HIGHEST


def shifted(value, axis, steps):
    count = lax.axis_size(axis)
    initial, last = (max(0, -steps), min(count, count - steps))
    return lax.ppermute(value, axis, [(source, source + steps) for source in range(initial, last)])


def entering(value, axis, join, neutral, backward):
    count, mine = (lax.axis_size(axis), lax.axis_index(axis))
    pieces = jax.tree.map(lambda part: lax.all_gather(part, axis), value)
    if backward:
        pieces = jax.tree.map(lambda part: part[::-1], pieces)
        mine = count - 1 - mine
    total = jax.tree.map(
        lambda part, zero: jnp.full_like(part, 0) + jnp.asarray(zero, part.dtype), value, neutral
    )

    def hop(position, total):
        longer = join(total, jax.tree.map(lambda part: part[position], pieces))
        return jax.tree.map(lambda new, old: jnp.where(position < mine, new, old), longer, total)

    return lax.fori_loop(0, count - 1, hop, total)


def matmul(left, right):
    return jnp.dot(left, right, precision=precise, preferred_element_type=jnp.float32)


def note_index(positions, lengths):
    starts = jnp.cumsum(lengths) - lengths
    hits = (positions[:, None] >= starts[None, :]).astype(jnp.int32)
    return jnp.sum(hits, axis=1) - 1


def block_edges(log_block, note_block, note_before):
    cumul = jnp.cumsum(log_block)
    entry = jnp.exp(cumul) * (note_block == note_before)
    leave = jnp.exp(cumul[-1] - cumul) * (note_block == note_block[-1])
    through = jnp.exp(cumul[-1]) * (note_block[-1] == note_before)
    return (cumul, entry, leave, through)


def block_forward(state, x_block, b_block, c_block, log_block, note_block, note_before):
    cumul, entry, leave, through = block_edges(log_block, note_block, note_before)
    length = note_block.shape[0]
    lower = jnp.arange(length)[:, None] >= jnp.arange(length)[None, :]
    linked = lower & (note_block[:, None] == note_block[None, :])
    decay_matrix = jnp.exp(jnp.where(linked, cumul[:, None] - cumul[None, :], 0.0)) * linked
    scores = matmul(c_block, b_block.T) * decay_matrix
    output = matmul(scores, x_block) + entry[:, None] * matmul(c_block, state.T)
    updated = through * state + matmul((x_block * leave[:, None]).T, b_block)
    return (output, updated)


def head_forward(state, x_head, b_blocks, c_blocks, log_head, note_blocks, befores):

    def head_advance(carry, block):
        output, updated = block_forward(carry, *block)
        return (updated, output)

    final, outputs = lax.scan(
        head_advance, state, (x_head, b_blocks, c_blocks, log_head, note_blocks, befores)
    )
    return (outputs, final)


def conv_forward(extended, weights, note_ext):
    width = weights.shape[0]
    count = extended.shape[0] - width + 1
    result = jnp.zeros((count, extended.shape[1]), jnp.float32)
    for k in range(width):
        linked = note_ext[k : k + count] == note_ext[width - 1 : width - 1 + count]
        result = result + weights[k][None, :] * extended[k : k + count] * linked[:, None]
    return result


def conv_backward(extended, weights, note_ext):
    width = weights.shape[0]
    count = extended.shape[0] - width + 1
    result = jnp.zeros((count, extended.shape[1]), jnp.float32)
    for k in range(width):
        lag = width - 1 - k
        linked = note_ext[lag : lag + count] == note_ext[:count]
        result = result + weights[k][None, :] * extended[lag : lag + count] * linked[:, None]
    return result


def silu_slope(values):
    sigma = jax.nn.sigmoid(values)
    return sigma * (1.0 + values * (1.0 - sigma))


def chain_combine(earlier, later):
    return (earlier[0] * later[0], later[0][:, None, None] * earlier[1] + later[1])


def local(pre_x, pre_bc, conv_x, conv_bc, log_decay, lengths, grad_out):
    tok_rows = pre_x.shape[0]
    head_count = log_decay.shape[0]
    rim_width = K - 1
    block_count = tok_rows // BLOCK
    seq_start = lax.axis_index("seq") * tok_rows
    positions = seq_start + jnp.arange(-rim_width, tok_rows + rim_width)
    note_all = note_index(positions, lengths)
    note_ids = note_all[rim_width : rim_width + tok_rows]
    before_x, before_bc = shifted(
        (pre_x[tok_rows - rim_width :], pre_bc[tok_rows - rim_width :]), "seq", 1
    )
    u_x = conv_forward(
        jnp.concatenate([before_x, pre_x]).astype(jnp.float32),
        conv_x,
        note_all[: tok_rows + rim_width],
    )
    u_bc = conv_forward(
        jnp.concatenate([before_bc, pre_bc]).astype(jnp.float32),
        conv_bc,
        note_all[: tok_rows + rim_width],
    )
    v_x = jax.nn.silu(u_x)
    v_bc = jax.nn.silu(u_bc)
    x_heads = v_x.reshape(block_count, BLOCK, head_count, P_SIZE).transpose(2, 0, 1, 3)
    b_blocks = v_bc[:, :N].reshape(block_count, BLOCK, N)
    c_blocks = v_bc[:, N:].reshape(block_count, BLOCK, N)
    log_blocks = log_decay.reshape(head_count, block_count, BLOCK)
    grad_heads = (
        grad_out.astype(jnp.float32)
        .reshape(block_count, BLOCK, head_count, P_SIZE)
        .transpose(2, 0, 1, 3)
    )
    note_blocks = note_ids.reshape(block_count, BLOCK)
    befores = jnp.concatenate([note_all[rim_width - 1 : rim_width], note_blocks[:-1, -1]])

    def state_only(x_head, log_head):

        def state_advance(carry, block):
            x_block, b_block, log_block, note_block, note_before = block
            _, _, leave, through = block_edges(log_block, note_block, note_before)
            state, keep = carry
            return (
                (through * state + matmul((x_block * leave[:, None]).T, b_block), keep * through),
                None,
            )

        start = (jnp.zeros((P_SIZE, N), jnp.float32), jnp.ones((), jnp.float32))
        final, _ = lax.scan(
            state_advance, start, (x_head, b_blocks, log_head, note_blocks, befores)
        )
        return final

    def adjoint_only(grad_head, log_head):

        def retreat(carry, block):
            grad_block, c_block, log_block, note_block, note_before = block
            _, entry, _, through = block_edges(log_block, note_block, note_before)
            return (through * carry + matmul((grad_block * entry[:, None]).T, c_block), None)

        final, _ = lax.scan(
            retreat,
            jnp.zeros((P_SIZE, N), jnp.float32),
            (grad_head, c_blocks, log_head, note_blocks, befores),
            reverse=True,
        )
        return final

    local_state, local_keep = jax.vmap(state_only)(x_heads, log_blocks)
    local_adjoint = jax.vmap(adjoint_only)(grad_heads, log_blocks)
    identity = (
        jnp.ones((head_count,), jnp.float32),
        jnp.zeros((head_count, P_SIZE, N), jnp.float32),
    )
    _, state_in = entering((local_keep, local_state), "seq", chain_combine, identity, False)
    _, adjoint_in = entering((local_keep, local_adjoint), "seq", chain_combine, identity, True)

    def local_forward(x_all, b_all, c_all, log_all):

        def one_head(state, x_head, log_head):
            return head_forward(state, x_head, b_all, c_all, log_head, note_blocks, befores)

        return jax.vmap(one_head)(state_in, x_all, log_all)

    _, pull = jax.vjp(local_forward, x_heads, b_blocks, c_blocks, log_blocks)
    grad_x_heads, grad_b, grad_c, grad_log = pull((grad_heads, adjoint_in))
    grad_log_decay = grad_log.reshape(head_count, tok_rows)
    grad_v_x = grad_x_heads.transpose(1, 2, 0, 3).reshape(tok_rows, head_count * P_SIZE)
    grad_v_bc = jnp.concatenate([grad_b.reshape(tok_rows, N), grad_c.reshape(tok_rows, N)], axis=1)
    grad_u_x = grad_v_x * silu_slope(u_x)
    grad_u_bc = grad_v_bc * silu_slope(u_bc)
    after_x, after_bc = shifted((grad_u_x[:rim_width], grad_u_bc[:rim_width]), "seq", -1)
    grad_pre_x = conv_backward(jnp.concatenate([grad_u_x, after_x]), conv_x, note_all[rim_width:])
    whole_bc = conv_backward(jnp.concatenate([grad_u_bc, after_bc]), conv_bc, note_all[rim_width:])
    grad_pre_bc = lax.psum_scatter(whole_bc, "head", scatter_dimension=0, tiled=True)
    return (grad_pre_x, grad_pre_bc, grad_log_decay)


def solution(mesh):
    placed = (
        P("seq", "head"),
        P("seq", None),
        P(None, "head"),
        P(),
        P("head", "seq"),
        P(),
        P("seq", "head"),
    )
    return jax.shard_map(
        local,
        mesh=mesh,
        in_specs=placed,
        out_specs=(P("seq", "head"), P(("seq", "head"), None), P("head", "seq")),
        check_vma=False,
    )
```

```python
import jax
import jax.numpy as jnp
from jax import lax
from jax.sharding import PartitionSpec as P

P_SIZE = 64
N = 128
K = 4
BLOCK = 256


precise = lax.Precision.HIGHEST


def shifted(value, axis, steps):
    count = lax.axis_size(axis)
    initial, last = (max(0, -steps), min(count, count - steps))
    return lax.ppermute(value, axis, [(source, source + steps) for source in range(initial, last)])


def entering(value, axis, join, neutral, backward):
    count, mine = (lax.axis_size(axis), lax.axis_index(axis))
    pieces = jax.tree.map(lambda part: lax.all_gather(part, axis), value)
    if backward:
        pieces = jax.tree.map(lambda part: part[::-1], pieces)
        mine = count - 1 - mine
    total = jax.tree.map(
        lambda part, zero: jnp.full_like(part, 0) + jnp.asarray(zero, part.dtype), value, neutral
    )

    def hop(position, total):
        longer = join(total, jax.tree.map(lambda part: part[position], pieces))
        return jax.tree.map(lambda new, old: jnp.where(position < mine, new, old), longer, total)

    return lax.fori_loop(0, count - 1, hop, total)


def matmul(left, right):
    return jnp.dot(left, right, precision=precise, preferred_element_type=jnp.float32)


def note_index(positions, lengths):
    starts = jnp.cumsum(lengths) - lengths
    hits = (positions[:, None] >= starts[None, :]).astype(jnp.int32)
    return jnp.sum(hits, axis=1) - 1


def block_edges(log_block, note_block, note_before):
    cumul = jnp.cumsum(log_block)
    entry = jnp.exp(cumul) * (note_block == note_before)
    leave = jnp.exp(cumul[-1] - cumul) * (note_block == note_block[-1])
    through = jnp.exp(cumul[-1]) * (note_block[-1] == note_before)
    return (cumul, entry, leave, through)


def block_forward(state, x_block, b_block, c_block, log_block, note_block, note_before):
    cumul, entry, leave, through = block_edges(log_block, note_block, note_before)
    length = note_block.shape[0]
    lower = jnp.arange(length)[:, None] >= jnp.arange(length)[None, :]
    linked = lower & (note_block[:, None] == note_block[None, :])
    decay_matrix = jnp.exp(jnp.where(linked, cumul[:, None] - cumul[None, :], 0.0)) * linked
    scores = matmul(c_block, b_block.T) * decay_matrix
    output = matmul(scores, x_block) + entry[:, None] * matmul(c_block, state.T)
    updated = through * state + matmul((x_block * leave[:, None]).T, b_block)
    return (output, updated)


def head_forward(state, x_head, b_blocks, c_blocks, log_head, note_blocks, befores):

    def head_advance(carry, block):
        output, updated = block_forward(carry, *block)
        return (updated, output)

    final, outputs = lax.scan(
        head_advance, state, (x_head, b_blocks, c_blocks, log_head, note_blocks, befores)
    )
    return (outputs, final)


def conv_forward(extended, weights, note_ext):
    width = weights.shape[0]
    count = extended.shape[0] - width + 1
    result = jnp.zeros((count, extended.shape[1]), jnp.float32)
    for k in range(width):
        linked = note_ext[k : k + count] == note_ext[width - 1 : width - 1 + count]
        result = result + weights[k][None, :] * extended[k : k + count] * linked[:, None]
    return result


def conv_backward(extended, weights, note_ext):
    width = weights.shape[0]
    count = extended.shape[0] - width + 1
    result = jnp.zeros((count, extended.shape[1]), jnp.float32)
    for k in range(width):
        lag = width - 1 - k
        linked = note_ext[lag : lag + count] == note_ext[:count]
        result = result + weights[k][None, :] * extended[lag : lag + count] * linked[:, None]
    return result


def silu_slope(values):
    sigma = jax.nn.sigmoid(values)
    return sigma * (1.0 + values * (1.0 - sigma))


def chain_combine(earlier, later):
    return (earlier[0] * later[0], later[0][:, None, None] * earlier[1] + later[1])


def local(pre_x, pre_bc, conv_x, conv_bc, log_decay, lengths, grad_out):
    tok_rows = pre_x.shape[0]
    head_count = log_decay.shape[0]
    rim_width = K - 1
    block_count = tok_rows // BLOCK
    seq_start = lax.axis_index("seq") * tok_rows
    positions = seq_start + jnp.arange(-rim_width, tok_rows + rim_width)
    note_all = note_index(positions, lengths)
    note_ids = note_all[rim_width : rim_width + tok_rows]
    before_x, before_bc = shifted(
        (pre_x[tok_rows - rim_width :], pre_bc[tok_rows - rim_width :]), "seq", 1
    )
    u_x = conv_forward(
        jnp.concatenate([before_x, pre_x]).astype(jnp.float32),
        conv_x,
        note_all[: tok_rows + rim_width],
    )
    u_bc = conv_forward(
        jnp.concatenate([before_bc, pre_bc]).astype(jnp.float32),
        conv_bc,
        note_all[: tok_rows + rim_width],
    )
    v_x = jax.nn.silu(u_x)
    v_bc = jax.nn.silu(u_bc)
    x_heads = v_x.reshape(block_count, BLOCK, head_count, P_SIZE).transpose(2, 0, 1, 3)
    b_blocks = v_bc[:, :N].reshape(block_count, BLOCK, N)
    c_blocks = v_bc[:, N:].reshape(block_count, BLOCK, N)
    log_blocks = log_decay.reshape(head_count, block_count, BLOCK)
    grad_heads = (
        grad_out.astype(jnp.float32)
        .reshape(block_count, BLOCK, head_count, P_SIZE)
        .transpose(2, 0, 1, 3)
    )
    note_blocks = note_ids.reshape(block_count, BLOCK)
    befores = jnp.concatenate([note_all[rim_width - 1 : rim_width], note_blocks[:-1, -1]])

    def state_only(x_head, log_head):

        def state_advance(carry, block):
            x_block, b_block, log_block, note_block, note_before = block
            _, _, leave, through = block_edges(log_block, note_block, note_before)
            state, keep = carry
            return (
                (through * state + matmul((x_block * leave[:, None]).T, b_block), keep * through),
                None,
            )

        start = (jnp.zeros((P_SIZE, N), jnp.float32), jnp.ones((), jnp.float32))
        final, _ = lax.scan(
            state_advance, start, (x_head, b_blocks, log_head, note_blocks, befores)
        )
        return final

    def adjoint_only(grad_head, log_head):

        def retreat(carry, block):
            grad_block, c_block, log_block, note_block, note_before = block
            _, entry, _, through = block_edges(log_block, note_block, note_before)
            return (through * carry + matmul((grad_block * entry[:, None]).T, c_block), None)

        final, _ = lax.scan(
            retreat,
            jnp.zeros((P_SIZE, N), jnp.float32),
            (grad_head, c_blocks, log_head, note_blocks, befores),
            reverse=True,
        )
        return final

    local_state, local_keep = jax.vmap(state_only)(x_heads, log_blocks)
    local_adjoint = jax.vmap(adjoint_only)(grad_heads, log_blocks)
    identity = (
        jnp.ones((head_count,), jnp.float32),
        jnp.zeros((head_count, P_SIZE, N), jnp.float32),
    )
    _, state_in = entering((local_keep, local_state), "seq", chain_combine, identity, False)
    _, adjoint_in = entering((local_keep, local_adjoint), "seq", chain_combine, identity, True)

    def local_forward(x_all, b_all, c_all, log_all):

        def one_head(state, x_head, log_head):
            return head_forward(state, x_head, b_all, c_all, log_head, note_blocks, befores)

        return jax.vmap(one_head)(state_in, x_all, log_all)

    _, pull = jax.vjp(local_forward, x_heads, b_blocks, c_blocks, log_blocks)
    grad_x_heads, grad_b, grad_c, grad_log = pull((grad_heads, adjoint_in))
    grad_log_decay = grad_log.reshape(head_count, tok_rows)
    grad_v_x = grad_x_heads.transpose(1, 2, 0, 3).reshape(tok_rows, head_count * P_SIZE)
    grad_v_bc = jnp.concatenate([grad_b.reshape(tok_rows, N), grad_c.reshape(tok_rows, N)], axis=1)
    grad_u_x = grad_v_x * silu_slope(u_x)
    grad_u_bc = grad_v_bc * silu_slope(u_bc)
    after_x, after_bc = shifted((grad_u_x[:rim_width], grad_u_bc[:rim_width]), "seq", -1)
    grad_pre_x = conv_backward(jnp.concatenate([grad_u_x, after_x]), conv_x, note_all[rim_width:])
    whole_bc = conv_backward(jnp.concatenate([grad_u_bc, after_bc]), conv_bc, note_all[rim_width:])
    head_size = lax.axis_size("head")
    pieces = whole_bc.reshape(head_size, tok_rows // head_size, whole_bc.shape[1])
    grad_pre_bc = lax.all_to_all(pieces, "head", 0, 0, tiled=False).sum(0)
    return (grad_pre_x, grad_pre_bc, grad_log_decay)


def solution(mesh):
    placed = (
        P("seq", "head"),
        P("seq", None),
        P(None, "head"),
        P(),
        P("head", "seq"),
        P(),
        P("seq", "head"),
    )
    return jax.shard_map(
        local,
        mesh=mesh,
        in_specs=placed,
        out_specs=(P("seq", "head"), P(("seq", "head"), None), P("head", "seq")),
        check_vma=False,
    )
```

```python
import jax
import jax.numpy as jnp
from jax import lax
from jax.sharding import PartitionSpec as P

P_SIZE = 64
N = 128
K = 4
BLOCK = 256


precise = lax.Precision.HIGHEST


def shifted(value, axis, steps):
    count = lax.axis_size(axis)
    initial, last = (max(0, -steps), min(count, count - steps))
    return lax.ppermute(value, axis, [(source, source + steps) for source in range(initial, last)])


def entering(value, axis, join, neutral, backward):
    count, mine = (lax.axis_size(axis), lax.axis_index(axis))
    pieces = jax.tree.map(lambda part: lax.all_gather(part, axis), value)
    if backward:
        pieces = jax.tree.map(lambda part: part[::-1], pieces)
        mine = count - 1 - mine
    total = jax.tree.map(
        lambda part, zero: jnp.full_like(part, 0) + jnp.asarray(zero, part.dtype), value, neutral
    )

    def hop(position, total):
        longer = join(total, jax.tree.map(lambda part: part[position], pieces))
        return jax.tree.map(lambda new, old: jnp.where(position < mine, new, old), longer, total)

    return lax.fori_loop(0, count - 1, hop, total)


def matmul(left, right):
    return jnp.dot(left, right, precision=precise, preferred_element_type=jnp.float32)


def note_index(positions, lengths):
    starts = jnp.cumsum(lengths) - lengths
    hits = (positions[:, None] >= starts[None, :]).astype(jnp.int32)
    return jnp.sum(hits, axis=1) - 1


def block_edges(log_block, note_block, note_before):
    cumul = jnp.cumsum(log_block)
    entry = jnp.exp(cumul) * (note_block == note_before)
    leave = jnp.exp(cumul[-1] - cumul) * (note_block == note_block[-1])
    through = jnp.exp(cumul[-1]) * (note_block[-1] == note_before)
    return (cumul, entry, leave, through)


def block_forward(state, x_block, b_block, c_block, log_block, note_block, note_before):
    cumul, entry, leave, through = block_edges(log_block, note_block, note_before)
    length = note_block.shape[0]
    lower = jnp.arange(length)[:, None] >= jnp.arange(length)[None, :]
    linked = lower & (note_block[:, None] == note_block[None, :])
    decay_matrix = jnp.exp(jnp.where(linked, cumul[:, None] - cumul[None, :], 0.0)) * linked
    scores = matmul(c_block, b_block.T) * decay_matrix
    output = matmul(scores, x_block) + entry[:, None] * matmul(c_block, state.T)
    updated = through * state + matmul((x_block * leave[:, None]).T, b_block)
    return (output, updated)


def head_forward(state, x_head, b_blocks, c_blocks, log_head, note_blocks, befores):

    def head_advance(carry, block):
        output, updated = block_forward(carry, *block)
        return (updated, output)

    final, outputs = lax.scan(
        head_advance, state, (x_head, b_blocks, c_blocks, log_head, note_blocks, befores)
    )
    return (outputs, final)


def conv_forward(extended, weights, note_ext):
    width = weights.shape[0]
    count = extended.shape[0] - width + 1
    result = jnp.zeros((count, extended.shape[1]), jnp.float32)
    for k in range(width):
        linked = note_ext[k : k + count] == note_ext[width - 1 : width - 1 + count]
        result = result + weights[k][None, :] * extended[k : k + count] * linked[:, None]
    return result


def conv_backward(extended, weights, note_ext):
    width = weights.shape[0]
    count = extended.shape[0] - width + 1
    result = jnp.zeros((count, extended.shape[1]), jnp.float32)
    for k in range(width):
        lag = width - 1 - k
        linked = note_ext[lag : lag + count] == note_ext[:count]
        result = result + weights[k][None, :] * extended[lag : lag + count] * linked[:, None]
    return result


def silu_slope(values):
    sigma = jax.nn.sigmoid(values)
    return sigma * (1.0 + values * (1.0 - sigma))


def chain_combine(earlier, later):
    return (earlier[0] * later[0], later[0][:, None, None] * earlier[1] + later[1])


def chain_in(value, keep, axis, direction):
    count = lax.axis_size(axis)
    packed = jnp.concatenate(
        [value.reshape(value.shape[0], -1), jnp.broadcast_to(keep[:, None], (keep.shape[0], 128))], axis=1
    )
    total = jnp.zeros_like(value)
    scale = jnp.ones_like(keep)
    for distance in range(1, count):
        arrived = shifted(packed, axis, direction * distance)
        part = arrived[:, : value[0].size].reshape(value.shape)
        total = total + scale[:, None, None] * part
        scale = scale * arrived[:, value[0].size]
    return total


def einsum(spec, *operands):
    return jnp.einsum(spec, *operands, precision=precise, preferred_element_type=jnp.float32)


def block_forward_all(state, x_all, b_all, c_all, log_all, note_blocks, befores):
    cumul = jnp.cumsum(log_all, axis=-1)
    entry = jnp.exp(cumul) * (note_blocks == befores[:, None])
    leave = jnp.exp(cumul[..., -1:] - cumul) * (note_blocks == note_blocks[:, -1:])
    through = jnp.exp(cumul[..., -1]) * (note_blocks[:, -1] == befores)
    length = note_blocks.shape[1]
    lower = jnp.arange(length)[:, None] >= jnp.arange(length)[None, :]
    linked = lower & (note_blocks[:, :, None] == note_blocks[:, None, :])
    differences = cumul[..., :, None] - cumul[..., None, :]
    decay_matrix = jnp.exp(jnp.where(linked, differences, 0.0)) * linked
    scores = einsum("bin,bjn->bij", c_all, b_all) * decay_matrix
    output = einsum("hbij,hbjp->hbip", scores, x_all)
    chunk = einsum("hbjp,bjn->hbpn", x_all * leave[..., None], b_all)
    starts = []
    for block in range(note_blocks.shape[0]):
        starts.append(state)
        state = through[:, block, None, None] * state + chunk[:, block]
    output = output + entry[..., None] * einsum("bin,hbpn->hbip", c_all, jnp.stack(starts, axis=1))
    return (output, state)


def local(pre_x, pre_bc, conv_x, conv_bc, log_decay, lengths, grad_out):
    tok_rows = pre_x.shape[0]
    head_count = log_decay.shape[0]
    rim_width = K - 1
    block_count = tok_rows // BLOCK
    seq_start = lax.axis_index("seq") * tok_rows
    positions = seq_start + jnp.arange(-rim_width, tok_rows + rim_width)
    note_all = note_index(positions, lengths)
    note_ids = note_all[rim_width : rim_width + tok_rows]
    before_x, before_bc = shifted(
        (pre_x[tok_rows - rim_width :], pre_bc[tok_rows - rim_width :]), "seq", 1
    )
    u_x = conv_forward(
        jnp.concatenate([before_x, pre_x]).astype(jnp.float32),
        conv_x,
        note_all[: tok_rows + rim_width],
    )
    u_bc = conv_forward(
        jnp.concatenate([before_bc, pre_bc]).astype(jnp.float32),
        conv_bc,
        note_all[: tok_rows + rim_width],
    )
    v_x = jax.nn.silu(u_x)
    v_bc = jax.nn.silu(u_bc)
    x_heads = v_x.reshape(block_count, BLOCK, head_count, P_SIZE).transpose(2, 0, 1, 3)
    b_blocks = v_bc[:, :N].reshape(block_count, BLOCK, N)
    c_blocks = v_bc[:, N:].reshape(block_count, BLOCK, N)
    log_blocks = log_decay.reshape(head_count, block_count, BLOCK)
    grad_heads = (
        grad_out.astype(jnp.float32)
        .reshape(block_count, BLOCK, head_count, P_SIZE)
        .transpose(2, 0, 1, 3)
    )
    note_blocks = note_ids.reshape(block_count, BLOCK)
    befores = jnp.concatenate([note_all[rim_width - 1 : rim_width], note_blocks[:-1, -1]])

    note_before = note_all[rim_width - 1]
    log_rows = log_decay.astype(jnp.float32)
    x_rows = v_x.reshape(tok_rows, head_count, P_SIZE)
    g_rows = grad_out.astype(jnp.float32).reshape(tok_rows, head_count, P_SIZE)
    shard_cumul = jnp.cumsum(log_rows, axis=-1)
    keep = jnp.exp(shard_cumul[:, -1]) * (note_ids[-1] == note_before)
    leave_rows = jnp.exp(shard_cumul[:, -1:] - shard_cumul) * (note_ids == note_ids[-1])
    entry_rows = jnp.exp(shard_cumul) * (note_ids == note_before)
    local_state = jnp.einsum(
        "thp,ht,tn->hpn", x_rows, leave_rows, v_bc[:, :N], precision=precise,
        preferred_element_type=jnp.float32,
    )
    local_adjoint = jnp.einsum(
        "thp,ht,tn->hpn", g_rows, entry_rows, v_bc[:, N:], precision=precise,
        preferred_element_type=jnp.float32,
    )
    state_in = chain_in(local_state, keep, "seq", 1)
    adjoint_in = chain_in(local_adjoint, keep, "seq", -1)

    def local_forward(x_all, b_all, c_all, log_all):
        return block_forward_all(
            state_in, x_all, b_all, c_all, log_all, note_blocks, befores
        )

    _, pull = jax.vjp(local_forward, x_heads, b_blocks, c_blocks, log_blocks)
    grad_x_heads, grad_b, grad_c, grad_log = pull((grad_heads, adjoint_in))
    grad_log_decay = grad_log.reshape(head_count, tok_rows)
    grad_v_x = grad_x_heads.transpose(1, 2, 0, 3).reshape(tok_rows, head_count * P_SIZE)
    grad_v_bc = jnp.concatenate([grad_b.reshape(tok_rows, N), grad_c.reshape(tok_rows, N)], axis=1)
    grad_u_x = grad_v_x * silu_slope(u_x)
    grad_u_bc = grad_v_bc * silu_slope(u_bc)
    after_x, after_bc = shifted((grad_u_x[:rim_width], grad_u_bc[:rim_width]), "seq", -1)
    grad_pre_x = conv_backward(jnp.concatenate([grad_u_x, after_x]), conv_x, note_all[rim_width:])
    whole_bc = conv_backward(jnp.concatenate([grad_u_bc, after_bc]), conv_bc, note_all[rim_width:])
    head_size = lax.axis_size("head")
    pieces = whole_bc.reshape(head_size, tok_rows // head_size, whole_bc.shape[1])
    grad_pre_bc = lax.all_to_all(pieces, "head", 0, 0, tiled=False).sum(0)
    return (grad_pre_x, grad_pre_bc, grad_log_decay)


def solution(mesh):
    placed = (
        P("seq", "head"),
        P("seq", None),
        P(None, "head"),
        P(),
        P("head", "seq"),
        P(),
        P("seq", "head"),
    )
    return jax.shard_map(
        local,
        mesh=mesh,
        in_specs=placed,
        out_specs=(P("seq", "head"), P(("seq", "head"), None), P("head", "seq")),
        check_vma=False,
    )
```

```python
import jax
import jax.numpy as jnp
from jax import lax
from jax.sharding import PartitionSpec as P

P_SIZE = 64
N = 128
K = 4
BLOCK = 256


precise = lax.Precision.HIGHEST


def shifted(value, axis, steps):
    count = lax.axis_size(axis)
    initial, last = (max(0, -steps), min(count, count - steps))
    return lax.ppermute(value, axis, [(source, source + steps) for source in range(initial, last)])


def entering(value, axis, join, neutral, backward):
    count, mine = (lax.axis_size(axis), lax.axis_index(axis))
    pieces = jax.tree.map(lambda part: lax.all_gather(part, axis), value)
    if backward:
        pieces = jax.tree.map(lambda part: part[::-1], pieces)
        mine = count - 1 - mine
    total = jax.tree.map(
        lambda part, zero: jnp.full_like(part, 0) + jnp.asarray(zero, part.dtype), value, neutral
    )

    def hop(position, total):
        longer = join(total, jax.tree.map(lambda part: part[position], pieces))
        return jax.tree.map(lambda new, old: jnp.where(position < mine, new, old), longer, total)

    return lax.fori_loop(0, count - 1, hop, total)


def matmul(left, right):
    return jnp.dot(left, right, precision=precise, preferred_element_type=jnp.float32)


def note_index(positions, lengths):
    starts = jnp.cumsum(lengths) - lengths
    hits = (positions[:, None] >= starts[None, :]).astype(jnp.int32)
    return jnp.sum(hits, axis=1) - 1


def block_edges(log_block, note_block, note_before):
    cumul = jnp.cumsum(log_block)
    entry = jnp.exp(cumul) * (note_block == note_before)
    leave = jnp.exp(cumul[-1] - cumul) * (note_block == note_block[-1])
    through = jnp.exp(cumul[-1]) * (note_block[-1] == note_before)
    return (cumul, entry, leave, through)


def block_forward(state, x_block, b_block, c_block, log_block, note_block, note_before):
    cumul, entry, leave, through = block_edges(log_block, note_block, note_before)
    length = note_block.shape[0]
    lower = jnp.arange(length)[:, None] >= jnp.arange(length)[None, :]
    linked = lower & (note_block[:, None] == note_block[None, :])
    decay_matrix = jnp.exp(jnp.where(linked, cumul[:, None] - cumul[None, :], 0.0)) * linked
    scores = matmul(c_block, b_block.T) * decay_matrix
    output = matmul(scores, x_block) + entry[:, None] * matmul(c_block, state.T)
    updated = through * state + matmul((x_block * leave[:, None]).T, b_block)
    return (output, updated)


def head_forward(state, x_head, b_blocks, c_blocks, log_head, note_blocks, befores):

    def head_advance(carry, block):
        output, updated = block_forward(carry, *block)
        return (updated, output)

    final, outputs = lax.scan(
        head_advance, state, (x_head, b_blocks, c_blocks, log_head, note_blocks, befores)
    )
    return (outputs, final)


def conv_forward(extended, weights, note_ext):
    width = weights.shape[0]
    count = extended.shape[0] - width + 1
    result = jnp.zeros((count, extended.shape[1]), jnp.float32)
    for k in range(width):
        linked = note_ext[k : k + count] == note_ext[width - 1 : width - 1 + count]
        result = result + weights[k][None, :] * extended[k : k + count] * linked[:, None]
    return result


def conv_backward(extended, weights, note_ext):
    width = weights.shape[0]
    count = extended.shape[0] - width + 1
    result = jnp.zeros((count, extended.shape[1]), jnp.float32)
    for k in range(width):
        lag = width - 1 - k
        linked = note_ext[lag : lag + count] == note_ext[:count]
        result = result + weights[k][None, :] * extended[lag : lag + count] * linked[:, None]
    return result


def silu_slope(values):
    sigma = jax.nn.sigmoid(values)
    return sigma * (1.0 + values * (1.0 - sigma))


def chain_combine(earlier, later):
    return (earlier[0] * later[0], later[0][:, None, None] * earlier[1] + later[1])


def chain_in(value, keep, axis, direction):
    count = lax.axis_size(axis)
    packed = jnp.concatenate(
        [value.reshape(value.shape[0], -1), jnp.broadcast_to(keep[:, None], (keep.shape[0], 128))], axis=1
    )
    total = jnp.zeros_like(value)
    scale = jnp.ones_like(keep)
    for distance in range(1, count):
        arrived = shifted(packed, axis, direction * distance)
        part = arrived[:, : value[0].size].reshape(value.shape)
        total = total + scale[:, None, None] * part
        scale = scale * arrived[:, value[0].size]
    return total


def running_sum(values):
    length = values.shape[-1]
    upper = (jnp.arange(length)[:, None] <= jnp.arange(length)[None, :]).astype(values.dtype)
    return jnp.dot(values, upper, precision=precise, preferred_element_type=jnp.float32)


def einsum(spec, *operands):
    return jnp.einsum(spec, *operands, precision=precise, preferred_element_type=jnp.float32)


def block_forward_all(state, x_all, b_all, c_all, log_all, note_blocks, befores):
    cumul = running_sum(log_all)
    entry = jnp.exp(cumul) * (note_blocks == befores[:, None])
    leave = jnp.exp(cumul[..., -1:] - cumul) * (note_blocks == note_blocks[:, -1:])
    through = jnp.exp(cumul[..., -1]) * (note_blocks[:, -1] == befores)
    length = note_blocks.shape[1]
    lower = jnp.arange(length)[:, None] >= jnp.arange(length)[None, :]
    linked = lower & (note_blocks[:, :, None] == note_blocks[:, None, :])
    differences = cumul[..., :, None] - cumul[..., None, :]
    decay_matrix = jnp.exp(jnp.where(linked, differences, 0.0)) * linked
    scores = einsum("bin,bjn->bij", c_all, b_all) * decay_matrix
    output = einsum("hbij,hbjp->hbip", scores, x_all)
    chunk = einsum("hbjp,bjn->hbpn", x_all * leave[..., None], b_all)
    starts = []
    for block in range(note_blocks.shape[0]):
        starts.append(state)
        state = through[:, block, None, None] * state + chunk[:, block]
    output = output + entry[..., None] * einsum("bin,hbpn->hbip", c_all, jnp.stack(starts, axis=1))
    return (output, state)


def local(pre_x, pre_bc, conv_x, conv_bc, log_decay, lengths, grad_out):
    tok_rows = pre_x.shape[0]
    head_count = log_decay.shape[0]
    rim_width = K - 1
    block_count = tok_rows // BLOCK
    seq_start = lax.axis_index("seq") * tok_rows
    positions = seq_start + jnp.arange(-rim_width, tok_rows + rim_width)
    note_all = note_index(positions, lengths)
    note_ids = note_all[rim_width : rim_width + tok_rows]
    before_both = shifted(
        jnp.concatenate([pre_x[tok_rows - rim_width :], pre_bc[tok_rows - rim_width :]], axis=1), "seq", 1
    )
    before_x, before_bc = before_both[:, : pre_x.shape[1]], before_both[:, pre_x.shape[1] :]
    u_x = conv_forward(
        jnp.concatenate([before_x, pre_x]).astype(jnp.float32),
        conv_x,
        note_all[: tok_rows + rim_width],
    )
    u_bc = conv_forward(
        jnp.concatenate([before_bc, pre_bc]).astype(jnp.float32),
        conv_bc,
        note_all[: tok_rows + rim_width],
    )
    v_x = jax.nn.silu(u_x)
    v_bc = jax.nn.silu(u_bc)
    x_heads = v_x.reshape(block_count, BLOCK, head_count, P_SIZE).transpose(2, 0, 1, 3)
    b_blocks = v_bc[:, :N].reshape(block_count, BLOCK, N)
    c_blocks = v_bc[:, N:].reshape(block_count, BLOCK, N)
    log_blocks = log_decay.reshape(head_count, block_count, BLOCK)
    grad_heads = (
        grad_out.astype(jnp.float32)
        .reshape(block_count, BLOCK, head_count, P_SIZE)
        .transpose(2, 0, 1, 3)
    )
    note_blocks = note_ids.reshape(block_count, BLOCK)
    befores = jnp.concatenate([note_all[rim_width - 1 : rim_width], note_blocks[:-1, -1]])

    note_before = note_all[rim_width - 1]
    log_rows = log_decay.astype(jnp.float32)
    x_rows = v_x.reshape(tok_rows, head_count, P_SIZE)
    g_rows = grad_out.astype(jnp.float32).reshape(tok_rows, head_count, P_SIZE)
    shard_cumul = running_sum(log_rows)
    keep = jnp.exp(shard_cumul[:, -1]) * (note_ids[-1] == note_before)
    leave_rows = jnp.exp(shard_cumul[:, -1:] - shard_cumul) * (note_ids == note_ids[-1])
    entry_rows = jnp.exp(shard_cumul) * (note_ids == note_before)
    local_state = jnp.einsum(
        "thp,ht,tn->hpn", x_rows, leave_rows, v_bc[:, :N], precision=precise,
        preferred_element_type=jnp.float32,
    )
    local_adjoint = jnp.einsum(
        "thp,ht,tn->hpn", g_rows, entry_rows, v_bc[:, N:], precision=precise,
        preferred_element_type=jnp.float32,
    )
    state_in = chain_in(local_state, keep, "seq", 1)
    adjoint_in = chain_in(local_adjoint, keep, "seq", -1)

    def local_forward(x_all, b_all, c_all, log_all):
        return block_forward_all(
            state_in, x_all, b_all, c_all, log_all, note_blocks, befores
        )

    _, pull = jax.vjp(local_forward, x_heads, b_blocks, c_blocks, log_blocks)
    grad_x_heads, grad_b, grad_c, grad_log = pull((grad_heads, adjoint_in))
    grad_log_decay = grad_log.reshape(head_count, tok_rows)
    grad_v_x = grad_x_heads.transpose(1, 2, 0, 3).reshape(tok_rows, head_count * P_SIZE)
    grad_v_bc = jnp.concatenate([grad_b.reshape(tok_rows, N), grad_c.reshape(tok_rows, N)], axis=1)
    grad_u_x = grad_v_x * silu_slope(u_x)
    grad_u_bc = grad_v_bc * silu_slope(u_bc)
    after_both = shifted(jnp.concatenate([grad_u_x[:rim_width], grad_u_bc[:rim_width]], axis=1), "seq", -1)
    after_x, after_bc = after_both[:, : grad_u_x.shape[1]], after_both[:, grad_u_x.shape[1] :]
    grad_pre_x = conv_backward(jnp.concatenate([grad_u_x, after_x]), conv_x, note_all[rim_width:])
    whole_bc = conv_backward(jnp.concatenate([grad_u_bc, after_bc]), conv_bc, note_all[rim_width:])
    head_size = lax.axis_size("head")
    pieces = whole_bc.reshape(head_size, tok_rows // head_size, whole_bc.shape[1])
    grad_pre_bc = lax.all_to_all(pieces, "head", 0, 0, tiled=False).sum(0)
    return (grad_pre_x, grad_pre_bc, grad_log_decay)


def solution(mesh):
    placed = (
        P("seq", "head"),
        P("seq", None),
        P(None, "head"),
        P(),
        P("head", "seq"),
        P(),
        P("seq", "head"),
    )
    return jax.shard_map(
        local,
        mesh=mesh,
        in_specs=placed,
        out_specs=(P("seq", "head"), P(("seq", "head"), None), P("head", "seq")),
        check_vma=False,
    )
```

```python
import jax
import jax.numpy as jnp
from jax import lax
from jax.sharding import PartitionSpec as P

P_SIZE = 64
N = 128
K = 4
BLOCK = 256


precise = lax.Precision.HIGHEST


def shifted(value, axis, steps):
    count = lax.axis_size(axis)
    initial, last = (max(0, -steps), min(count, count - steps))
    return lax.ppermute(value, axis, [(source, source + steps) for source in range(initial, last)])


def entering(value, axis, join, neutral, backward):
    count, mine = (lax.axis_size(axis), lax.axis_index(axis))
    pieces = jax.tree.map(lambda part: lax.all_gather(part, axis), value)
    if backward:
        pieces = jax.tree.map(lambda part: part[::-1], pieces)
        mine = count - 1 - mine
    total = jax.tree.map(
        lambda part, zero: jnp.full_like(part, 0) + jnp.asarray(zero, part.dtype), value, neutral
    )

    def hop(position, total):
        longer = join(total, jax.tree.map(lambda part: part[position], pieces))
        return jax.tree.map(lambda new, old: jnp.where(position < mine, new, old), longer, total)

    return lax.fori_loop(0, count - 1, hop, total)


def matmul(left, right):
    return jnp.dot(left, right, precision=precise, preferred_element_type=jnp.float32)


def note_index(positions, lengths):
    starts = jnp.cumsum(lengths) - lengths
    hits = (positions[:, None] >= starts[None, :]).astype(jnp.int32)
    return jnp.sum(hits, axis=1) - 1


def block_edges(log_block, note_block, note_before):
    cumul = jnp.cumsum(log_block)
    entry = jnp.exp(cumul) * (note_block == note_before)
    leave = jnp.exp(cumul[-1] - cumul) * (note_block == note_block[-1])
    through = jnp.exp(cumul[-1]) * (note_block[-1] == note_before)
    return (cumul, entry, leave, through)


def block_forward(state, x_block, b_block, c_block, log_block, note_block, note_before):
    cumul, entry, leave, through = block_edges(log_block, note_block, note_before)
    length = note_block.shape[0]
    lower = jnp.arange(length)[:, None] >= jnp.arange(length)[None, :]
    linked = lower & (note_block[:, None] == note_block[None, :])
    decay_matrix = jnp.exp(jnp.where(linked, cumul[:, None] - cumul[None, :], 0.0)) * linked
    scores = matmul(c_block, b_block.T) * decay_matrix
    output = matmul(scores, x_block) + entry[:, None] * matmul(c_block, state.T)
    updated = through * state + matmul((x_block * leave[:, None]).T, b_block)
    return (output, updated)


def head_forward(state, x_head, b_blocks, c_blocks, log_head, note_blocks, befores):

    def head_advance(carry, block):
        output, updated = block_forward(carry, *block)
        return (updated, output)

    final, outputs = lax.scan(
        head_advance, state, (x_head, b_blocks, c_blocks, log_head, note_blocks, befores)
    )
    return (outputs, final)


def conv_forward(extended, weights, note_ext):
    width = weights.shape[0]
    count = extended.shape[0] - width + 1
    result = jnp.zeros((count, extended.shape[1]), jnp.float32)
    for k in range(width):
        linked = note_ext[k : k + count] == note_ext[width - 1 : width - 1 + count]
        result = result + weights[k][None, :] * extended[k : k + count] * linked[:, None]
    return result


def conv_backward(extended, weights, note_ext):
    width = weights.shape[0]
    count = extended.shape[0] - width + 1
    result = jnp.zeros((count, extended.shape[1]), jnp.float32)
    for k in range(width):
        lag = width - 1 - k
        linked = note_ext[lag : lag + count] == note_ext[:count]
        result = result + weights[k][None, :] * extended[lag : lag + count] * linked[:, None]
    return result


def silu_slope(values):
    sigma = jax.nn.sigmoid(values)
    return sigma * (1.0 + values * (1.0 - sigma))


def chain_combine(earlier, later):
    return (earlier[0] * later[0], later[0][:, None, None] * earlier[1] + later[1])


def chain_in(value, keep, axis, direction):
    count = lax.axis_size(axis)
    packed = jnp.concatenate(
        [value.reshape(value.shape[0], -1), jnp.broadcast_to(keep[:, None], (keep.shape[0], 128))], axis=1
    )
    total = jnp.zeros_like(value)
    scale = jnp.ones_like(keep)
    for distance in range(1, count):
        arrived = shifted(packed, axis, direction * distance)
        part = arrived[:, : value[0].size].reshape(value.shape)
        total = total + scale[:, None, None] * part
        scale = scale * arrived[:, value[0].size]
    return total


def running_sum(values):
    length = values.shape[-1]
    upper = (jnp.arange(length)[:, None] <= jnp.arange(length)[None, :]).astype(values.dtype)
    return jnp.dot(values, upper, precision=precise, preferred_element_type=jnp.float32)


def einsum(spec, *operands):
    return jnp.einsum(spec, *operands, precision=precise, preferred_element_type=jnp.float32)


def block_forward_all(state, x_all, b_all, c_all, log_all, note_blocks, befores):
    cumul = running_sum(log_all)
    entry = jnp.exp(cumul) * (note_blocks == befores[:, None])
    leave = jnp.exp(cumul[..., -1:] - cumul) * (note_blocks == note_blocks[:, -1:])
    through = jnp.exp(cumul[..., -1]) * (note_blocks[:, -1] == befores)
    length = note_blocks.shape[1]
    lower = jnp.arange(length)[:, None] >= jnp.arange(length)[None, :]
    linked = lower & (note_blocks[:, :, None] == note_blocks[:, None, :])
    differences = cumul[..., :, None] - cumul[..., None, :]
    decay_matrix = jnp.exp(jnp.where(linked, differences, 0.0)) * linked
    scores = einsum("bin,bjn->bij", c_all, b_all) * decay_matrix
    output = einsum("hbij,hbjp->hbip", scores, x_all)
    chunk = einsum("hbjp,bjn->hbpn", x_all * leave[..., None], b_all)
    starts = []
    for block in range(note_blocks.shape[0]):
        starts.append(state)
        state = through[:, block, None, None] * state + chunk[:, block]
    output = output + entry[..., None] * einsum("bin,hbpn->hbip", c_all, jnp.stack(starts, axis=1))
    return (output, state)


def local(pre_x, pre_bc, conv_x, conv_bc, log_decay, lengths, grad_out):
    tok_rows = pre_x.shape[0]
    head_count = log_decay.shape[0]
    rim_width = K - 1
    block_count = tok_rows // BLOCK
    seq_start = lax.axis_index("seq") * tok_rows
    positions = seq_start + jnp.arange(-rim_width, tok_rows + rim_width)
    note_all = note_index(positions, lengths)
    note_ids = note_all[rim_width : rim_width + tok_rows]
    before_both = shifted(
        jnp.concatenate([pre_x[tok_rows - rim_width :], pre_bc[tok_rows - rim_width :]], axis=1), "seq", 1
    )
    before_x, before_bc = before_both[:, : pre_x.shape[1]], before_both[:, pre_x.shape[1] :]
    u_x = conv_forward(
        jnp.concatenate([before_x, pre_x]).astype(jnp.float32),
        conv_x,
        note_all[: tok_rows + rim_width],
    )
    u_bc = conv_forward(
        jnp.concatenate([before_bc, pre_bc]).astype(jnp.float32),
        conv_bc,
        note_all[: tok_rows + rim_width],
    )
    v_x = jax.nn.silu(u_x)
    v_bc = jax.nn.silu(u_bc)
    x_heads = v_x.reshape(block_count, BLOCK, head_count, P_SIZE).transpose(2, 0, 1, 3)
    b_blocks = v_bc[:, :N].reshape(block_count, BLOCK, N)
    c_blocks = v_bc[:, N:].reshape(block_count, BLOCK, N)
    log_blocks = log_decay.reshape(head_count, block_count, BLOCK)
    grad_heads = (
        grad_out.astype(jnp.float32)
        .reshape(block_count, BLOCK, head_count, P_SIZE)
        .transpose(2, 0, 1, 3)
    )
    note_blocks = note_ids.reshape(block_count, BLOCK)
    befores = jnp.concatenate([note_all[rim_width - 1 : rim_width], note_blocks[:-1, -1]])

    note_before = note_all[rim_width - 1]
    log_rows = log_decay.astype(jnp.float32)
    x_rows = v_x.reshape(tok_rows, head_count, P_SIZE)
    g_rows = grad_out.astype(jnp.float32).reshape(tok_rows, head_count, P_SIZE)
    shard_cumul = running_sum(log_rows)
    keep = jnp.exp(shard_cumul[:, -1]) * (note_ids[-1] == note_before)
    leave_rows = jnp.exp(shard_cumul[:, -1:] - shard_cumul) * (note_ids == note_ids[-1])
    entry_rows = jnp.exp(shard_cumul) * (note_ids == note_before)
    local_state = jnp.einsum(
        "thp,ht,tn->hpn", x_rows, leave_rows, v_bc[:, :N], precision=precise,
        preferred_element_type=jnp.float32,
    )
    local_adjoint = jnp.einsum(
        "thp,ht,tn->hpn", g_rows, entry_rows, v_bc[:, N:], precision=precise,
        preferred_element_type=jnp.float32,
    )
    state_in = chain_in(local_state, keep, "seq", 1)
    adjoint_in = chain_in(local_adjoint, keep, "seq", -1)

    def local_forward(x_all, b_all, c_all, log_all):
        return block_forward_all(
            state_in, x_all, b_all, c_all, log_all, note_blocks, befores
        )

    _, pull = jax.vjp(local_forward, x_heads, b_blocks, c_blocks, log_blocks)
    grad_x_heads, grad_b, grad_c, grad_log = pull((grad_heads, adjoint_in))
    grad_log_decay = grad_log.reshape(head_count, tok_rows)
    grad_v_x = grad_x_heads.transpose(1, 2, 0, 3).reshape(tok_rows, head_count * P_SIZE)
    grad_v_bc = jnp.concatenate([grad_b.reshape(tok_rows, N), grad_c.reshape(tok_rows, N)], axis=1)
    grad_u_x = grad_v_x * silu_slope(u_x)
    grad_u_bc = grad_v_bc * silu_slope(u_bc)
    after_both = shifted(jnp.concatenate([grad_u_x[:rim_width], grad_u_bc[:rim_width]], axis=1), "seq", -1)
    after_x, after_bc = after_both[:, : grad_u_x.shape[1]], after_both[:, grad_u_x.shape[1] :]
    grad_pre_x = conv_backward(jnp.concatenate([grad_u_x, after_x]), conv_x, note_all[rim_width:])
    whole_bc = conv_backward(jnp.concatenate([grad_u_bc, after_bc]), conv_bc, note_all[rim_width:])
    chips, cores = lax.axis_size("chip"), lax.axis_size("core")
    pieces = whole_bc.reshape(chips, cores, tok_rows // (chips * cores), whole_bc.shape[1])
    core = lax.axis_index("core")
    mine = lax.dynamic_index_in_dim(pieces, core, 1, keepdims=False)
    other = lax.dynamic_index_in_dim(pieces, 1 - core, 1, keepdims=False)
    pair_sum = mine + lax.ppermute(other, "core", [(0, 1), (1, 0)])
    grad_pre_bc = lax.all_to_all(pair_sum, "chip", 0, 0, tiled=False).sum(0)
    return (grad_pre_x, grad_pre_bc, grad_log_decay)


def solution(mesh):
    seq_size, head_size = mesh.shape["seq"], mesh.shape["head"]
    split = jax.sharding.Mesh(
        mesh.devices.reshape(seq_size, head_size // 2, 2), ("seq", "chip", "core")
    )
    head = ("chip", "core")
    placed = (
        P("seq", head),
        P("seq", None),
        P(None, head),
        P(),
        P(head, "seq"),
        P(),
        P("seq", head),
    )
    return jax.shard_map(
        local,
        mesh=split,
        in_specs=placed,
        out_specs=(P("seq", head), P(("seq",) + head, None), P(head, "seq")),
        check_vma=False,
    )
```

```python
import functools
import jax
import jax.numpy as jnp
from jax import lax
from jax.experimental import pallas as pl
from jax.experimental.pallas import tpu as pltpu
from jax.sharding import PartitionSpec as P

MESH = pl.DeviceIdType.MESH

P_SIZE = 64
N = 128
K = 4
BLOCK = 256


precise = lax.Precision.HIGHEST


def shifted(value, axis, steps):
    count = lax.axis_size(axis)
    initial, last = (max(0, -steps), min(count, count - steps))
    return lax.ppermute(value, axis, [(source, source + steps) for source in range(initial, last)])


def entering(value, axis, join, neutral, backward):
    count, mine = (lax.axis_size(axis), lax.axis_index(axis))
    pieces = jax.tree.map(lambda part: lax.all_gather(part, axis), value)
    if backward:
        pieces = jax.tree.map(lambda part: part[::-1], pieces)
        mine = count - 1 - mine
    total = jax.tree.map(
        lambda part, zero: jnp.full_like(part, 0) + jnp.asarray(zero, part.dtype), value, neutral
    )

    def hop(position, total):
        longer = join(total, jax.tree.map(lambda part: part[position], pieces))
        return jax.tree.map(lambda new, old: jnp.where(position < mine, new, old), longer, total)

    return lax.fori_loop(0, count - 1, hop, total)


def matmul(left, right):
    return jnp.dot(left, right, precision=precise, preferred_element_type=jnp.float32)


def note_index(positions, lengths):
    starts = jnp.cumsum(lengths) - lengths
    hits = (positions[:, None] >= starts[None, :]).astype(jnp.int32)
    return jnp.sum(hits, axis=1) - 1


def block_edges(log_block, note_block, note_before):
    cumul = jnp.cumsum(log_block)
    entry = jnp.exp(cumul) * (note_block == note_before)
    leave = jnp.exp(cumul[-1] - cumul) * (note_block == note_block[-1])
    through = jnp.exp(cumul[-1]) * (note_block[-1] == note_before)
    return (cumul, entry, leave, through)


def block_forward(state, x_block, b_block, c_block, log_block, note_block, note_before):
    cumul, entry, leave, through = block_edges(log_block, note_block, note_before)
    length = note_block.shape[0]
    lower = jnp.arange(length)[:, None] >= jnp.arange(length)[None, :]
    linked = lower & (note_block[:, None] == note_block[None, :])
    decay_matrix = jnp.exp(jnp.where(linked, cumul[:, None] - cumul[None, :], 0.0)) * linked
    scores = matmul(c_block, b_block.T) * decay_matrix
    output = matmul(scores, x_block) + entry[:, None] * matmul(c_block, state.T)
    updated = through * state + matmul((x_block * leave[:, None]).T, b_block)
    return (output, updated)


def head_forward(state, x_head, b_blocks, c_blocks, log_head, note_blocks, befores):

    def head_advance(carry, block):
        output, updated = block_forward(carry, *block)
        return (updated, output)

    final, outputs = lax.scan(
        head_advance, state, (x_head, b_blocks, c_blocks, log_head, note_blocks, befores)
    )
    return (outputs, final)


def conv_forward(extended, weights, note_ext):
    width = weights.shape[0]
    count = extended.shape[0] - width + 1
    result = jnp.zeros((count, extended.shape[1]), jnp.float32)
    for k in range(width):
        linked = note_ext[k : k + count] == note_ext[width - 1 : width - 1 + count]
        result = result + weights[k][None, :] * extended[k : k + count] * linked[:, None]
    return result


def conv_backward(extended, weights, note_ext):
    width = weights.shape[0]
    count = extended.shape[0] - width + 1
    result = jnp.zeros((count, extended.shape[1]), jnp.float32)
    for k in range(width):
        lag = width - 1 - k
        linked = note_ext[lag : lag + count] == note_ext[:count]
        result = result + weights[k][None, :] * extended[lag : lag + count] * linked[:, None]
    return result


def silu_slope(values):
    sigma = jax.nn.sigmoid(values)
    return sigma * (1.0 + values * (1.0 - sigma))


def chain_combine(earlier, later):
    return (earlier[0] * later[0], later[0][:, None, None] * earlier[1] + later[1])


def chain_in(value, keep, axis, direction):
    count = lax.axis_size(axis)
    packed = jnp.concatenate(
        [value.reshape(value.shape[0], -1), jnp.broadcast_to(keep[:, None], (keep.shape[0], 128))], axis=1
    )
    total = jnp.zeros_like(value)
    scale = jnp.ones_like(keep)
    for distance in range(1, count):
        arrived = shifted(packed, axis, direction * distance)
        part = arrived[:, : value[0].size].reshape(value.shape)
        total = total + scale[:, None, None] * part
        scale = scale * arrived[:, value[0].size]
    return total


def running_sum(values):
    length = values.shape[-1]
    upper = (jnp.arange(length)[:, None] <= jnp.arange(length)[None, :]).astype(values.dtype)
    return jnp.dot(values, upper, precision=precise, preferred_element_type=jnp.float32)


def einsum(spec, *operands):
    return jnp.einsum(spec, *operands, precision=precise, preferred_element_type=jnp.float32)


def block_forward_all(state, x_all, b_all, c_all, log_all, note_blocks, befores):
    cumul = running_sum(log_all)
    entry = jnp.exp(cumul) * (note_blocks == befores[:, None])
    leave = jnp.exp(cumul[..., -1:] - cumul) * (note_blocks == note_blocks[:, -1:])
    through = jnp.exp(cumul[..., -1]) * (note_blocks[:, -1] == befores)
    length = note_blocks.shape[1]
    lower = jnp.arange(length)[:, None] >= jnp.arange(length)[None, :]
    linked = lower & (note_blocks[:, :, None] == note_blocks[:, None, :])
    differences = cumul[..., :, None] - cumul[..., None, :]
    decay_matrix = jnp.exp(jnp.where(linked, differences, 0.0)) * linked
    scores = einsum("bin,bjn->bij", c_all, b_all) * decay_matrix
    output = einsum("hbij,hbjp->hbip", scores, x_all)
    chunk = einsum("hbjp,bjn->hbpn", x_all * leave[..., None], b_all)
    starts = []
    for block in range(note_blocks.shape[0]):
        starts.append(state)
        state = through[:, block, None, None] * state + chunk[:, block]
    output = output + entry[..., None] * einsum("bin,hbpn->hbip", c_all, jnp.stack(starts, axis=1))
    return (output, state)


def reduce_kernel(count, cores, pieces_ref, out_ref, landed, send_sems, recv_sems):
    seq = lax.axis_index("seq")
    me = lax.axis_index("chip") * cores + lax.axis_index("core")

    def place(peer):
        return (seq, peer // cores, peer % cores)

    barrier = pltpu.get_barrier_semaphore()

    def greet(step, carry):
        peer = lax.rem(me + step, count)
        pl.semaphore_signal(barrier, inc=1, device_id=place(peer), device_id_type=MESH)
        return carry

    lax.fori_loop(1, count, greet, 0)
    pl.semaphore_wait(barrier, count - 1)

    def outgoing(step):
        peer = lax.rem(me + step, count)
        return pltpu.make_async_remote_copy(
            src_ref=pieces_ref.at[peer],
            dst_ref=landed.at[count - 1 - step],
            send_sem=send_sems.at[step - 1],
            recv_sem=recv_sems.at[count - 1 - step],
            device_id=place(peer),
            device_id_type=MESH,
        )

    def send(step, carry):
        outgoing(step).start()
        return carry

    lax.fori_loop(1, count, send, 0)

    def finish(step, carry):
        outgoing(step).wait_send()
        outgoing(count - step).wait_recv()
        return carry

    lax.fori_loop(1, count, finish, 0)

    def accumulate(slot, total):
        return total + landed[slot]

    out_ref[...] = lax.fori_loop(0, count - 1, accumulate, pieces_ref[me])


def head_reduce(partial):
    cores = lax.axis_size("core")
    count = lax.axis_size("chip") * cores
    rows, columns = partial.shape[0] // count, partial.shape[1]
    return pl.pallas_call(
        functools.partial(reduce_kernel, count, cores),
        out_shape=jax.ShapeDtypeStruct((rows, columns), jnp.float32),
        in_specs=[pl.BlockSpec(memory_space=pltpu.VMEM)],
        out_specs=pl.BlockSpec(memory_space=pltpu.VMEM),
        scratch_shapes=[
            pltpu.VMEM((count - 1, rows, columns), jnp.float32),
            pltpu.SemaphoreType.DMA((count - 1,)),
            pltpu.SemaphoreType.DMA((count - 1,)),
        ],
        compiler_params=pltpu.CompilerParams(collective_id=0, has_side_effects=True),
    )(partial.reshape(count, rows, columns))


def local(pre_x, pre_bc, conv_x, conv_bc, log_decay, lengths, grad_out):
    tok_rows = pre_x.shape[0]
    head_count = log_decay.shape[0]
    rim_width = K - 1
    block_count = tok_rows // BLOCK
    seq_start = lax.axis_index("seq") * tok_rows
    positions = seq_start + jnp.arange(-rim_width, tok_rows + rim_width)
    note_all = note_index(positions, lengths)
    note_ids = note_all[rim_width : rim_width + tok_rows]
    before_both = shifted(
        jnp.concatenate([pre_x[tok_rows - rim_width :], pre_bc[tok_rows - rim_width :]], axis=1), "seq", 1
    )
    before_x, before_bc = before_both[:, : pre_x.shape[1]], before_both[:, pre_x.shape[1] :]
    u_x = conv_forward(
        jnp.concatenate([before_x, pre_x]).astype(jnp.float32),
        conv_x,
        note_all[: tok_rows + rim_width],
    )
    u_bc = conv_forward(
        jnp.concatenate([before_bc, pre_bc]).astype(jnp.float32),
        conv_bc,
        note_all[: tok_rows + rim_width],
    )
    v_x = jax.nn.silu(u_x)
    v_bc = jax.nn.silu(u_bc)
    x_heads = v_x.reshape(block_count, BLOCK, head_count, P_SIZE).transpose(2, 0, 1, 3)
    b_blocks = v_bc[:, :N].reshape(block_count, BLOCK, N)
    c_blocks = v_bc[:, N:].reshape(block_count, BLOCK, N)
    log_blocks = log_decay.reshape(head_count, block_count, BLOCK)
    grad_heads = (
        grad_out.astype(jnp.float32)
        .reshape(block_count, BLOCK, head_count, P_SIZE)
        .transpose(2, 0, 1, 3)
    )
    note_blocks = note_ids.reshape(block_count, BLOCK)
    befores = jnp.concatenate([note_all[rim_width - 1 : rim_width], note_blocks[:-1, -1]])

    note_before = note_all[rim_width - 1]
    log_rows = log_decay.astype(jnp.float32)
    x_rows = v_x.reshape(tok_rows, head_count, P_SIZE)
    g_rows = grad_out.astype(jnp.float32).reshape(tok_rows, head_count, P_SIZE)
    shard_cumul = running_sum(log_rows)
    keep = jnp.exp(shard_cumul[:, -1]) * (note_ids[-1] == note_before)
    leave_rows = jnp.exp(shard_cumul[:, -1:] - shard_cumul) * (note_ids == note_ids[-1])
    entry_rows = jnp.exp(shard_cumul) * (note_ids == note_before)
    local_state = jnp.einsum(
        "thp,ht,tn->hpn", x_rows, leave_rows, v_bc[:, :N], precision=precise,
        preferred_element_type=jnp.float32,
    )
    local_adjoint = jnp.einsum(
        "thp,ht,tn->hpn", g_rows, entry_rows, v_bc[:, N:], precision=precise,
        preferred_element_type=jnp.float32,
    )
    state_in = chain_in(local_state, keep, "seq", 1)
    adjoint_in = chain_in(local_adjoint, keep, "seq", -1)

    def local_forward(x_all, b_all, c_all, log_all):
        return block_forward_all(
            state_in, x_all, b_all, c_all, log_all, note_blocks, befores
        )

    _, pull = jax.vjp(local_forward, x_heads, b_blocks, c_blocks, log_blocks)
    grad_x_heads, grad_b, grad_c, grad_log = pull((grad_heads, adjoint_in))
    grad_log_decay = grad_log.reshape(head_count, tok_rows)
    grad_v_x = grad_x_heads.transpose(1, 2, 0, 3).reshape(tok_rows, head_count * P_SIZE)
    grad_v_bc = jnp.concatenate([grad_b.reshape(tok_rows, N), grad_c.reshape(tok_rows, N)], axis=1)
    grad_u_x = grad_v_x * silu_slope(u_x)
    grad_u_bc = grad_v_bc * silu_slope(u_bc)
    after_both = shifted(jnp.concatenate([grad_u_x[:rim_width], grad_u_bc[:rim_width]], axis=1), "seq", -1)
    after_x, after_bc = after_both[:, : grad_u_x.shape[1]], after_both[:, grad_u_x.shape[1] :]
    grad_pre_x = conv_backward(jnp.concatenate([grad_u_x, after_x]), conv_x, note_all[rim_width:])
    whole_bc = conv_backward(jnp.concatenate([grad_u_bc, after_bc]), conv_bc, note_all[rim_width:])
    grad_pre_bc = head_reduce(whole_bc)
    return (grad_pre_x, grad_pre_bc, grad_log_decay)


def solution(mesh):
    seq_size, head_size = mesh.shape["seq"], mesh.shape["head"]
    split = jax.sharding.Mesh(
        mesh.devices.reshape(seq_size, head_size // 2, 2), ("seq", "chip", "core")
    )
    head = ("chip", "core")
    placed = (
        P("seq", head),
        P("seq", None),
        P(None, head),
        P(),
        P(head, "seq"),
        P(),
        P("seq", head),
    )
    return jax.shard_map(
        local,
        mesh=split,
        in_specs=placed,
        out_specs=(P("seq", head), P(("seq",) + head, None), P(head, "seq")),
        check_vma=False,
    )
```

```python
import jax
import jax.numpy as jnp
from jax import lax
from jax.sharding import PartitionSpec as P

P_SIZE = 64
N = 128
K = 4
BLOCK = 256


precise = lax.Precision.HIGHEST


def shifted(value, axis, steps):
    count = lax.axis_size(axis)
    initial, last = (max(0, -steps), min(count, count - steps))
    return lax.ppermute(value, axis, [(source, source + steps) for source in range(initial, last)])


def entering(value, axis, join, neutral, backward):
    count, mine = (lax.axis_size(axis), lax.axis_index(axis))
    pieces = jax.tree.map(lambda part: lax.all_gather(part, axis), value)
    if backward:
        pieces = jax.tree.map(lambda part: part[::-1], pieces)
        mine = count - 1 - mine
    total = jax.tree.map(
        lambda part, zero: jnp.full_like(part, 0) + jnp.asarray(zero, part.dtype), value, neutral
    )

    def hop(position, total):
        longer = join(total, jax.tree.map(lambda part: part[position], pieces))
        return jax.tree.map(lambda new, old: jnp.where(position < mine, new, old), longer, total)

    return lax.fori_loop(0, count - 1, hop, total)


def matmul(left, right):
    return jnp.dot(left, right, precision=precise, preferred_element_type=jnp.float32)


def note_index(positions, lengths):
    starts = jnp.cumsum(lengths) - lengths
    hits = (positions[:, None] >= starts[None, :]).astype(jnp.int32)
    return jnp.sum(hits, axis=1) - 1


def block_edges(log_block, note_block, note_before):
    cumul = jnp.cumsum(log_block)
    entry = jnp.exp(cumul) * (note_block == note_before)
    leave = jnp.exp(cumul[-1] - cumul) * (note_block == note_block[-1])
    through = jnp.exp(cumul[-1]) * (note_block[-1] == note_before)
    return (cumul, entry, leave, through)


def block_forward(state, x_block, b_block, c_block, log_block, note_block, note_before):
    cumul, entry, leave, through = block_edges(log_block, note_block, note_before)
    length = note_block.shape[0]
    lower = jnp.arange(length)[:, None] >= jnp.arange(length)[None, :]
    linked = lower & (note_block[:, None] == note_block[None, :])
    decay_matrix = jnp.exp(jnp.where(linked, cumul[:, None] - cumul[None, :], 0.0)) * linked
    scores = matmul(c_block, b_block.T) * decay_matrix
    output = matmul(scores, x_block) + entry[:, None] * matmul(c_block, state.T)
    updated = through * state + matmul((x_block * leave[:, None]).T, b_block)
    return (output, updated)


def head_forward(state, x_head, b_blocks, c_blocks, log_head, note_blocks, befores):

    def head_advance(carry, block):
        output, updated = block_forward(carry, *block)
        return (updated, output)

    final, outputs = lax.scan(
        head_advance, state, (x_head, b_blocks, c_blocks, log_head, note_blocks, befores)
    )
    return (outputs, final)


def conv_forward(extended, weights, note_ext):
    width = weights.shape[0]
    count = extended.shape[0] - width + 1
    result = jnp.zeros((count, extended.shape[1]), jnp.float32)
    for k in range(width):
        linked = note_ext[k : k + count] == note_ext[width - 1 : width - 1 + count]
        result = result + weights[k][None, :] * extended[k : k + count] * linked[:, None]
    return result


def conv_backward(extended, weights, note_ext):
    width = weights.shape[0]
    count = extended.shape[0] - width + 1
    result = jnp.zeros((count, extended.shape[1]), jnp.float32)
    for k in range(width):
        lag = width - 1 - k
        linked = note_ext[lag : lag + count] == note_ext[:count]
        result = result + weights[k][None, :] * extended[lag : lag + count] * linked[:, None]
    return result


def silu_slope(values):
    sigma = jax.nn.sigmoid(values)
    return sigma * (1.0 + values * (1.0 - sigma))


def chain_combine(earlier, later):
    return (earlier[0] * later[0], later[0][:, None, None] * earlier[1] + later[1])


def chain_in(value, keep, axis, direction):
    count = lax.axis_size(axis)
    packed = jnp.concatenate(
        [value.reshape(value.shape[0], -1), jnp.broadcast_to(keep[:, None], (keep.shape[0], 128))], axis=1
    )
    total = jnp.zeros_like(value)
    scale = jnp.ones_like(keep)
    for distance in range(1, count):
        arrived = shifted(packed, axis, direction * distance)
        part = arrived[:, : value[0].size].reshape(value.shape)
        total = total + scale[:, None, None] * part
        scale = scale * arrived[:, value[0].size]
    return total


def running_sum(values):
    length = values.shape[-1]
    upper = (jnp.arange(length)[:, None] <= jnp.arange(length)[None, :]).astype(values.dtype)
    return jnp.dot(values, upper, precision=precise, preferred_element_type=jnp.float32)


def chain_both(state, adjoint, keep, axis):
    count, mine = lax.axis_size(axis), lax.axis_index(axis)
    heads, size = state.shape[0], state[0].size
    tail = jnp.broadcast_to(keep[:, None], (heads, 128))
    later = jnp.concatenate([state.reshape(heads, size), tail], axis=1)
    earlier = jnp.concatenate([adjoint.reshape(heads, size), tail], axis=1)
    targets = jnp.arange(count)[:, None, None]
    outgoing = jnp.where(targets > mine, later[None], jnp.where(targets < mine, earlier[None], 0.0))
    arrived = lax.all_to_all(outgoing, axis, 0, 0, tiled=False)
    parts = arrived[:, :, :size].reshape((count,) + state.shape)
    keeps = arrived[:, :, size]
    totals = []
    for order in (range(count - 1, -1, -1), range(count)):
        total = jnp.zeros_like(state)
        scale = jnp.ones_like(keep)
        for source in order:
            near = (source < mine) if order.step < 0 else (source > mine)
            total = total + jnp.where(near, scale, 0.0)[:, None, None] * parts[source]
            scale = jnp.where(near, scale * keeps[source], scale)
        totals.append(total)
    return totals[0], totals[1]


def einsum(spec, *operands):
    return jnp.einsum(spec, *operands, precision=precise, preferred_element_type=jnp.float32)


def block_forward_all(state, x_all, b_all, c_all, log_all, note_blocks, befores):
    cumul = running_sum(log_all)
    entry = jnp.exp(cumul) * (note_blocks == befores[:, None])
    leave = jnp.exp(cumul[..., -1:] - cumul) * (note_blocks == note_blocks[:, -1:])
    through = jnp.exp(cumul[..., -1]) * (note_blocks[:, -1] == befores)
    length = note_blocks.shape[1]
    lower = jnp.arange(length)[:, None] >= jnp.arange(length)[None, :]
    linked = lower & (note_blocks[:, :, None] == note_blocks[:, None, :])
    differences = cumul[..., :, None] - cumul[..., None, :]
    decay_matrix = jnp.exp(jnp.where(linked, differences, 0.0)) * linked
    scores = einsum("bin,bjn->bij", c_all, b_all) * decay_matrix
    output = einsum("hbij,hbjp->hbip", scores, x_all)
    chunk = einsum("hbjp,bjn->hbpn", x_all * leave[..., None], b_all)
    starts = []
    for block in range(note_blocks.shape[0]):
        starts.append(state)
        state = through[:, block, None, None] * state + chunk[:, block]
    output = output + entry[..., None] * einsum("bin,hbpn->hbip", c_all, jnp.stack(starts, axis=1))
    return (output, state)


def local(pre_x, pre_bc, conv_x, conv_bc, log_decay, lengths, grad_out):
    tok_rows = pre_x.shape[0]
    head_count = log_decay.shape[0]
    rim_width = K - 1
    block_count = tok_rows // BLOCK
    seq_start = lax.axis_index("seq") * tok_rows
    positions = seq_start + jnp.arange(-rim_width, tok_rows + rim_width)
    note_all = note_index(positions, lengths)
    note_ids = note_all[rim_width : rim_width + tok_rows]
    before_both = shifted(
        jnp.concatenate([pre_x[tok_rows - rim_width :], pre_bc[tok_rows - rim_width :]], axis=1), "seq", 1
    )
    before_x, before_bc = before_both[:, : pre_x.shape[1]], before_both[:, pre_x.shape[1] :]
    u_x = conv_forward(
        jnp.concatenate([before_x, pre_x]).astype(jnp.float32),
        conv_x,
        note_all[: tok_rows + rim_width],
    )
    u_bc = conv_forward(
        jnp.concatenate([before_bc, pre_bc]).astype(jnp.float32),
        conv_bc,
        note_all[: tok_rows + rim_width],
    )
    v_x = jax.nn.silu(u_x)
    v_bc = jax.nn.silu(u_bc)
    x_heads = v_x.reshape(block_count, BLOCK, head_count, P_SIZE).transpose(2, 0, 1, 3)
    b_blocks = v_bc[:, :N].reshape(block_count, BLOCK, N)
    c_blocks = v_bc[:, N:].reshape(block_count, BLOCK, N)
    log_blocks = log_decay.reshape(head_count, block_count, BLOCK)
    grad_heads = (
        grad_out.astype(jnp.float32)
        .reshape(block_count, BLOCK, head_count, P_SIZE)
        .transpose(2, 0, 1, 3)
    )
    note_blocks = note_ids.reshape(block_count, BLOCK)
    befores = jnp.concatenate([note_all[rim_width - 1 : rim_width], note_blocks[:-1, -1]])

    note_before = note_all[rim_width - 1]
    log_rows = log_decay.astype(jnp.float32)
    x_rows = v_x.reshape(tok_rows, head_count, P_SIZE)
    g_rows = grad_out.astype(jnp.float32).reshape(tok_rows, head_count, P_SIZE)
    shard_cumul = running_sum(log_rows)
    keep = jnp.exp(shard_cumul[:, -1]) * (note_ids[-1] == note_before)
    leave_rows = jnp.exp(shard_cumul[:, -1:] - shard_cumul) * (note_ids == note_ids[-1])
    entry_rows = jnp.exp(shard_cumul) * (note_ids == note_before)
    local_state = jnp.einsum(
        "thp,ht,tn->hpn", x_rows, leave_rows, v_bc[:, :N], precision=precise,
        preferred_element_type=jnp.float32,
    )
    local_adjoint = jnp.einsum(
        "thp,ht,tn->hpn", g_rows, entry_rows, v_bc[:, N:], precision=precise,
        preferred_element_type=jnp.float32,
    )
    state_in, adjoint_in = chain_both(local_state, local_adjoint, keep, "seq")

    def local_forward(x_all, b_all, c_all, log_all):
        return block_forward_all(
            state_in, x_all, b_all, c_all, log_all, note_blocks, befores
        )

    _, pull = jax.vjp(local_forward, x_heads, b_blocks, c_blocks, log_blocks)
    grad_x_heads, grad_b, grad_c, grad_log = pull((grad_heads, adjoint_in))
    grad_log_decay = grad_log.reshape(head_count, tok_rows)
    grad_v_x = grad_x_heads.transpose(1, 2, 0, 3).reshape(tok_rows, head_count * P_SIZE)
    grad_v_bc = jnp.concatenate([grad_b.reshape(tok_rows, N), grad_c.reshape(tok_rows, N)], axis=1)
    grad_u_x = grad_v_x * silu_slope(u_x)
    grad_u_bc = grad_v_bc * silu_slope(u_bc)
    after_both = shifted(jnp.concatenate([grad_u_x[:rim_width], grad_u_bc[:rim_width]], axis=1), "seq", -1)
    after_x, after_bc = after_both[:, : grad_u_x.shape[1]], after_both[:, grad_u_x.shape[1] :]
    grad_pre_x = conv_backward(jnp.concatenate([grad_u_x, after_x]), conv_x, note_all[rim_width:])
    whole_bc = conv_backward(jnp.concatenate([grad_u_bc, after_bc]), conv_bc, note_all[rim_width:])
    chips, cores = lax.axis_size("chip"), lax.axis_size("core")
    pieces = whole_bc.reshape(chips, cores, tok_rows // (chips * cores), whole_bc.shape[1])
    core = lax.axis_index("core")
    mine = lax.dynamic_index_in_dim(pieces, core, 1, keepdims=False)
    other = lax.dynamic_index_in_dim(pieces, 1 - core, 1, keepdims=False)
    pair_sum = mine + lax.ppermute(other, "core", [(0, 1), (1, 0)])
    grad_pre_bc = lax.all_to_all(pair_sum, "chip", 0, 0, tiled=False).sum(0)
    return (grad_pre_x, grad_pre_bc, grad_log_decay)


def solution(mesh):
    seq_size, head_size = mesh.shape["seq"], mesh.shape["head"]
    split = jax.sharding.Mesh(
        mesh.devices.reshape(seq_size, head_size // 2, 2), ("seq", "chip", "core")
    )
    head = ("chip", "core")
    placed = (
        P("seq", head),
        P("seq", None),
        P(None, head),
        P(),
        P(head, "seq"),
        P(),
        P("seq", head),
    )
    return jax.shard_map(
        local,
        mesh=split,
        in_specs=placed,
        out_specs=(P("seq", head), P(("seq",) + head, None), P(head, "seq")),
        check_vma=False,
    )
```

```python
import jax
import jax.numpy as jnp
from jax import lax
from jax.sharding import PartitionSpec as P

P_SIZE = 64
N = 128
K = 4
BLOCK = 256


precise = lax.Precision.HIGHEST


def shifted(value, axis, steps):
    count = lax.axis_size(axis)
    initial, last = (max(0, -steps), min(count, count - steps))
    return lax.ppermute(value, axis, [(source, source + steps) for source in range(initial, last)])


def entering(value, axis, join, neutral, backward):
    count, mine = (lax.axis_size(axis), lax.axis_index(axis))
    pieces = jax.tree.map(lambda part: lax.all_gather(part, axis), value)
    if backward:
        pieces = jax.tree.map(lambda part: part[::-1], pieces)
        mine = count - 1 - mine
    total = jax.tree.map(
        lambda part, zero: jnp.full_like(part, 0) + jnp.asarray(zero, part.dtype), value, neutral
    )

    def hop(position, total):
        longer = join(total, jax.tree.map(lambda part: part[position], pieces))
        return jax.tree.map(lambda new, old: jnp.where(position < mine, new, old), longer, total)

    return lax.fori_loop(0, count - 1, hop, total)


def matmul(left, right):
    return jnp.dot(left, right, precision=precise, preferred_element_type=jnp.float32)


def note_index(positions, lengths):
    starts = jnp.cumsum(lengths) - lengths
    hits = (positions[:, None] >= starts[None, :]).astype(jnp.int32)
    return jnp.sum(hits, axis=1) - 1


def block_edges(log_block, note_block, note_before):
    cumul = jnp.cumsum(log_block)
    entry = jnp.exp(cumul) * (note_block == note_before)
    leave = jnp.exp(cumul[-1] - cumul) * (note_block == note_block[-1])
    through = jnp.exp(cumul[-1]) * (note_block[-1] == note_before)
    return (cumul, entry, leave, through)


def block_forward(state, x_block, b_block, c_block, log_block, note_block, note_before):
    cumul, entry, leave, through = block_edges(log_block, note_block, note_before)
    length = note_block.shape[0]
    lower = jnp.arange(length)[:, None] >= jnp.arange(length)[None, :]
    linked = lower & (note_block[:, None] == note_block[None, :])
    decay_matrix = jnp.exp(jnp.where(linked, cumul[:, None] - cumul[None, :], 0.0)) * linked
    scores = matmul(c_block, b_block.T) * decay_matrix
    output = matmul(scores, x_block) + entry[:, None] * matmul(c_block, state.T)
    updated = through * state + matmul((x_block * leave[:, None]).T, b_block)
    return (output, updated)


def head_forward(state, x_head, b_blocks, c_blocks, log_head, note_blocks, befores):

    def head_advance(carry, block):
        output, updated = block_forward(carry, *block)
        return (updated, output)

    final, outputs = lax.scan(
        head_advance, state, (x_head, b_blocks, c_blocks, log_head, note_blocks, befores)
    )
    return (outputs, final)


def conv_forward(extended, weights, note_ext):
    width = weights.shape[0]
    count = extended.shape[0] - width + 1
    result = jnp.zeros((count, extended.shape[1]), jnp.float32)
    for k in range(width):
        linked = note_ext[k : k + count] == note_ext[width - 1 : width - 1 + count]
        result = result + weights[k][None, :] * extended[k : k + count] * linked[:, None]
    return result


def conv_backward(extended, weights, note_ext):
    width = weights.shape[0]
    count = extended.shape[0] - width + 1
    result = jnp.zeros((count, extended.shape[1]), jnp.float32)
    for k in range(width):
        lag = width - 1 - k
        linked = note_ext[lag : lag + count] == note_ext[:count]
        result = result + weights[k][None, :] * extended[lag : lag + count] * linked[:, None]
    return result


def silu_slope(values):
    sigma = jax.nn.sigmoid(values)
    return sigma * (1.0 + values * (1.0 - sigma))


def chain_combine(earlier, later):
    return (earlier[0] * later[0], later[0][:, None, None] * earlier[1] + later[1])


def chain_in(value, keep, axis, direction):
    count = lax.axis_size(axis)
    packed = jnp.concatenate(
        [value.reshape(value.shape[0], -1), jnp.broadcast_to(keep[:, None], (keep.shape[0], 128))], axis=1
    )
    total = jnp.zeros_like(value)
    scale = jnp.ones_like(keep)
    for distance in range(1, count):
        arrived = shifted(packed, axis, direction * distance)
        part = arrived[:, : value[0].size].reshape(value.shape)
        total = total + scale[:, None, None] * part
        scale = scale * arrived[:, value[0].size]
    return total


def running_sum(values):
    length = values.shape[-1]
    upper = (jnp.arange(length)[:, None] <= jnp.arange(length)[None, :]).astype(values.dtype)
    return jnp.dot(values, upper, precision=precise, preferred_element_type=jnp.float32)


def chain_both(state, adjoint, keep, axis):
    count, mine = lax.axis_size(axis), lax.axis_index(axis)
    heads, size = state.shape[0], state[0].size
    tail = jnp.broadcast_to(keep[:, None], (heads, 128))
    later = jnp.concatenate([state.reshape(heads, size), tail], axis=1)
    earlier = jnp.concatenate([adjoint.reshape(heads, size), tail], axis=1)
    targets = jnp.arange(count)[:, None, None]
    outgoing = jnp.where(targets > mine, later[None], jnp.where(targets < mine, earlier[None], 0.0))
    arrived = lax.all_to_all(outgoing, axis, 0, 0, tiled=False)
    parts = arrived[:, :, :size].reshape((count,) + state.shape)
    keeps = arrived[:, :, size]
    totals = []
    for order in (range(count - 1, -1, -1), range(count)):
        total = jnp.zeros_like(state)
        scale = jnp.ones_like(keep)
        for source in order:
            near = (source < mine) if order.step < 0 else (source > mine)
            total = total + jnp.where(near, scale, 0.0)[:, None, None] * parts[source]
            scale = jnp.where(near, scale * keeps[source], scale)
        totals.append(total)
    return totals[0], totals[1]


def einsum(spec, *operands):
    return jnp.einsum(spec, *operands, precision=lax.Precision.HIGH, preferred_element_type=jnp.float32)


def block_forward_all(state, x_all, b_all, c_all, log_all, note_blocks, befores):
    cumul = running_sum(log_all)
    entry = jnp.exp(cumul) * (note_blocks == befores[:, None])
    leave = jnp.exp(cumul[..., -1:] - cumul) * (note_blocks == note_blocks[:, -1:])
    through = jnp.exp(cumul[..., -1]) * (note_blocks[:, -1] == befores)
    length = note_blocks.shape[1]
    lower = jnp.arange(length)[:, None] >= jnp.arange(length)[None, :]
    linked = lower & (note_blocks[:, :, None] == note_blocks[:, None, :])
    differences = cumul[..., :, None] - cumul[..., None, :]
    decay_matrix = jnp.exp(jnp.where(linked, differences, 0.0)) * linked
    scores = einsum("bin,bjn->bij", c_all, b_all) * decay_matrix
    output = einsum("hbij,hbjp->hbip", scores, x_all)
    chunk = einsum("hbjp,bjn->hbpn", x_all * leave[..., None], b_all)
    starts = []
    for block in range(note_blocks.shape[0]):
        starts.append(state)
        state = through[:, block, None, None] * state + chunk[:, block]
    output = output + entry[..., None] * einsum("bin,hbpn->hbip", c_all, jnp.stack(starts, axis=1))
    return (output, state)


def local(pre_x, pre_bc, conv_x, conv_bc, log_decay, lengths, grad_out):
    tok_rows = pre_x.shape[0]
    head_count = log_decay.shape[0]
    rim_width = K - 1
    block_count = tok_rows // BLOCK
    seq_start = lax.axis_index("seq") * tok_rows
    positions = seq_start + jnp.arange(-rim_width, tok_rows + rim_width)
    note_all = note_index(positions, lengths)
    note_ids = note_all[rim_width : rim_width + tok_rows]
    before_both = shifted(
        jnp.concatenate([pre_x[tok_rows - rim_width :], pre_bc[tok_rows - rim_width :]], axis=1), "seq", 1
    )
    before_x, before_bc = before_both[:, : pre_x.shape[1]], before_both[:, pre_x.shape[1] :]
    u_x = conv_forward(
        jnp.concatenate([before_x, pre_x]).astype(jnp.float32),
        conv_x,
        note_all[: tok_rows + rim_width],
    )
    u_bc = conv_forward(
        jnp.concatenate([before_bc, pre_bc]).astype(jnp.float32),
        conv_bc,
        note_all[: tok_rows + rim_width],
    )
    v_x = jax.nn.silu(u_x)
    v_bc = jax.nn.silu(u_bc)
    x_heads = v_x.reshape(block_count, BLOCK, head_count, P_SIZE).transpose(2, 0, 1, 3)
    b_blocks = v_bc[:, :N].reshape(block_count, BLOCK, N)
    c_blocks = v_bc[:, N:].reshape(block_count, BLOCK, N)
    log_blocks = log_decay.reshape(head_count, block_count, BLOCK)
    grad_heads = (
        grad_out.astype(jnp.float32)
        .reshape(block_count, BLOCK, head_count, P_SIZE)
        .transpose(2, 0, 1, 3)
    )
    note_blocks = note_ids.reshape(block_count, BLOCK)
    befores = jnp.concatenate([note_all[rim_width - 1 : rim_width], note_blocks[:-1, -1]])

    note_before = note_all[rim_width - 1]
    log_rows = log_decay.astype(jnp.float32)
    x_rows = v_x.reshape(tok_rows, head_count, P_SIZE)
    g_rows = grad_out.astype(jnp.float32).reshape(tok_rows, head_count, P_SIZE)
    shard_cumul = running_sum(log_rows)
    keep = jnp.exp(shard_cumul[:, -1]) * (note_ids[-1] == note_before)
    leave_rows = jnp.exp(shard_cumul[:, -1:] - shard_cumul) * (note_ids == note_ids[-1])
    entry_rows = jnp.exp(shard_cumul) * (note_ids == note_before)
    local_state = jnp.einsum(
        "thp,ht,tn->hpn", x_rows, leave_rows, v_bc[:, :N], precision=precise,
        preferred_element_type=jnp.float32,
    )
    local_adjoint = jnp.einsum(
        "thp,ht,tn->hpn", g_rows, entry_rows, v_bc[:, N:], precision=precise,
        preferred_element_type=jnp.float32,
    )
    state_in, adjoint_in = chain_both(local_state, local_adjoint, keep, "seq")

    def local_forward(x_all, b_all, c_all, log_all):
        return block_forward_all(
            state_in, x_all, b_all, c_all, log_all, note_blocks, befores
        )

    _, pull = jax.vjp(local_forward, x_heads, b_blocks, c_blocks, log_blocks)
    grad_x_heads, grad_b, grad_c, grad_log = pull((grad_heads, adjoint_in))
    grad_log_decay = grad_log.reshape(head_count, tok_rows)
    grad_v_x = grad_x_heads.transpose(1, 2, 0, 3).reshape(tok_rows, head_count * P_SIZE)
    grad_v_bc = jnp.concatenate([grad_b.reshape(tok_rows, N), grad_c.reshape(tok_rows, N)], axis=1)
    grad_u_x = grad_v_x * silu_slope(u_x)
    grad_u_bc = grad_v_bc * silu_slope(u_bc)
    after_both = shifted(jnp.concatenate([grad_u_x[:rim_width], grad_u_bc[:rim_width]], axis=1), "seq", -1)
    after_x, after_bc = after_both[:, : grad_u_x.shape[1]], after_both[:, grad_u_x.shape[1] :]
    grad_pre_x = conv_backward(jnp.concatenate([grad_u_x, after_x]), conv_x, note_all[rim_width:])
    whole_bc = conv_backward(jnp.concatenate([grad_u_bc, after_bc]), conv_bc, note_all[rim_width:])
    chips, cores = lax.axis_size("chip"), lax.axis_size("core")
    pieces = whole_bc.reshape(chips, cores, tok_rows // (chips * cores), whole_bc.shape[1])
    core = lax.axis_index("core")
    mine = lax.dynamic_index_in_dim(pieces, core, 1, keepdims=False)
    other = lax.dynamic_index_in_dim(pieces, 1 - core, 1, keepdims=False)
    pair_sum = mine + lax.ppermute(other, "core", [(0, 1), (1, 0)])
    grad_pre_bc = lax.all_to_all(pair_sum, "chip", 0, 0, tiled=False).sum(0)
    return (grad_pre_x, grad_pre_bc, grad_log_decay)


def solution(mesh):
    seq_size, head_size = mesh.shape["seq"], mesh.shape["head"]
    split = jax.sharding.Mesh(
        mesh.devices.reshape(seq_size, head_size // 2, 2), ("seq", "chip", "core")
    )
    head = ("chip", "core")
    placed = (
        P("seq", head),
        P("seq", None),
        P(None, head),
        P(),
        P(head, "seq"),
        P(),
        P("seq", head),
    )
    return jax.shard_map(
        local,
        mesh=split,
        in_specs=placed,
        out_specs=(P("seq", head), P(("seq",) + head, None), P(head, "seq")),
        check_vma=False,
    )
```

```python
import functools
import jax
import jax.numpy as jnp
from jax import lax
from jax.experimental import pallas as pl
from jax.experimental.pallas import tpu as pltpu
from jax.sharding import PartitionSpec as P

MESH = pl.DeviceIdType.MESH

P_SIZE = 64
N = 128
K = 4
BLOCK = 256


precise = lax.Precision.HIGHEST


def shifted(value, axis, steps):
    count = lax.axis_size(axis)
    initial, last = (max(0, -steps), min(count, count - steps))
    return lax.ppermute(value, axis, [(source, source + steps) for source in range(initial, last)])


def entering(value, axis, join, neutral, backward):
    count, mine = (lax.axis_size(axis), lax.axis_index(axis))
    pieces = jax.tree.map(lambda part: lax.all_gather(part, axis), value)
    if backward:
        pieces = jax.tree.map(lambda part: part[::-1], pieces)
        mine = count - 1 - mine
    total = jax.tree.map(
        lambda part, zero: jnp.full_like(part, 0) + jnp.asarray(zero, part.dtype), value, neutral
    )

    def hop(position, total):
        longer = join(total, jax.tree.map(lambda part: part[position], pieces))
        return jax.tree.map(lambda new, old: jnp.where(position < mine, new, old), longer, total)

    return lax.fori_loop(0, count - 1, hop, total)


def matmul(left, right):
    return jnp.dot(left, right, precision=precise, preferred_element_type=jnp.float32)


def note_index(positions, lengths):
    starts = jnp.cumsum(lengths) - lengths
    hits = (positions[:, None] >= starts[None, :]).astype(jnp.int32)
    return jnp.sum(hits, axis=1) - 1


def block_edges(log_block, note_block, note_before):
    cumul = jnp.cumsum(log_block)
    entry = jnp.exp(cumul) * (note_block == note_before)
    leave = jnp.exp(cumul[-1] - cumul) * (note_block == note_block[-1])
    through = jnp.exp(cumul[-1]) * (note_block[-1] == note_before)
    return (cumul, entry, leave, through)


def block_forward(state, x_block, b_block, c_block, log_block, note_block, note_before):
    cumul, entry, leave, through = block_edges(log_block, note_block, note_before)
    length = note_block.shape[0]
    lower = jnp.arange(length)[:, None] >= jnp.arange(length)[None, :]
    linked = lower & (note_block[:, None] == note_block[None, :])
    decay_matrix = jnp.exp(jnp.where(linked, cumul[:, None] - cumul[None, :], 0.0)) * linked
    scores = matmul(c_block, b_block.T) * decay_matrix
    output = matmul(scores, x_block) + entry[:, None] * matmul(c_block, state.T)
    updated = through * state + matmul((x_block * leave[:, None]).T, b_block)
    return (output, updated)


def head_forward(state, x_head, b_blocks, c_blocks, log_head, note_blocks, befores):

    def head_advance(carry, block):
        output, updated = block_forward(carry, *block)
        return (updated, output)

    final, outputs = lax.scan(
        head_advance, state, (x_head, b_blocks, c_blocks, log_head, note_blocks, befores)
    )
    return (outputs, final)


def conv_forward(extended, weights, note_ext):
    width = weights.shape[0]
    count = extended.shape[0] - width + 1
    result = jnp.zeros((count, extended.shape[1]), jnp.float32)
    for k in range(width):
        linked = note_ext[k : k + count] == note_ext[width - 1 : width - 1 + count]
        result = result + weights[k][None, :] * extended[k : k + count] * linked[:, None]
    return result


def conv_backward(extended, weights, note_ext):
    width = weights.shape[0]
    count = extended.shape[0] - width + 1
    result = jnp.zeros((count, extended.shape[1]), jnp.float32)
    for k in range(width):
        lag = width - 1 - k
        linked = note_ext[lag : lag + count] == note_ext[:count]
        result = result + weights[k][None, :] * extended[lag : lag + count] * linked[:, None]
    return result


def silu_slope(values):
    sigma = jax.nn.sigmoid(values)
    return sigma * (1.0 + values * (1.0 - sigma))


def chain_combine(earlier, later):
    return (earlier[0] * later[0], later[0][:, None, None] * earlier[1] + later[1])


def chain_in(value, keep, axis, direction):
    count = lax.axis_size(axis)
    packed = jnp.concatenate(
        [value.reshape(value.shape[0], -1), jnp.broadcast_to(keep[:, None], (keep.shape[0], 128))], axis=1
    )
    total = jnp.zeros_like(value)
    scale = jnp.ones_like(keep)
    for distance in range(1, count):
        arrived = shifted(packed, axis, direction * distance)
        part = arrived[:, : value[0].size].reshape(value.shape)
        total = total + scale[:, None, None] * part
        scale = scale * arrived[:, value[0].size]
    return total


def running_sum(values):
    length = values.shape[-1]
    upper = (jnp.arange(length)[:, None] <= jnp.arange(length)[None, :]).astype(values.dtype)
    return jnp.dot(values, upper, precision=precise, preferred_element_type=jnp.float32)


def chain_both(state, adjoint, keep, axis):
    count, mine = lax.axis_size(axis), lax.axis_index(axis)
    heads, size = state.shape[0], state[0].size
    tail = jnp.broadcast_to(keep[:, None], (heads, 128))
    later = jnp.concatenate([state.reshape(heads, size), tail], axis=1)
    earlier = jnp.concatenate([adjoint.reshape(heads, size), tail], axis=1)
    targets = jnp.arange(count)[:, None, None]
    outgoing = jnp.where(targets > mine, later[None], jnp.where(targets < mine, earlier[None], 0.0))
    arrived = lax.all_to_all(outgoing, axis, 0, 0, tiled=False)
    parts = arrived[:, :, :size].reshape((count,) + state.shape)
    keeps = arrived[:, :, size]
    totals = []
    for order in (range(count - 1, -1, -1), range(count)):
        total = jnp.zeros_like(state)
        scale = jnp.ones_like(keep)
        for source in order:
            near = (source < mine) if order.step < 0 else (source > mine)
            total = total + jnp.where(near, scale, 0.0)[:, None, None] * parts[source]
            scale = jnp.where(near, scale * keeps[source], scale)
        totals.append(total)
    return totals[0], totals[1]


def einsum(spec, *operands):
    return jnp.einsum(spec, *operands, precision=lax.Precision.HIGH, preferred_element_type=jnp.float32)


def block_forward_all(state, x_all, b_all, c_all, log_all, note_blocks, befores):
    cumul = running_sum(log_all)
    entry = jnp.exp(cumul) * (note_blocks == befores[:, None])
    leave = jnp.exp(cumul[..., -1:] - cumul) * (note_blocks == note_blocks[:, -1:])
    through = jnp.exp(cumul[..., -1]) * (note_blocks[:, -1] == befores)
    length = note_blocks.shape[1]
    lower = jnp.arange(length)[:, None] >= jnp.arange(length)[None, :]
    linked = lower & (note_blocks[:, :, None] == note_blocks[:, None, :])
    differences = cumul[..., :, None] - cumul[..., None, :]
    decay_matrix = jnp.exp(jnp.where(linked, differences, 0.0)) * linked
    scores = einsum("bin,bjn->bij", c_all, b_all) * decay_matrix
    output = einsum("hbij,hbjp->hbip", scores, x_all)
    chunk = einsum("hbjp,bjn->hbpn", x_all * leave[..., None], b_all)
    starts = []
    for block in range(note_blocks.shape[0]):
        starts.append(state)
        state = through[:, block, None, None] * state + chunk[:, block]
    output = output + entry[..., None] * einsum("bin,hbpn->hbip", c_all, jnp.stack(starts, axis=1))
    return (output, state)


def reduce_kernel(count, pieces_ref, out_ref, landed, send_sems, recv_sems):
    seq, core = lax.axis_index("seq"), lax.axis_index("core")
    me = lax.axis_index("chip")

    def place(peer):
        return (seq, peer, core)

    barrier = pltpu.get_barrier_semaphore()

    def greet(step, carry):
        peer = lax.rem(me + step, count)
        pl.semaphore_signal(barrier, inc=1, device_id=place(peer), device_id_type=MESH)
        return carry

    lax.fori_loop(1, count, greet, 0)
    pl.semaphore_wait(barrier, count - 1)

    def outgoing(step):
        peer = lax.rem(me + step, count)
        return pltpu.make_async_remote_copy(
            src_ref=pieces_ref.at[peer],
            dst_ref=landed.at[count - 1 - step],
            send_sem=send_sems.at[step - 1],
            recv_sem=recv_sems.at[count - 1 - step],
            device_id=place(peer),
            device_id_type=MESH,
        )

    def send(step, carry):
        outgoing(step).start()
        return carry

    lax.fori_loop(1, count, send, 0)

    def finish(step, carry):
        outgoing(step).wait_send()
        outgoing(count - step).wait_recv()
        return carry

    lax.fori_loop(1, count, finish, 0)

    def accumulate(slot, total):
        return total + landed[slot]

    out_ref[...] = lax.fori_loop(0, count - 1, accumulate, pieces_ref[me])


def chip_reduce(pieces):
    count, rows, columns = pieces.shape
    return pl.pallas_call(
        functools.partial(reduce_kernel, count),
        out_shape=jax.ShapeDtypeStruct((rows, columns), jnp.float32),
        in_specs=[pl.BlockSpec(memory_space=pltpu.VMEM)],
        out_specs=pl.BlockSpec(memory_space=pltpu.VMEM),
        scratch_shapes=[
            pltpu.VMEM((count - 1, rows, columns), jnp.float32),
            pltpu.SemaphoreType.DMA((count - 1,)),
            pltpu.SemaphoreType.DMA((count - 1,)),
        ],
        compiler_params=pltpu.CompilerParams(collective_id=0, has_side_effects=True),
    )(pieces)


def local(pre_x, pre_bc, conv_x, conv_bc, log_decay, lengths, grad_out):
    tok_rows = pre_x.shape[0]
    head_count = log_decay.shape[0]
    rim_width = K - 1
    block_count = tok_rows // BLOCK
    seq_start = lax.axis_index("seq") * tok_rows
    positions = seq_start + jnp.arange(-rim_width, tok_rows + rim_width)
    note_all = note_index(positions, lengths)
    note_ids = note_all[rim_width : rim_width + tok_rows]
    before_both = shifted(
        jnp.concatenate([pre_x[tok_rows - rim_width :], pre_bc[tok_rows - rim_width :]], axis=1), "seq", 1
    )
    before_x, before_bc = before_both[:, : pre_x.shape[1]], before_both[:, pre_x.shape[1] :]
    u_x = conv_forward(
        jnp.concatenate([before_x, pre_x]).astype(jnp.float32),
        conv_x,
        note_all[: tok_rows + rim_width],
    )
    u_bc = conv_forward(
        jnp.concatenate([before_bc, pre_bc]).astype(jnp.float32),
        conv_bc,
        note_all[: tok_rows + rim_width],
    )
    v_x = jax.nn.silu(u_x)
    v_bc = jax.nn.silu(u_bc)
    x_heads = v_x.reshape(block_count, BLOCK, head_count, P_SIZE).transpose(2, 0, 1, 3)
    b_blocks = v_bc[:, :N].reshape(block_count, BLOCK, N)
    c_blocks = v_bc[:, N:].reshape(block_count, BLOCK, N)
    log_blocks = log_decay.reshape(head_count, block_count, BLOCK)
    grad_heads = (
        grad_out.astype(jnp.float32)
        .reshape(block_count, BLOCK, head_count, P_SIZE)
        .transpose(2, 0, 1, 3)
    )
    note_blocks = note_ids.reshape(block_count, BLOCK)
    befores = jnp.concatenate([note_all[rim_width - 1 : rim_width], note_blocks[:-1, -1]])

    note_before = note_all[rim_width - 1]
    log_rows = log_decay.astype(jnp.float32)
    x_rows = v_x.reshape(tok_rows, head_count, P_SIZE)
    g_rows = grad_out.astype(jnp.float32).reshape(tok_rows, head_count, P_SIZE)
    shard_cumul = running_sum(log_rows)
    keep = jnp.exp(shard_cumul[:, -1]) * (note_ids[-1] == note_before)
    leave_rows = jnp.exp(shard_cumul[:, -1:] - shard_cumul) * (note_ids == note_ids[-1])
    entry_rows = jnp.exp(shard_cumul) * (note_ids == note_before)
    local_state = jnp.einsum(
        "thp,ht,tn->hpn", x_rows, leave_rows, v_bc[:, :N], precision=precise,
        preferred_element_type=jnp.float32,
    )
    local_adjoint = jnp.einsum(
        "thp,ht,tn->hpn", g_rows, entry_rows, v_bc[:, N:], precision=precise,
        preferred_element_type=jnp.float32,
    )
    state_in, adjoint_in = chain_both(local_state, local_adjoint, keep, "seq")

    def local_forward(x_all, b_all, c_all, log_all):
        return block_forward_all(
            state_in, x_all, b_all, c_all, log_all, note_blocks, befores
        )

    _, pull = jax.vjp(local_forward, x_heads, b_blocks, c_blocks, log_blocks)
    grad_x_heads, grad_b, grad_c, grad_log = pull((grad_heads, adjoint_in))
    grad_log_decay = grad_log.reshape(head_count, tok_rows)
    grad_v_x = grad_x_heads.transpose(1, 2, 0, 3).reshape(tok_rows, head_count * P_SIZE)
    grad_v_bc = jnp.concatenate([grad_b.reshape(tok_rows, N), grad_c.reshape(tok_rows, N)], axis=1)
    grad_u_x = grad_v_x * silu_slope(u_x)
    grad_u_bc = grad_v_bc * silu_slope(u_bc)
    after_both = shifted(jnp.concatenate([grad_u_x[:rim_width], grad_u_bc[:rim_width]], axis=1), "seq", -1)
    after_x, after_bc = after_both[:, : grad_u_x.shape[1]], after_both[:, grad_u_x.shape[1] :]
    grad_pre_x = conv_backward(jnp.concatenate([grad_u_x, after_x]), conv_x, note_all[rim_width:])
    whole_bc = conv_backward(jnp.concatenate([grad_u_bc, after_bc]), conv_bc, note_all[rim_width:])
    chips, cores = lax.axis_size("chip"), lax.axis_size("core")
    pieces = whole_bc.reshape(chips, cores, tok_rows // (chips * cores), whole_bc.shape[1])
    core = lax.axis_index("core")
    mine = lax.dynamic_index_in_dim(pieces, core, 1, keepdims=False)
    other = lax.dynamic_index_in_dim(pieces, 1 - core, 1, keepdims=False)
    pair_sum = mine + lax.ppermute(other, "core", [(0, 1), (1, 0)])
    grad_pre_bc = chip_reduce(pair_sum)
    return (grad_pre_x, grad_pre_bc, grad_log_decay)


def solution(mesh):
    seq_size, head_size = mesh.shape["seq"], mesh.shape["head"]
    split = jax.sharding.Mesh(
        mesh.devices.reshape(seq_size, head_size // 2, 2), ("seq", "chip", "core")
    )
    head = ("chip", "core")
    placed = (
        P("seq", head),
        P("seq", None),
        P(None, head),
        P(),
        P(head, "seq"),
        P(),
        P("seq", head),
    )
    return jax.shard_map(
        local,
        mesh=split,
        in_specs=placed,
        out_specs=(P("seq", head), P(("seq",) + head, None), P(head, "seq")),
        check_vma=False,
    )
```

```python
import jax
import jax.numpy as jnp
from jax import lax
from jax.experimental import pallas as pl
from jax.experimental.pallas import tpu as pltpu
from jax.sharding import PartitionSpec as P

P_SIZE = 64
N = 128
K = 4
BLOCK = 256


precise = lax.Precision.HIGHEST


def shifted(value, axis, steps):
    count = lax.axis_size(axis)
    initial, last = (max(0, -steps), min(count, count - steps))
    return lax.ppermute(value, axis, [(source, source + steps) for source in range(initial, last)])


def entering(value, axis, join, neutral, backward):
    count, mine = (lax.axis_size(axis), lax.axis_index(axis))
    pieces = jax.tree.map(lambda part: lax.all_gather(part, axis), value)
    if backward:
        pieces = jax.tree.map(lambda part: part[::-1], pieces)
        mine = count - 1 - mine
    total = jax.tree.map(
        lambda part, zero: jnp.full_like(part, 0) + jnp.asarray(zero, part.dtype), value, neutral
    )

    def hop(position, total):
        longer = join(total, jax.tree.map(lambda part: part[position], pieces))
        return jax.tree.map(lambda new, old: jnp.where(position < mine, new, old), longer, total)

    return lax.fori_loop(0, count - 1, hop, total)


def matmul(left, right):
    return jnp.dot(left, right, precision=precise, preferred_element_type=jnp.float32)


def note_index(positions, lengths):
    starts = jnp.cumsum(lengths) - lengths
    hits = (positions[:, None] >= starts[None, :]).astype(jnp.int32)
    return jnp.sum(hits, axis=1) - 1


def block_edges(log_block, note_block, note_before):
    cumul = jnp.cumsum(log_block)
    entry = jnp.exp(cumul) * (note_block == note_before)
    leave = jnp.exp(cumul[-1] - cumul) * (note_block == note_block[-1])
    through = jnp.exp(cumul[-1]) * (note_block[-1] == note_before)
    return (cumul, entry, leave, through)


def block_forward(state, x_block, b_block, c_block, log_block, note_block, note_before):
    cumul, entry, leave, through = block_edges(log_block, note_block, note_before)
    length = note_block.shape[0]
    lower = jnp.arange(length)[:, None] >= jnp.arange(length)[None, :]
    linked = lower & (note_block[:, None] == note_block[None, :])
    decay_matrix = jnp.exp(jnp.where(linked, cumul[:, None] - cumul[None, :], 0.0)) * linked
    scores = matmul(c_block, b_block.T) * decay_matrix
    output = matmul(scores, x_block) + entry[:, None] * matmul(c_block, state.T)
    updated = through * state + matmul((x_block * leave[:, None]).T, b_block)
    return (output, updated)


def head_forward(state, x_head, b_blocks, c_blocks, log_head, note_blocks, befores):

    def head_advance(carry, block):
        output, updated = block_forward(carry, *block)
        return (updated, output)

    final, outputs = lax.scan(
        head_advance, state, (x_head, b_blocks, c_blocks, log_head, note_blocks, befores)
    )
    return (outputs, final)


def conv_forward(extended, weights, note_ext):
    width = weights.shape[0]
    count = extended.shape[0] - width + 1
    result = jnp.zeros((count, extended.shape[1]), jnp.float32)
    for k in range(width):
        linked = note_ext[k : k + count] == note_ext[width - 1 : width - 1 + count]
        result = result + weights[k][None, :] * extended[k : k + count] * linked[:, None]
    return result


def conv_backward(extended, weights, note_ext):
    width = weights.shape[0]
    count = extended.shape[0] - width + 1
    result = jnp.zeros((count, extended.shape[1]), jnp.float32)
    for k in range(width):
        lag = width - 1 - k
        linked = note_ext[lag : lag + count] == note_ext[:count]
        result = result + weights[k][None, :] * extended[lag : lag + count] * linked[:, None]
    return result


def silu_slope(values):
    sigma = jax.nn.sigmoid(values)
    return sigma * (1.0 + values * (1.0 - sigma))


def chain_combine(earlier, later):
    return (earlier[0] * later[0], later[0][:, None, None] * earlier[1] + later[1])


def chain_in(value, keep, axis, direction):
    count = lax.axis_size(axis)
    packed = jnp.concatenate(
        [value.reshape(value.shape[0], -1), jnp.broadcast_to(keep[:, None], (keep.shape[0], 128))], axis=1
    )
    total = jnp.zeros_like(value)
    scale = jnp.ones_like(keep)
    for distance in range(1, count):
        arrived = shifted(packed, axis, direction * distance)
        part = arrived[:, : value[0].size].reshape(value.shape)
        total = total + scale[:, None, None] * part
        scale = scale * arrived[:, value[0].size]
    return total


def running_sum(values):
    length = values.shape[-1]
    upper = (jnp.arange(length)[:, None] <= jnp.arange(length)[None, :]).astype(values.dtype)
    return jnp.dot(values, upper, precision=precise, preferred_element_type=jnp.float32)


def chain_both(state, adjoint, keep, axis):
    count, mine = lax.axis_size(axis), lax.axis_index(axis)
    heads, size = state.shape[0], state[0].size
    tail = jnp.broadcast_to(keep[:, None], (heads, 128))
    later = jnp.concatenate([state.reshape(heads, size), tail], axis=1)
    earlier = jnp.concatenate([adjoint.reshape(heads, size), tail], axis=1)
    targets = jnp.arange(count)[:, None, None]
    outgoing = jnp.where(targets > mine, later[None], jnp.where(targets < mine, earlier[None], 0.0))
    arrived = lax.all_to_all(outgoing, axis, 0, 0, tiled=False)
    parts = arrived[:, :, :size].reshape((count,) + state.shape)
    keeps = arrived[:, :, size]
    totals = []
    for order in (range(count - 1, -1, -1), range(count)):
        total = jnp.zeros_like(state)
        scale = jnp.ones_like(keep)
        for source in order:
            near = (source < mine) if order.step < 0 else (source > mine)
            total = total + jnp.where(near, scale, 0.0)[:, None, None] * parts[source]
            scale = jnp.where(near, scale * keeps[source], scale)
        totals.append(total)
    return totals[0], totals[1]


def einsum(spec, *operands):
    return jnp.einsum(spec, *operands, precision=lax.Precision.HIGH, preferred_element_type=jnp.float32)


def block_forward_all(state, x_all, b_all, c_all, log_all, note_blocks, befores):
    cumul = running_sum(log_all)
    entry = jnp.exp(cumul) * (note_blocks == befores[:, None])
    leave = jnp.exp(cumul[..., -1:] - cumul) * (note_blocks == note_blocks[:, -1:])
    through = jnp.exp(cumul[..., -1]) * (note_blocks[:, -1] == befores)
    length = note_blocks.shape[1]
    lower = jnp.arange(length)[:, None] >= jnp.arange(length)[None, :]
    linked = lower & (note_blocks[:, :, None] == note_blocks[:, None, :])
    differences = cumul[..., :, None] - cumul[..., None, :]
    decay_matrix = jnp.exp(jnp.where(linked, differences, 0.0)) * linked
    scores = einsum("bin,bjn->bij", c_all, b_all) * decay_matrix
    output = einsum("hbij,hbjp->hbip", scores, x_all)
    chunk = einsum("hbjp,bjn->hbpn", x_all * leave[..., None], b_all)
    starts = []
    for block in range(note_blocks.shape[0]):
        starts.append(state)
        state = through[:, block, None, None] * state + chunk[:, block]
    output = output + entry[..., None] * einsum("bin,hbpn->hbip", c_all, jnp.stack(starts, axis=1))
    return (output, state)


def conv_silu_kernel(ext_x, ext_bc, taps_x, taps_bc, links, u_x, v_x, u_bc, v_bc):
    rows = u_x.shape[0]
    tile = 128
    for ext, taps, u, v in ((ext_x, taps_x, u_x, v_x), (ext_bc, taps_bc, u_bc, v_bc)):
        for start in range(0, rows, tile):
            total = jnp.zeros((tile, u.shape[1]), jnp.float32)
            for k in range(taps.shape[0]):
                total = total + taps[k : k + 1, :] * ext[start + k : start + k + tile, :] * links[
                    start : start + tile, k : k + 1
                ]
            u[start : start + tile, :] = total
            v[start : start + tile, :] = total / (1.0 + jnp.exp(-total))


def conv_silu(ext_x, ext_bc, taps_x, taps_bc, links):
    rows = links.shape[0]
    shapes = [
        jax.ShapeDtypeStruct((rows, ext_x.shape[1]), jnp.float32),
        jax.ShapeDtypeStruct((rows, ext_x.shape[1]), jnp.float32),
        jax.ShapeDtypeStruct((rows, ext_bc.shape[1]), jnp.float32),
        jax.ShapeDtypeStruct((rows, ext_bc.shape[1]), jnp.float32),
    ]
    return pl.pallas_call(
        conv_silu_kernel,
        out_shape=shapes,
        in_specs=[pl.BlockSpec(memory_space=pltpu.VMEM)] * 5,
        out_specs=[pl.BlockSpec(memory_space=pltpu.VMEM)] * 4,
    )(ext_x, ext_bc, taps_x, taps_bc, links)


def local(pre_x, pre_bc, conv_x, conv_bc, log_decay, lengths, grad_out):
    tok_rows = pre_x.shape[0]
    head_count = log_decay.shape[0]
    rim_width = K - 1
    block_count = tok_rows // BLOCK
    seq_start = lax.axis_index("seq") * tok_rows
    positions = seq_start + jnp.arange(-rim_width, tok_rows + rim_width)
    note_all = note_index(positions, lengths)
    note_ids = note_all[rim_width : rim_width + tok_rows]
    before_both = shifted(
        jnp.concatenate([pre_x[tok_rows - rim_width :], pre_bc[tok_rows - rim_width :]], axis=1), "seq", 1
    )
    before_x, before_bc = before_both[:, : pre_x.shape[1]], before_both[:, pre_x.shape[1] :]
    links = jnp.stack(
        [note_all[k : k + tok_rows] == note_ids for k in range(K)], axis=1
    ).astype(jnp.float32)
    u_x, v_x, u_bc, v_bc = conv_silu(
        jnp.concatenate([before_x, pre_x]).astype(jnp.float32),
        jnp.concatenate([before_bc, pre_bc]).astype(jnp.float32),
        conv_x,
        conv_bc,
        links,
    )
    x_heads = v_x.reshape(block_count, BLOCK, head_count, P_SIZE).transpose(2, 0, 1, 3)
    b_blocks = v_bc[:, :N].reshape(block_count, BLOCK, N)
    c_blocks = v_bc[:, N:].reshape(block_count, BLOCK, N)
    log_blocks = log_decay.reshape(head_count, block_count, BLOCK)
    grad_heads = (
        grad_out.astype(jnp.float32)
        .reshape(block_count, BLOCK, head_count, P_SIZE)
        .transpose(2, 0, 1, 3)
    )
    note_blocks = note_ids.reshape(block_count, BLOCK)
    befores = jnp.concatenate([note_all[rim_width - 1 : rim_width], note_blocks[:-1, -1]])

    note_before = note_all[rim_width - 1]
    log_rows = log_decay.astype(jnp.float32)
    x_rows = v_x.reshape(tok_rows, head_count, P_SIZE)
    g_rows = grad_out.astype(jnp.float32).reshape(tok_rows, head_count, P_SIZE)
    shard_cumul = running_sum(log_rows)
    keep = jnp.exp(shard_cumul[:, -1]) * (note_ids[-1] == note_before)
    leave_rows = jnp.exp(shard_cumul[:, -1:] - shard_cumul) * (note_ids == note_ids[-1])
    entry_rows = jnp.exp(shard_cumul) * (note_ids == note_before)
    local_state = jnp.einsum(
        "thp,ht,tn->hpn", x_rows, leave_rows, v_bc[:, :N], precision=precise,
        preferred_element_type=jnp.float32,
    )
    local_adjoint = jnp.einsum(
        "thp,ht,tn->hpn", g_rows, entry_rows, v_bc[:, N:], precision=precise,
        preferred_element_type=jnp.float32,
    )
    state_in, adjoint_in = chain_both(local_state, local_adjoint, keep, "seq")

    def local_forward(x_all, b_all, c_all, log_all):
        return block_forward_all(
            state_in, x_all, b_all, c_all, log_all, note_blocks, befores
        )

    _, pull = jax.vjp(local_forward, x_heads, b_blocks, c_blocks, log_blocks)
    grad_x_heads, grad_b, grad_c, grad_log = pull((grad_heads, adjoint_in))
    grad_log_decay = grad_log.reshape(head_count, tok_rows)
    grad_v_x = grad_x_heads.transpose(1, 2, 0, 3).reshape(tok_rows, head_count * P_SIZE)
    grad_v_bc = jnp.concatenate([grad_b.reshape(tok_rows, N), grad_c.reshape(tok_rows, N)], axis=1)
    grad_u_x = grad_v_x * silu_slope(u_x)
    grad_u_bc = grad_v_bc * silu_slope(u_bc)
    after_both = shifted(jnp.concatenate([grad_u_x[:rim_width], grad_u_bc[:rim_width]], axis=1), "seq", -1)
    after_x, after_bc = after_both[:, : grad_u_x.shape[1]], after_both[:, grad_u_x.shape[1] :]
    grad_pre_x = conv_backward(jnp.concatenate([grad_u_x, after_x]), conv_x, note_all[rim_width:])
    whole_bc = conv_backward(jnp.concatenate([grad_u_bc, after_bc]), conv_bc, note_all[rim_width:])
    chips, cores = lax.axis_size("chip"), lax.axis_size("core")
    pieces = whole_bc.reshape(chips, cores, tok_rows // (chips * cores), whole_bc.shape[1])
    core = lax.axis_index("core")
    mine = lax.dynamic_index_in_dim(pieces, core, 1, keepdims=False)
    other = lax.dynamic_index_in_dim(pieces, 1 - core, 1, keepdims=False)
    pair_sum = mine + lax.ppermute(other, "core", [(0, 1), (1, 0)])
    grad_pre_bc = lax.all_to_all(pair_sum, "chip", 0, 0, tiled=False).sum(0)
    return (grad_pre_x, grad_pre_bc, grad_log_decay)


def solution(mesh):
    seq_size, head_size = mesh.shape["seq"], mesh.shape["head"]
    split = jax.sharding.Mesh(
        mesh.devices.reshape(seq_size, head_size // 2, 2), ("seq", "chip", "core")
    )
    head = ("chip", "core")
    placed = (
        P("seq", head),
        P("seq", None),
        P(None, head),
        P(),
        P(head, "seq"),
        P(),
        P("seq", head),
    )
    return jax.shard_map(
        local,
        mesh=split,
        in_specs=placed,
        out_specs=(P("seq", head), P(("seq",) + head, None), P(head, "seq")),
        check_vma=False,
    )
```

```python
import jax
import jax.numpy as jnp
from jax import lax
from jax.sharding import PartitionSpec as P

P_SIZE = 64
N = 128
K = 4
BLOCK = 256


precise = lax.Precision.HIGHEST


def shifted(value, axis, steps):
    count = lax.axis_size(axis)
    initial, last = (max(0, -steps), min(count, count - steps))
    return lax.ppermute(value, axis, [(source, source + steps) for source in range(initial, last)])


def entering(value, axis, join, neutral, backward):
    count, mine = (lax.axis_size(axis), lax.axis_index(axis))
    pieces = jax.tree.map(lambda part: lax.all_gather(part, axis), value)
    if backward:
        pieces = jax.tree.map(lambda part: part[::-1], pieces)
        mine = count - 1 - mine
    total = jax.tree.map(
        lambda part, zero: jnp.full_like(part, 0) + jnp.asarray(zero, part.dtype), value, neutral
    )

    def hop(position, total):
        longer = join(total, jax.tree.map(lambda part: part[position], pieces))
        return jax.tree.map(lambda new, old: jnp.where(position < mine, new, old), longer, total)

    return lax.fori_loop(0, count - 1, hop, total)


def matmul(left, right):
    return jnp.dot(left, right, precision=precise, preferred_element_type=jnp.float32)


def note_index(positions, lengths):
    starts = jnp.cumsum(lengths) - lengths
    hits = (positions[:, None] >= starts[None, :]).astype(jnp.int32)
    return jnp.sum(hits, axis=1) - 1


def block_edges(log_block, note_block, note_before):
    cumul = jnp.cumsum(log_block)
    entry = jnp.exp(cumul) * (note_block == note_before)
    leave = jnp.exp(cumul[-1] - cumul) * (note_block == note_block[-1])
    through = jnp.exp(cumul[-1]) * (note_block[-1] == note_before)
    return (cumul, entry, leave, through)


def block_forward(state, x_block, b_block, c_block, log_block, note_block, note_before):
    cumul, entry, leave, through = block_edges(log_block, note_block, note_before)
    length = note_block.shape[0]
    lower = jnp.arange(length)[:, None] >= jnp.arange(length)[None, :]
    linked = lower & (note_block[:, None] == note_block[None, :])
    decay_matrix = jnp.exp(jnp.where(linked, cumul[:, None] - cumul[None, :], 0.0)) * linked
    scores = matmul(c_block, b_block.T) * decay_matrix
    output = matmul(scores, x_block) + entry[:, None] * matmul(c_block, state.T)
    updated = through * state + matmul((x_block * leave[:, None]).T, b_block)
    return (output, updated)


def head_forward(state, x_head, b_blocks, c_blocks, log_head, note_blocks, befores):

    def head_advance(carry, block):
        output, updated = block_forward(carry, *block)
        return (updated, output)

    final, outputs = lax.scan(
        head_advance, state, (x_head, b_blocks, c_blocks, log_head, note_blocks, befores)
    )
    return (outputs, final)


def conv_forward(extended, weights, note_ext):
    width = weights.shape[0]
    count = extended.shape[0] - width + 1
    result = jnp.zeros((count, extended.shape[1]), jnp.float32)
    for k in range(width):
        linked = note_ext[k : k + count] == note_ext[width - 1 : width - 1 + count]
        result = result + weights[k][None, :] * extended[k : k + count] * linked[:, None]
    return result


def conv_backward(extended, weights, note_ext):
    width = weights.shape[0]
    count = extended.shape[0] - width + 1
    result = jnp.zeros((count, extended.shape[1]), jnp.float32)
    for k in range(width):
        lag = width - 1 - k
        linked = note_ext[lag : lag + count] == note_ext[:count]
        result = result + weights[k][None, :] * extended[lag : lag + count] * linked[:, None]
    return result


def silu_slope(values):
    sigma = jax.nn.sigmoid(values)
    return sigma * (1.0 + values * (1.0 - sigma))


def chain_combine(earlier, later):
    return (earlier[0] * later[0], later[0][:, None, None] * earlier[1] + later[1])


def chain_in(value, keep, axis, direction):
    count = lax.axis_size(axis)
    packed = jnp.concatenate(
        [value.reshape(value.shape[0], -1), jnp.broadcast_to(keep[:, None], (keep.shape[0], 128))], axis=1
    )
    total = jnp.zeros_like(value)
    scale = jnp.ones_like(keep)
    for distance in range(1, count):
        arrived = shifted(packed, axis, direction * distance)
        part = arrived[:, : value[0].size].reshape(value.shape)
        total = total + scale[:, None, None] * part
        scale = scale * arrived[:, value[0].size]
    return total


def running_sum(values):
    length = values.shape[-1]
    upper = (jnp.arange(length)[:, None] <= jnp.arange(length)[None, :]).astype(values.dtype)
    return jnp.dot(values, upper, precision=precise, preferred_element_type=jnp.float32)


def chain_both(state, adjoint, keep, axis):
    count, mine = lax.axis_size(axis), lax.axis_index(axis)
    heads, size = state.shape[0], state[0].size
    tail = jnp.broadcast_to(keep[:, None], (heads, 128))
    later = jnp.concatenate([state.reshape(heads, size), tail], axis=1)
    earlier = jnp.concatenate([adjoint.reshape(heads, size), tail], axis=1)
    targets = jnp.arange(count)[:, None, None]
    outgoing = jnp.where(targets > mine, later[None], jnp.where(targets < mine, earlier[None], 0.0))
    arrived = lax.all_to_all(outgoing, axis, 0, 0, tiled=False)
    keeps = arrived[:, :, size]
    totals = []
    for order in (range(count - 1, -1, -1), range(count)):
        weights = [None] * count
        scale = jnp.ones_like(keep)
        for source in order:
            near = (source < mine) if order.step < 0 else (source > mine)
            weights[source] = jnp.where(near, scale, 0.0)
            scale = jnp.where(near, scale * keeps[source], scale)
        combined = jnp.sum(jnp.stack(weights)[:, :, None] * arrived, axis=0)
        totals.append(combined[:, :size].reshape(state.shape))
    return totals[0], totals[1]


def einsum(spec, *operands):
    return jnp.einsum(spec, *operands, precision=lax.Precision.HIGH, preferred_element_type=jnp.float32)


def block_forward_all(state, x_all, b_all, c_all, log_all, note_blocks, befores):
    cumul = running_sum(log_all)
    entry = jnp.exp(cumul) * (note_blocks == befores[:, None])
    leave = jnp.exp(cumul[..., -1:] - cumul) * (note_blocks == note_blocks[:, -1:])
    through = jnp.exp(cumul[..., -1]) * (note_blocks[:, -1] == befores)
    length = note_blocks.shape[1]
    lower = jnp.arange(length)[:, None] >= jnp.arange(length)[None, :]
    linked = lower & (note_blocks[:, :, None] == note_blocks[:, None, :])
    differences = cumul[..., :, None] - cumul[..., None, :]
    decay_matrix = jnp.exp(jnp.where(linked, differences, 0.0)) * linked
    scores = einsum("bin,bjn->bij", c_all, b_all) * decay_matrix
    output = einsum("hbij,hbjp->hbip", scores, x_all)
    chunk = einsum("hbjp,bjn->hbpn", x_all * leave[..., None], b_all)
    starts = []
    for block in range(note_blocks.shape[0]):
        starts.append(state)
        state = through[:, block, None, None] * state + chunk[:, block]
    output = output + entry[..., None] * einsum("bin,hbpn->hbip", c_all, jnp.stack(starts, axis=1))
    return (output, state)


def local(pre_x, pre_bc, conv_x, conv_bc, log_decay, lengths, grad_out):
    tok_rows = pre_x.shape[0]
    head_count = log_decay.shape[0]
    rim_width = K - 1
    block_count = tok_rows // BLOCK
    seq_start = lax.axis_index("seq") * tok_rows
    positions = seq_start + jnp.arange(-rim_width, tok_rows + rim_width)
    note_all = note_index(positions, lengths)
    note_ids = note_all[rim_width : rim_width + tok_rows]
    before_both = shifted(
        jnp.concatenate([pre_x[tok_rows - rim_width :], pre_bc[tok_rows - rim_width :]], axis=1), "seq", 1
    )
    before_x, before_bc = before_both[:, : pre_x.shape[1]], before_both[:, pre_x.shape[1] :]
    u_x = conv_forward(
        jnp.concatenate([before_x, pre_x]).astype(jnp.float32),
        conv_x,
        note_all[: tok_rows + rim_width],
    )
    u_bc = conv_forward(
        jnp.concatenate([before_bc, pre_bc]).astype(jnp.float32),
        conv_bc,
        note_all[: tok_rows + rim_width],
    )
    v_x = jax.nn.silu(u_x)
    v_bc = jax.nn.silu(u_bc)
    x_heads = v_x.reshape(block_count, BLOCK, head_count, P_SIZE).transpose(2, 0, 1, 3)
    b_blocks = v_bc[:, :N].reshape(block_count, BLOCK, N)
    c_blocks = v_bc[:, N:].reshape(block_count, BLOCK, N)
    log_blocks = log_decay.reshape(head_count, block_count, BLOCK)
    grad_heads = (
        grad_out.astype(jnp.float32)
        .reshape(block_count, BLOCK, head_count, P_SIZE)
        .transpose(2, 0, 1, 3)
    )
    note_blocks = note_ids.reshape(block_count, BLOCK)
    befores = jnp.concatenate([note_all[rim_width - 1 : rim_width], note_blocks[:-1, -1]])

    note_before = note_all[rim_width - 1]
    log_rows = log_decay.astype(jnp.float32)
    x_rows = v_x.reshape(tok_rows, head_count, P_SIZE)
    g_rows = grad_out.astype(jnp.float32).reshape(tok_rows, head_count, P_SIZE)
    shard_cumul = running_sum(log_rows)
    keep = jnp.exp(shard_cumul[:, -1]) * (note_ids[-1] == note_before)
    leave_rows = jnp.exp(shard_cumul[:, -1:] - shard_cumul) * (note_ids == note_ids[-1])
    entry_rows = jnp.exp(shard_cumul) * (note_ids == note_before)
    local_state = jnp.einsum(
        "thp,ht,tn->hpn", x_rows, leave_rows, v_bc[:, :N], precision=precise,
        preferred_element_type=jnp.float32,
    )
    local_adjoint = jnp.einsum(
        "thp,ht,tn->hpn", g_rows, entry_rows, v_bc[:, N:], precision=precise,
        preferred_element_type=jnp.float32,
    )
    state_in, adjoint_in = chain_both(local_state, local_adjoint, keep, "seq")

    def local_forward(x_all, b_all, c_all, log_all):
        return block_forward_all(
            state_in, x_all, b_all, c_all, log_all, note_blocks, befores
        )

    _, pull = jax.vjp(local_forward, x_heads, b_blocks, c_blocks, log_blocks)
    grad_x_heads, grad_b, grad_c, grad_log = pull((grad_heads, adjoint_in))
    grad_log_decay = grad_log.reshape(head_count, tok_rows)
    grad_v_x = grad_x_heads.transpose(1, 2, 0, 3).reshape(tok_rows, head_count * P_SIZE)
    grad_v_bc = jnp.concatenate([grad_b.reshape(tok_rows, N), grad_c.reshape(tok_rows, N)], axis=1)
    grad_u_x = grad_v_x * silu_slope(u_x)
    grad_u_bc = grad_v_bc * silu_slope(u_bc)
    after_both = shifted(jnp.concatenate([grad_u_x[:rim_width], grad_u_bc[:rim_width]], axis=1), "seq", -1)
    after_x, after_bc = after_both[:, : grad_u_x.shape[1]], after_both[:, grad_u_x.shape[1] :]
    grad_pre_x = conv_backward(jnp.concatenate([grad_u_x, after_x]), conv_x, note_all[rim_width:])
    whole_bc = conv_backward(jnp.concatenate([grad_u_bc, after_bc]), conv_bc, note_all[rim_width:])
    chips, cores = lax.axis_size("chip"), lax.axis_size("core")
    pieces = whole_bc.reshape(chips, cores, tok_rows // (chips * cores), whole_bc.shape[1])
    core = lax.axis_index("core")
    mine = lax.dynamic_index_in_dim(pieces, core, 1, keepdims=False)
    other = lax.dynamic_index_in_dim(pieces, 1 - core, 1, keepdims=False)
    pair_sum = mine + lax.ppermute(other, "core", [(0, 1), (1, 0)])
    grad_pre_bc = lax.all_to_all(pair_sum, "chip", 0, 0, tiled=False).sum(0)
    return (grad_pre_x, grad_pre_bc, grad_log_decay)


def solution(mesh):
    seq_size, head_size = mesh.shape["seq"], mesh.shape["head"]
    split = jax.sharding.Mesh(
        mesh.devices.reshape(seq_size, head_size // 2, 2), ("seq", "chip", "core")
    )
    head = ("chip", "core")
    placed = (
        P("seq", head),
        P("seq", None),
        P(None, head),
        P(),
        P(head, "seq"),
        P(),
        P("seq", head),
    )
    return jax.shard_map(
        local,
        mesh=split,
        in_specs=placed,
        out_specs=(P("seq", head), P(("seq",) + head, None), P(head, "seq")),
        check_vma=False,
    )
```

```python
import jax
import jax.numpy as jnp
from jax import lax
from jax.sharding import PartitionSpec as P

P_SIZE = 64
N = 128
K = 4
BLOCK = 256


precise = lax.Precision.HIGHEST


def shifted(value, axis, steps):
    count = lax.axis_size(axis)
    initial, last = (max(0, -steps), min(count, count - steps))
    return lax.ppermute(value, axis, [(source, source + steps) for source in range(initial, last)])


def entering(value, axis, join, neutral, backward):
    count, mine = (lax.axis_size(axis), lax.axis_index(axis))
    pieces = jax.tree.map(lambda part: lax.all_gather(part, axis), value)
    if backward:
        pieces = jax.tree.map(lambda part: part[::-1], pieces)
        mine = count - 1 - mine
    total = jax.tree.map(
        lambda part, zero: jnp.full_like(part, 0) + jnp.asarray(zero, part.dtype), value, neutral
    )

    def hop(position, total):
        longer = join(total, jax.tree.map(lambda part: part[position], pieces))
        return jax.tree.map(lambda new, old: jnp.where(position < mine, new, old), longer, total)

    return lax.fori_loop(0, count - 1, hop, total)


def matmul(left, right):
    return jnp.dot(left, right, precision=precise, preferred_element_type=jnp.float32)


def note_index(positions, lengths):
    starts = jnp.cumsum(lengths) - lengths
    hits = (positions[:, None] >= starts[None, :]).astype(jnp.int32)
    return jnp.sum(hits, axis=1) - 1


def block_edges(log_block, note_block, note_before):
    cumul = jnp.cumsum(log_block)
    entry = jnp.exp(cumul) * (note_block == note_before)
    leave = jnp.exp(cumul[-1] - cumul) * (note_block == note_block[-1])
    through = jnp.exp(cumul[-1]) * (note_block[-1] == note_before)
    return (cumul, entry, leave, through)


def block_forward(state, x_block, b_block, c_block, log_block, note_block, note_before):
    cumul, entry, leave, through = block_edges(log_block, note_block, note_before)
    length = note_block.shape[0]
    lower = jnp.arange(length)[:, None] >= jnp.arange(length)[None, :]
    linked = lower & (note_block[:, None] == note_block[None, :])
    decay_matrix = jnp.exp(jnp.where(linked, cumul[:, None] - cumul[None, :], 0.0)) * linked
    scores = matmul(c_block, b_block.T) * decay_matrix
    output = matmul(scores, x_block) + entry[:, None] * matmul(c_block, state.T)
    updated = through * state + matmul((x_block * leave[:, None]).T, b_block)
    return (output, updated)


def head_forward(state, x_head, b_blocks, c_blocks, log_head, note_blocks, befores):

    def head_advance(carry, block):
        output, updated = block_forward(carry, *block)
        return (updated, output)

    final, outputs = lax.scan(
        head_advance, state, (x_head, b_blocks, c_blocks, log_head, note_blocks, befores)
    )
    return (outputs, final)


def conv_forward(extended, weights, note_ext):
    width = weights.shape[0]
    count = extended.shape[0] - width + 1
    result = jnp.zeros((count, extended.shape[1]), jnp.float32)
    for k in range(width):
        linked = note_ext[k : k + count] == note_ext[width - 1 : width - 1 + count]
        result = result + weights[k][None, :] * extended[k : k + count] * linked[:, None]
    return result


def conv_backward(extended, weights, note_ext):
    width = weights.shape[0]
    count = extended.shape[0] - width + 1
    result = jnp.zeros((count, extended.shape[1]), jnp.float32)
    for k in range(width):
        lag = width - 1 - k
        linked = note_ext[lag : lag + count] == note_ext[:count]
        result = result + weights[k][None, :] * extended[lag : lag + count] * linked[:, None]
    return result


def silu_slope(values):
    sigma = jax.nn.sigmoid(values)
    return sigma * (1.0 + values * (1.0 - sigma))


def chain_combine(earlier, later):
    return (earlier[0] * later[0], later[0][:, None, None] * earlier[1] + later[1])


def chain_in(value, keep, axis, direction):
    count = lax.axis_size(axis)
    packed = jnp.concatenate(
        [value.reshape(value.shape[0], -1), jnp.broadcast_to(keep[:, None], (keep.shape[0], 128))], axis=1
    )
    total = jnp.zeros_like(value)
    scale = jnp.ones_like(keep)
    for distance in range(1, count):
        arrived = shifted(packed, axis, direction * distance)
        part = arrived[:, : value[0].size].reshape(value.shape)
        total = total + scale[:, None, None] * part
        scale = scale * arrived[:, value[0].size]
    return total


def running_sum(values):
    length = values.shape[-1]
    upper = (jnp.arange(length)[:, None] <= jnp.arange(length)[None, :]).astype(values.dtype)
    return jnp.dot(values, upper, precision=precise, preferred_element_type=jnp.float32)


def chain_both(state, adjoint, keep, axis):
    count, mine = lax.axis_size(axis), lax.axis_index(axis)
    heads, size = state.shape[0], state[0].size
    tail = jnp.broadcast_to(keep[:, None], (heads, 128))
    later = jnp.concatenate([state.reshape(heads, size), tail], axis=1)
    earlier = jnp.concatenate([adjoint.reshape(heads, size), tail], axis=1)
    targets = jnp.arange(count)[:, None, None]
    outgoing = jnp.where(targets > mine, later[None], jnp.where(targets < mine, earlier[None], 0.0))
    arrived = lax.all_to_all(outgoing, axis, 0, 0, tiled=False)
    keeps = arrived[:, :, size]
    totals = []
    for order in (range(count - 1, -1, -1), range(count)):
        weights = [None] * count
        scale = jnp.ones_like(keep)
        for source in order:
            near = (source < mine) if order.step < 0 else (source > mine)
            weights[source] = jnp.where(near, scale, 0.0)
            scale = jnp.where(near, scale * keeps[source], scale)
        combined = jnp.sum(jnp.stack(weights)[:, :, None] * arrived, axis=0)
        totals.append(combined[:, :size].reshape(state.shape))
    return totals[0], totals[1]


def einsum(spec, *operands):
    return jnp.einsum(spec, *operands, precision=lax.Precision.HIGH, preferred_element_type=jnp.float32)


def block_forward_all(state, x_all, b_all, c_all, log_all, note_blocks, befores):
    cumul = running_sum(log_all)
    entry = jnp.exp(cumul) * (note_blocks == befores[:, None])
    leave = jnp.exp(cumul[..., -1:] - cumul) * (note_blocks == note_blocks[:, -1:])
    through = jnp.exp(cumul[..., -1]) * (note_blocks[:, -1] == befores)
    length = note_blocks.shape[1]
    lower = jnp.arange(length)[:, None] >= jnp.arange(length)[None, :]
    linked = lower & (note_blocks[:, :, None] == note_blocks[:, None, :])
    differences = cumul[..., :, None] - cumul[..., None, :]
    decay_matrix = jnp.exp(jnp.where(linked, differences, 0.0)) * linked
    scores = einsum("bin,bjn->bij", c_all, b_all) * decay_matrix
    output = einsum("hbij,hbjp->hbip", scores, x_all)
    chunk = einsum("hbjp,bjn->hbpn", x_all * leave[..., None], b_all)
    starts = []
    for block in range(note_blocks.shape[0]):
        starts.append(state)
        state = through[:, block, None, None] * state + chunk[:, block]
    output = output + entry[..., None] * einsum("bin,hbpn->hbip", c_all, jnp.stack(starts, axis=1))
    return (output, state)


def local(pre_x, pre_bc, conv_x, conv_bc, log_decay, lengths, grad_out):
    tok_rows = pre_x.shape[0]
    head_count = log_decay.shape[0]
    rim_width = K - 1
    block_count = tok_rows // BLOCK
    seq_start = lax.axis_index("seq") * tok_rows
    positions = seq_start + jnp.arange(-rim_width, tok_rows + rim_width)
    note_all = note_index(positions, lengths)
    note_ids = note_all[rim_width : rim_width + tok_rows]
    before_both = shifted(
        jnp.concatenate([pre_x[tok_rows - rim_width :], pre_bc[tok_rows - rim_width :]], axis=1), "seq", 1
    )
    before_x, before_bc = before_both[:, : pre_x.shape[1]], before_both[:, pre_x.shape[1] :]
    u_x = conv_forward(
        jnp.concatenate([before_x, pre_x]).astype(jnp.float32),
        conv_x,
        note_all[: tok_rows + rim_width],
    )
    u_bc = conv_forward(
        jnp.concatenate([before_bc, pre_bc]).astype(jnp.float32),
        conv_bc,
        note_all[: tok_rows + rim_width],
    )
    v_x = jax.nn.silu(u_x)
    v_bc = jax.nn.silu(u_bc)
    x_heads = v_x.reshape(block_count, BLOCK, head_count, P_SIZE).transpose(2, 0, 1, 3)
    b_blocks = v_bc[:, :N].reshape(block_count, BLOCK, N)
    c_blocks = v_bc[:, N:].reshape(block_count, BLOCK, N)
    log_blocks = log_decay.reshape(head_count, block_count, BLOCK)
    grad_heads = (
        grad_out.astype(jnp.float32)
        .reshape(block_count, BLOCK, head_count, P_SIZE)
        .transpose(2, 0, 1, 3)
    )
    note_blocks = note_ids.reshape(block_count, BLOCK)
    befores = jnp.concatenate([note_all[rim_width - 1 : rim_width], note_blocks[:-1, -1]])

    note_before = note_all[rim_width - 1]
    log_rows = log_decay.astype(jnp.float32)
    x_rows = v_x.reshape(tok_rows, head_count, P_SIZE)
    g_rows = grad_out.astype(jnp.float32).reshape(tok_rows, head_count, P_SIZE)
    block_cumul = running_sum(log_blocks)
    offsets = [jnp.zeros_like(block_cumul[:, 0, -1])]
    for block in range(block_count - 1):
        offsets.append(offsets[-1] + block_cumul[:, block, -1])
    shard_cumul = (block_cumul + jnp.stack(offsets, axis=1)[:, :, None]).reshape(head_count, tok_rows)
    keep = jnp.exp(shard_cumul[:, -1]) * (note_ids[-1] == note_before)
    leave_rows = jnp.exp(shard_cumul[:, -1:] - shard_cumul) * (note_ids == note_ids[-1])
    entry_rows = jnp.exp(shard_cumul) * (note_ids == note_before)
    local_state = jnp.einsum(
        "thp,ht,tn->hpn", x_rows, leave_rows, v_bc[:, :N], precision=lax.Precision.HIGH,
        preferred_element_type=jnp.float32,
    )
    local_adjoint = jnp.einsum(
        "thp,ht,tn->hpn", g_rows, entry_rows, v_bc[:, N:], precision=lax.Precision.HIGH,
        preferred_element_type=jnp.float32,
    )
    state_in, adjoint_in = chain_both(local_state, local_adjoint, keep, "seq")

    def local_forward(x_all, b_all, c_all, log_all):
        return block_forward_all(
            state_in, x_all, b_all, c_all, log_all, note_blocks, befores
        )

    _, pull = jax.vjp(local_forward, x_heads, b_blocks, c_blocks, log_blocks)
    grad_x_heads, grad_b, grad_c, grad_log = pull((grad_heads, adjoint_in))
    grad_log_decay = grad_log.reshape(head_count, tok_rows)
    grad_v_x = grad_x_heads.transpose(1, 2, 0, 3).reshape(tok_rows, head_count * P_SIZE)
    grad_v_bc = jnp.concatenate([grad_b.reshape(tok_rows, N), grad_c.reshape(tok_rows, N)], axis=1)
    grad_u_x = grad_v_x * silu_slope(u_x)
    grad_u_bc = grad_v_bc * silu_slope(u_bc)
    after_both = shifted(jnp.concatenate([grad_u_x[:rim_width], grad_u_bc[:rim_width]], axis=1), "seq", -1)
    after_x, after_bc = after_both[:, : grad_u_x.shape[1]], after_both[:, grad_u_x.shape[1] :]
    grad_pre_x = conv_backward(jnp.concatenate([grad_u_x, after_x]), conv_x, note_all[rim_width:])
    whole_bc = conv_backward(jnp.concatenate([grad_u_bc, after_bc]), conv_bc, note_all[rim_width:])
    chips, cores = lax.axis_size("chip"), lax.axis_size("core")
    pieces = whole_bc.reshape(chips, cores, tok_rows // (chips * cores), whole_bc.shape[1])
    core = lax.axis_index("core")
    mine = lax.dynamic_index_in_dim(pieces, core, 1, keepdims=False)
    other = lax.dynamic_index_in_dim(pieces, 1 - core, 1, keepdims=False)
    pair_sum = mine + lax.ppermute(other, "core", [(0, 1), (1, 0)])
    grad_pre_bc = lax.all_to_all(pair_sum, "chip", 0, 0, tiled=False).sum(0)
    return (grad_pre_x, grad_pre_bc, grad_log_decay)


def solution(mesh):
    seq_size, head_size = mesh.shape["seq"], mesh.shape["head"]
    split = jax.sharding.Mesh(
        mesh.devices.reshape(seq_size, head_size // 2, 2), ("seq", "chip", "core")
    )
    head = ("chip", "core")
    placed = (
        P("seq", head),
        P("seq", None),
        P(None, head),
        P(),
        P(head, "seq"),
        P(),
        P("seq", head),
    )
    return jax.shard_map(
        local,
        mesh=split,
        in_specs=placed,
        out_specs=(P("seq", head), P(("seq",) + head, None), P(head, "seq")),
        check_vma=False,
    )
```

```python
import jax
import jax.numpy as jnp
from jax import lax
from jax.sharding import PartitionSpec as P

P_SIZE = 64
N = 128
K = 4
BLOCK = 256


precise = lax.Precision.HIGHEST


def shifted(value, axis, steps):
    count = lax.axis_size(axis)
    initial, last = (max(0, -steps), min(count, count - steps))
    return lax.ppermute(value, axis, [(source, source + steps) for source in range(initial, last)])


def entering(value, axis, join, neutral, backward):
    count, mine = (lax.axis_size(axis), lax.axis_index(axis))
    pieces = jax.tree.map(lambda part: lax.all_gather(part, axis), value)
    if backward:
        pieces = jax.tree.map(lambda part: part[::-1], pieces)
        mine = count - 1 - mine
    total = jax.tree.map(
        lambda part, zero: jnp.full_like(part, 0) + jnp.asarray(zero, part.dtype), value, neutral
    )

    def hop(position, total):
        longer = join(total, jax.tree.map(lambda part: part[position], pieces))
        return jax.tree.map(lambda new, old: jnp.where(position < mine, new, old), longer, total)

    return lax.fori_loop(0, count - 1, hop, total)


def matmul(left, right):
    return jnp.dot(left, right, precision=precise, preferred_element_type=jnp.float32)


def note_index(positions, lengths):
    starts = jnp.cumsum(lengths) - lengths
    hits = (positions[:, None] >= starts[None, :]).astype(jnp.int32)
    return jnp.sum(hits, axis=1) - 1


def block_edges(log_block, note_block, note_before):
    cumul = jnp.cumsum(log_block)
    entry = jnp.exp(cumul) * (note_block == note_before)
    leave = jnp.exp(cumul[-1] - cumul) * (note_block == note_block[-1])
    through = jnp.exp(cumul[-1]) * (note_block[-1] == note_before)
    return (cumul, entry, leave, through)


def block_forward(state, x_block, b_block, c_block, log_block, note_block, note_before):
    cumul, entry, leave, through = block_edges(log_block, note_block, note_before)
    length = note_block.shape[0]
    lower = jnp.arange(length)[:, None] >= jnp.arange(length)[None, :]
    linked = lower & (note_block[:, None] == note_block[None, :])
    decay_matrix = jnp.exp(jnp.where(linked, cumul[:, None] - cumul[None, :], 0.0)) * linked
    scores = matmul(c_block, b_block.T) * decay_matrix
    output = matmul(scores, x_block) + entry[:, None] * matmul(c_block, state.T)
    updated = through * state + matmul((x_block * leave[:, None]).T, b_block)
    return (output, updated)


def head_forward(state, x_head, b_blocks, c_blocks, log_head, note_blocks, befores):

    def head_advance(carry, block):
        output, updated = block_forward(carry, *block)
        return (updated, output)

    final, outputs = lax.scan(
        head_advance, state, (x_head, b_blocks, c_blocks, log_head, note_blocks, befores)
    )
    return (outputs, final)


def conv_forward(extended, weights, note_ext):
    width = weights.shape[0]
    count = extended.shape[0] - width + 1
    result = jnp.zeros((count, extended.shape[1]), jnp.float32)
    for k in range(width):
        linked = note_ext[k : k + count] == note_ext[width - 1 : width - 1 + count]
        result = result + weights[k][None, :] * extended[k : k + count] * linked[:, None]
    return result


def conv_backward(extended, weights, note_ext):
    width = weights.shape[0]
    count = extended.shape[0] - width + 1
    result = jnp.zeros((count, extended.shape[1]), jnp.float32)
    for k in range(width):
        lag = width - 1 - k
        linked = note_ext[lag : lag + count] == note_ext[:count]
        result = result + weights[k][None, :] * extended[lag : lag + count] * linked[:, None]
    return result


def silu_slope(values):
    sigma = jax.nn.sigmoid(values)
    return sigma * (1.0 + values * (1.0 - sigma))


def chain_combine(earlier, later):
    return (earlier[0] * later[0], later[0][:, None, None] * earlier[1] + later[1])


def chain_in(value, keep, axis, direction):
    count = lax.axis_size(axis)
    packed = jnp.concatenate(
        [value.reshape(value.shape[0], -1), jnp.broadcast_to(keep[:, None], (keep.shape[0], 128))], axis=1
    )
    total = jnp.zeros_like(value)
    scale = jnp.ones_like(keep)
    for distance in range(1, count):
        arrived = shifted(packed, axis, direction * distance)
        part = arrived[:, : value[0].size].reshape(value.shape)
        total = total + scale[:, None, None] * part
        scale = scale * arrived[:, value[0].size]
    return total


def running_sum(values):
    length = values.shape[-1]
    upper = (jnp.arange(length)[:, None] <= jnp.arange(length)[None, :]).astype(values.dtype)
    return jnp.dot(values, upper, precision=precise, preferred_element_type=jnp.float32)


def chain_both(state, adjoint, keep, axis):
    count, mine = lax.axis_size(axis), lax.axis_index(axis)
    heads, size = state.shape[0], state[0].size
    tail = jnp.broadcast_to(keep[:, None], (heads, 128))
    later = jnp.concatenate([state.reshape(heads, size), tail], axis=1)
    earlier = jnp.concatenate([adjoint.reshape(heads, size), tail], axis=1)
    targets = jnp.arange(count)[:, None, None]
    outgoing = jnp.where(targets > mine, later[None], jnp.where(targets < mine, earlier[None], 0.0))
    arrived = lax.all_to_all(outgoing, axis, 0, 0, tiled=False)
    keeps = arrived[:, :, size]
    totals = []
    for order in (range(count - 1, -1, -1), range(count)):
        weights = [None] * count
        scale = jnp.ones_like(keep)
        for source in order:
            near = (source < mine) if order.step < 0 else (source > mine)
            weights[source] = jnp.where(near, scale, 0.0)
            scale = jnp.where(near, scale * keeps[source], scale)
        combined = jnp.sum(jnp.stack(weights)[:, :, None] * arrived, axis=0)
        totals.append(combined[:, :size].reshape(state.shape))
    return totals[0], totals[1]


def einsum(spec, *operands):
    return jnp.einsum(spec, *operands, precision=lax.Precision.HIGH, preferred_element_type=jnp.float32)


def block_forward_all(state, x_all, b_all, c_all, log_all, note_blocks, befores):
    cumul = running_sum(log_all)
    entry = jnp.exp(cumul) * (note_blocks == befores[:, None])
    leave = jnp.exp(cumul[..., -1:] - cumul) * (note_blocks == note_blocks[:, -1:])
    through = jnp.exp(cumul[..., -1]) * (note_blocks[:, -1] == befores)
    length = note_blocks.shape[1]
    lower = jnp.arange(length)[:, None] >= jnp.arange(length)[None, :]
    linked = lower & (note_blocks[:, :, None] == note_blocks[:, None, :])
    differences = cumul[..., :, None] - cumul[..., None, :]
    decay_matrix = jnp.exp(jnp.where(linked, differences, 0.0)) * linked
    scores = einsum("bin,bjn->bij", c_all, b_all) * decay_matrix
    output = einsum("hbij,hbjp->hbip", scores, x_all)
    chunk = einsum("hbjp,bjn->hbpn", x_all * leave[..., None], b_all)
    starts = []
    for block in range(note_blocks.shape[0]):
        starts.append(state)
        state = through[:, block, None, None] * state + chunk[:, block]
    output = output + entry[..., None] * einsum("bin,hbpn->hbip", c_all, jnp.stack(starts, axis=1))
    return (output, state)


def local(pre_x, pre_bc, conv_x, conv_bc, log_decay, lengths, grad_out):
    tok_rows = pre_x.shape[0]
    head_count = log_decay.shape[0]
    rim_width = K - 1
    block_count = tok_rows // BLOCK
    seq_start = lax.axis_index("seq") * tok_rows
    positions = seq_start + jnp.arange(-rim_width, tok_rows + rim_width)
    note_all = note_index(positions, lengths)
    note_ids = note_all[rim_width : rim_width + tok_rows]
    before_both = shifted(
        jnp.concatenate([pre_x[tok_rows - rim_width :], pre_bc[tok_rows - rim_width :]], axis=1), "seq", 1
    )
    before_x, before_bc = before_both[:, : pre_x.shape[1]], before_both[:, pre_x.shape[1] :]
    u_x = conv_forward(
        jnp.concatenate([before_x, pre_x]).astype(jnp.float32),
        conv_x,
        note_all[: tok_rows + rim_width],
    )
    u_bc = conv_forward(
        jnp.concatenate([before_bc, pre_bc]).astype(jnp.float32),
        conv_bc,
        note_all[: tok_rows + rim_width],
    )
    v_x = jax.nn.silu(u_x)
    v_bc = jax.nn.silu(u_bc)
    x_heads = v_x.reshape(block_count, BLOCK, head_count, P_SIZE).transpose(2, 0, 1, 3)
    b_blocks = v_bc[:, :N].reshape(block_count, BLOCK, N)
    c_blocks = v_bc[:, N:].reshape(block_count, BLOCK, N)
    log_blocks = log_decay.reshape(head_count, block_count, BLOCK)
    grad_heads = (
        grad_out.astype(jnp.float32)
        .reshape(block_count, BLOCK, head_count, P_SIZE)
        .transpose(2, 0, 1, 3)
    )
    note_blocks = note_ids.reshape(block_count, BLOCK)
    befores = jnp.concatenate([note_all[rim_width - 1 : rim_width], note_blocks[:-1, -1]])

    note_before = note_all[rim_width - 1]
    log_rows = log_decay.astype(jnp.float32)
    x_rows = v_x.reshape(tok_rows, head_count, P_SIZE)
    g_rows = grad_out.astype(jnp.float32).reshape(tok_rows, head_count, P_SIZE)
    block_cumul = running_sum(log_blocks)
    offsets = [jnp.zeros_like(block_cumul[:, 0, -1])]
    for block in range(block_count - 1):
        offsets.append(offsets[-1] + block_cumul[:, block, -1])
    shard_cumul = (block_cumul + jnp.stack(offsets, axis=1)[:, :, None]).reshape(head_count, tok_rows)
    keep = jnp.exp(shard_cumul[:, -1]) * (note_ids[-1] == note_before)
    leave_rows = jnp.exp(shard_cumul[:, -1:] - shard_cumul) * (note_ids == note_ids[-1])
    entry_rows = jnp.exp(shard_cumul) * (note_ids == note_before)
    local_state = jnp.einsum(
        "thp,ht,tn->hpn", x_rows, leave_rows, v_bc[:, :N], precision=lax.Precision.HIGH,
        preferred_element_type=jnp.float32,
    )
    local_adjoint = jnp.einsum(
        "thp,ht,tn->hpn", g_rows, entry_rows, v_bc[:, N:], precision=lax.Precision.HIGH,
        preferred_element_type=jnp.float32,
    )
    state_in, adjoint_in = chain_both(local_state, local_adjoint, keep, "seq")

    def local_forward(x_all, b_all, c_all, log_all):
        return block_forward_all(
            state_in, x_all, b_all, c_all, log_all, note_blocks, befores
        )

    _, pull = jax.vjp(local_forward, x_heads, b_blocks, c_blocks, log_blocks)
    grad_x_heads, grad_b, grad_c, grad_log = pull((grad_heads, adjoint_in))
    grad_log_decay = grad_log.reshape(head_count, tok_rows)
    grad_v_x = grad_x_heads.transpose(1, 2, 0, 3).reshape(tok_rows, head_count * P_SIZE)
    grad_v_bc = jnp.concatenate([grad_b.reshape(tok_rows, N), grad_c.reshape(tok_rows, N)], axis=1)
    grad_u_x = grad_v_x * silu_slope(u_x)
    grad_u_bc = grad_v_bc * silu_slope(u_bc)
    after_bc = shifted(grad_u_bc[:rim_width], "seq", -1)
    after_x = shifted(grad_u_x[:rim_width], "seq", -1)
    grad_pre_x = conv_backward(jnp.concatenate([grad_u_x, after_x]), conv_x, note_all[rim_width:])
    whole_bc = conv_backward(jnp.concatenate([grad_u_bc, after_bc]), conv_bc, note_all[rim_width:])
    chips, cores = lax.axis_size("chip"), lax.axis_size("core")
    pieces = whole_bc.reshape(chips, cores, tok_rows // (chips * cores), whole_bc.shape[1])
    core = lax.axis_index("core")
    mine = lax.dynamic_index_in_dim(pieces, core, 1, keepdims=False)
    other = lax.dynamic_index_in_dim(pieces, 1 - core, 1, keepdims=False)
    pair_sum = mine + lax.ppermute(other, "core", [(0, 1), (1, 0)])
    grad_pre_bc = lax.all_to_all(pair_sum, "chip", 0, 0, tiled=False).sum(0)
    return (grad_pre_x, grad_pre_bc, grad_log_decay)


def solution(mesh):
    seq_size, head_size = mesh.shape["seq"], mesh.shape["head"]
    split = jax.sharding.Mesh(
        mesh.devices.reshape(seq_size, head_size // 2, 2), ("seq", "chip", "core")
    )
    head = ("chip", "core")
    placed = (
        P("seq", head),
        P("seq", None),
        P(None, head),
        P(),
        P(head, "seq"),
        P(),
        P("seq", head),
    )
    return jax.shard_map(
        local,
        mesh=split,
        in_specs=placed,
        out_specs=(P("seq", head), P(("seq",) + head, None), P(head, "seq")),
        check_vma=False,
    )
```

```python
import jax
import jax.numpy as jnp
from jax import lax
from jax.sharding import PartitionSpec as P

P_SIZE = 64
N = 128
K = 4
BLOCK = 256


precise = lax.Precision.HIGHEST


def shifted(value, axis, steps):
    count = lax.axis_size(axis)
    initial, last = (max(0, -steps), min(count, count - steps))
    return lax.ppermute(value, axis, [(source, source + steps) for source in range(initial, last)])


def entering(value, axis, join, neutral, backward):
    count, mine = (lax.axis_size(axis), lax.axis_index(axis))
    pieces = jax.tree.map(lambda part: lax.all_gather(part, axis), value)
    if backward:
        pieces = jax.tree.map(lambda part: part[::-1], pieces)
        mine = count - 1 - mine
    total = jax.tree.map(
        lambda part, zero: jnp.full_like(part, 0) + jnp.asarray(zero, part.dtype), value, neutral
    )

    def hop(position, total):
        longer = join(total, jax.tree.map(lambda part: part[position], pieces))
        return jax.tree.map(lambda new, old: jnp.where(position < mine, new, old), longer, total)

    return lax.fori_loop(0, count - 1, hop, total)


def matmul(left, right):
    return jnp.dot(left, right, precision=precise, preferred_element_type=jnp.float32)


def note_index(positions, lengths):
    starts = jnp.cumsum(lengths) - lengths
    hits = (positions[:, None] >= starts[None, :]).astype(jnp.int32)
    return jnp.sum(hits, axis=1) - 1


def block_edges(log_block, note_block, note_before):
    cumul = jnp.cumsum(log_block)
    entry = jnp.exp(cumul) * (note_block == note_before)
    leave = jnp.exp(cumul[-1] - cumul) * (note_block == note_block[-1])
    through = jnp.exp(cumul[-1]) * (note_block[-1] == note_before)
    return (cumul, entry, leave, through)


def block_forward(state, x_block, b_block, c_block, log_block, note_block, note_before):
    cumul, entry, leave, through = block_edges(log_block, note_block, note_before)
    length = note_block.shape[0]
    lower = jnp.arange(length)[:, None] >= jnp.arange(length)[None, :]
    linked = lower & (note_block[:, None] == note_block[None, :])
    decay_matrix = jnp.exp(jnp.where(linked, cumul[:, None] - cumul[None, :], 0.0)) * linked
    scores = matmul(c_block, b_block.T) * decay_matrix
    output = matmul(scores, x_block) + entry[:, None] * matmul(c_block, state.T)
    updated = through * state + matmul((x_block * leave[:, None]).T, b_block)
    return (output, updated)


def head_forward(state, x_head, b_blocks, c_blocks, log_head, note_blocks, befores):

    def head_advance(carry, block):
        output, updated = block_forward(carry, *block)
        return (updated, output)

    final, outputs = lax.scan(
        head_advance, state, (x_head, b_blocks, c_blocks, log_head, note_blocks, befores)
    )
    return (outputs, final)


def conv_forward(extended, weights, note_ext):
    width = weights.shape[0]
    count = extended.shape[0] - width + 1
    result = jnp.zeros((count, extended.shape[1]), jnp.float32)
    for k in range(width):
        linked = note_ext[k : k + count] == note_ext[width - 1 : width - 1 + count]
        result = result + weights[k][None, :] * extended[k : k + count] * linked[:, None]
    return result


def conv_backward(extended, weights, note_ext):
    width = weights.shape[0]
    count = extended.shape[0] - width + 1
    result = jnp.zeros((count, extended.shape[1]), jnp.float32)
    for k in range(width):
        lag = width - 1 - k
        linked = note_ext[lag : lag + count] == note_ext[:count]
        result = result + weights[k][None, :] * extended[lag : lag + count] * linked[:, None]
    return result


def silu_slope(values):
    sigma = jax.nn.sigmoid(values)
    return sigma * (1.0 + values * (1.0 - sigma))


def chain_combine(earlier, later):
    return (earlier[0] * later[0], later[0][:, None, None] * earlier[1] + later[1])


def chain_in(value, keep, axis, direction):
    count = lax.axis_size(axis)
    packed = jnp.concatenate(
        [value.reshape(value.shape[0], -1), jnp.broadcast_to(keep[:, None], (keep.shape[0], 128))], axis=1
    )
    total = jnp.zeros_like(value)
    scale = jnp.ones_like(keep)
    for distance in range(1, count):
        arrived = shifted(packed, axis, direction * distance)
        part = arrived[:, : value[0].size].reshape(value.shape)
        total = total + scale[:, None, None] * part
        scale = scale * arrived[:, value[0].size]
    return total


def running_sum(values):
    length = values.shape[-1]
    upper = (jnp.arange(length)[:, None] <= jnp.arange(length)[None, :]).astype(values.dtype)
    return jnp.dot(values, upper, precision=precise, preferred_element_type=jnp.float32)


def chain_both(state, adjoint, keep, axis):
    count, mine = lax.axis_size(axis), lax.axis_index(axis)
    heads, size = state.shape[0], state[0].size
    tail = jnp.broadcast_to(keep[:, None], (heads, 128))
    later = jnp.concatenate([state.reshape(heads, size), tail], axis=1)
    earlier = jnp.concatenate([adjoint.reshape(heads, size), tail], axis=1)
    targets = jnp.arange(count)[:, None, None]
    outgoing = jnp.where(targets > mine, later[None], jnp.where(targets < mine, earlier[None], 0.0))
    arrived = lax.all_to_all(outgoing, axis, 0, 0, tiled=False)
    keeps = arrived[:, :, size]
    totals = []
    for order in (range(count - 1, -1, -1), range(count)):
        weights = [None] * count
        scale = jnp.ones_like(keep)
        for source in order:
            near = (source < mine) if order.step < 0 else (source > mine)
            weights[source] = jnp.where(near, scale, 0.0)
            scale = jnp.where(near, scale * keeps[source], scale)
        combined = jnp.sum(jnp.stack(weights)[:, :, None] * arrived, axis=0)
        totals.append(combined[:, :size].reshape(state.shape))
    return totals[0], totals[1]


def einsum(spec, *operands):
    return jnp.einsum(spec, *operands, precision=lax.Precision.HIGH, preferred_element_type=jnp.float32)


def block_forward_all(state, x_all, b_all, c_all, log_all, note_blocks, befores):
    cumul = running_sum(log_all)
    entry = jnp.exp(cumul) * (note_blocks == befores[:, None])
    leave = jnp.exp(cumul[..., -1:] - cumul) * (note_blocks == note_blocks[:, -1:])
    through = jnp.exp(cumul[..., -1]) * (note_blocks[:, -1] == befores)
    length = note_blocks.shape[1]
    lower = jnp.arange(length)[:, None] >= jnp.arange(length)[None, :]
    linked = lower & (note_blocks[:, :, None] == note_blocks[:, None, :])
    differences = cumul[..., :, None] - cumul[..., None, :]
    decay_matrix = jnp.exp(jnp.where(linked, differences, 0.0)) * linked
    scores = einsum("bin,bjn->bij", c_all, b_all) * decay_matrix
    output = einsum("hbij,hbjp->hbip", scores, x_all)
    chunk = einsum("hbjp,bjn->hbpn", x_all * leave[..., None], b_all)
    starts = []
    for block in range(note_blocks.shape[0]):
        starts.append(state)
        state = through[:, block, None, None] * state + chunk[:, block]
    output = output + entry[..., None] * einsum("bin,hbpn->hbip", c_all, jnp.stack(starts, axis=1))
    return (output, state)


def local(pre_x, pre_bc, conv_x, conv_bc, log_decay, lengths, grad_out):
    tok_rows = pre_x.shape[0]
    head_count = log_decay.shape[0]
    rim_width = K - 1
    block_count = tok_rows // BLOCK
    seq_start = lax.axis_index("seq") * tok_rows
    positions = seq_start + jnp.arange(-rim_width, tok_rows + rim_width)
    note_all = note_index(positions, lengths)
    note_ids = note_all[rim_width : rim_width + tok_rows]
    before_both = shifted(
        jnp.concatenate([pre_x[tok_rows - rim_width :], pre_bc[tok_rows - rim_width :]], axis=1), "seq", 1
    )
    before_x, before_bc = before_both[:, : pre_x.shape[1]], before_both[:, pre_x.shape[1] :]
    u_x = conv_forward(
        jnp.concatenate([before_x, pre_x]).astype(jnp.float32),
        conv_x,
        note_all[: tok_rows + rim_width],
    )
    u_bc = conv_forward(
        jnp.concatenate([before_bc, pre_bc]).astype(jnp.float32),
        conv_bc,
        note_all[: tok_rows + rim_width],
    )
    v_x = jax.nn.silu(u_x)
    v_bc = jax.nn.silu(u_bc)
    x_heads = v_x.reshape(block_count, BLOCK, head_count, P_SIZE).transpose(2, 0, 1, 3)
    b_blocks = v_bc[:, :N].reshape(block_count, BLOCK, N)
    c_blocks = v_bc[:, N:].reshape(block_count, BLOCK, N)
    log_blocks = log_decay.reshape(head_count, block_count, BLOCK)
    grad_heads = (
        grad_out.astype(jnp.float32)
        .reshape(block_count, BLOCK, head_count, P_SIZE)
        .transpose(2, 0, 1, 3)
    )
    note_blocks = note_ids.reshape(block_count, BLOCK)
    befores = jnp.concatenate([note_all[rim_width - 1 : rim_width], note_blocks[:-1, -1]])

    note_before = note_all[rim_width - 1]
    log_rows = log_decay.astype(jnp.float32)
    x_rows = v_x.reshape(tok_rows, head_count, P_SIZE)
    g_rows = grad_out.astype(jnp.float32).reshape(tok_rows, head_count, P_SIZE)
    block_cumul = running_sum(log_blocks)
    offsets = [jnp.zeros_like(block_cumul[:, 0, -1])]
    for block in range(block_count - 1):
        offsets.append(offsets[-1] + block_cumul[:, block, -1])
    shard_cumul = (block_cumul + jnp.stack(offsets, axis=1)[:, :, None]).reshape(head_count, tok_rows)
    keep = jnp.exp(shard_cumul[:, -1]) * (note_ids[-1] == note_before)
    leave_rows = jnp.exp(shard_cumul[:, -1:] - shard_cumul) * (note_ids == note_ids[-1])
    entry_rows = jnp.exp(shard_cumul) * (note_ids == note_before)
    local_state = jnp.einsum(
        "thp,ht,tn->hpn", x_rows, leave_rows, v_bc[:, :N], precision=lax.Precision.HIGH,
        preferred_element_type=jnp.float32,
    )
    local_adjoint = jnp.einsum(
        "thp,ht,tn->hpn", g_rows, entry_rows, v_bc[:, N:], precision=lax.Precision.HIGH,
        preferred_element_type=jnp.float32,
    )
    state_in, adjoint_in = chain_both(local_state, local_adjoint, keep, "seq")

    def local_forward(x_all, b_all, c_all, log_all):
        return block_forward_all(
            state_in, x_all, b_all, c_all, log_all, note_blocks, befores
        )

    _, pull = jax.vjp(local_forward, x_heads, b_blocks, c_blocks, log_blocks)
    grad_x_heads, grad_b, grad_c, grad_log = pull((grad_heads, adjoint_in))
    grad_log_decay = grad_log.reshape(head_count, tok_rows)
    grad_v_x = grad_x_heads.transpose(1, 2, 0, 3).reshape(tok_rows, head_count * P_SIZE)
    grad_v_bc = jnp.concatenate([grad_b.reshape(tok_rows, N), grad_c.reshape(tok_rows, N)], axis=1)
    grad_u_x = grad_v_x * silu_slope(u_x)
    grad_u_bc = grad_v_bc * silu_slope(u_bc)
    after_bc = shifted(grad_u_bc[:rim_width], "seq", -1)
    after_x = shifted(grad_u_x[:rim_width], "seq", -1)
    grad_pre_x = conv_backward(jnp.concatenate([grad_u_x, after_x]), conv_x, note_all[rim_width:])
    bulk_bc = conv_backward(
        jnp.concatenate([grad_u_bc, jnp.zeros_like(after_bc)]), conv_bc, note_all[rim_width:]
    )
    tail_bc = conv_backward(
        jnp.concatenate([grad_u_bc[tok_rows - rim_width :], after_bc]),
        conv_bc,
        note_all[tok_rows : tok_rows + 2 * rim_width],
    )
    whole_bc = jnp.concatenate([bulk_bc[: tok_rows - rim_width], tail_bc])
    chips, cores = lax.axis_size("chip"), lax.axis_size("core")
    pieces = whole_bc.reshape(chips, cores, tok_rows // (chips * cores), whole_bc.shape[1])
    core = lax.axis_index("core")
    mine = lax.dynamic_index_in_dim(pieces, core, 1, keepdims=False)
    other = lax.dynamic_index_in_dim(pieces, 1 - core, 1, keepdims=False)
    pair_sum = mine + lax.ppermute(other, "core", [(0, 1), (1, 0)])
    grad_pre_bc = lax.all_to_all(pair_sum, "chip", 0, 0, tiled=False).sum(0)
    return (grad_pre_x, grad_pre_bc, grad_log_decay)


def solution(mesh):
    seq_size, head_size = mesh.shape["seq"], mesh.shape["head"]
    split = jax.sharding.Mesh(
        mesh.devices.reshape(seq_size, head_size // 2, 2), ("seq", "chip", "core")
    )
    head = ("chip", "core")
    placed = (
        P("seq", head),
        P("seq", None),
        P(None, head),
        P(),
        P(head, "seq"),
        P(),
        P("seq", head),
    )
    return jax.shard_map(
        local,
        mesh=split,
        in_specs=placed,
        out_specs=(P("seq", head), P(("seq",) + head, None), P(head, "seq")),
        check_vma=False,
    )
```

```python
import jax
import jax.numpy as jnp
from jax import lax
from jax.sharding import PartitionSpec as P

P_SIZE = 64
N = 128
K = 4
BLOCK = 256


precise = lax.Precision.HIGHEST


def shifted(value, axis, steps):
    count = lax.axis_size(axis)
    initial, last = (max(0, -steps), min(count, count - steps))
    return lax.ppermute(value, axis, [(source, source + steps) for source in range(initial, last)])


def entering(value, axis, join, neutral, backward):
    count, mine = (lax.axis_size(axis), lax.axis_index(axis))
    pieces = jax.tree.map(lambda part: lax.all_gather(part, axis), value)
    if backward:
        pieces = jax.tree.map(lambda part: part[::-1], pieces)
        mine = count - 1 - mine
    total = jax.tree.map(
        lambda part, zero: jnp.full_like(part, 0) + jnp.asarray(zero, part.dtype), value, neutral
    )

    def hop(position, total):
        longer = join(total, jax.tree.map(lambda part: part[position], pieces))
        return jax.tree.map(lambda new, old: jnp.where(position < mine, new, old), longer, total)

    return lax.fori_loop(0, count - 1, hop, total)


def matmul(left, right):
    return jnp.dot(left, right, precision=precise, preferred_element_type=jnp.float32)


def note_index(positions, lengths):
    starts = jnp.cumsum(lengths) - lengths
    hits = (positions[:, None] >= starts[None, :]).astype(jnp.int32)
    return jnp.sum(hits, axis=1) - 1


def block_edges(log_block, note_block, note_before):
    cumul = jnp.cumsum(log_block)
    entry = jnp.exp(cumul) * (note_block == note_before)
    leave = jnp.exp(cumul[-1] - cumul) * (note_block == note_block[-1])
    through = jnp.exp(cumul[-1]) * (note_block[-1] == note_before)
    return (cumul, entry, leave, through)


def block_forward(state, x_block, b_block, c_block, log_block, note_block, note_before):
    cumul, entry, leave, through = block_edges(log_block, note_block, note_before)
    length = note_block.shape[0]
    lower = jnp.arange(length)[:, None] >= jnp.arange(length)[None, :]
    linked = lower & (note_block[:, None] == note_block[None, :])
    decay_matrix = jnp.exp(jnp.where(linked, cumul[:, None] - cumul[None, :], 0.0)) * linked
    scores = matmul(c_block, b_block.T) * decay_matrix
    output = matmul(scores, x_block) + entry[:, None] * matmul(c_block, state.T)
    updated = through * state + matmul((x_block * leave[:, None]).T, b_block)
    return (output, updated)


def head_forward(state, x_head, b_blocks, c_blocks, log_head, note_blocks, befores):

    def head_advance(carry, block):
        output, updated = block_forward(carry, *block)
        return (updated, output)

    final, outputs = lax.scan(
        head_advance, state, (x_head, b_blocks, c_blocks, log_head, note_blocks, befores)
    )
    return (outputs, final)


def conv_forward(extended, weights, note_ext):
    width = weights.shape[0]
    count = extended.shape[0] - width + 1
    result = jnp.zeros((count, extended.shape[1]), jnp.float32)
    for k in range(width):
        linked = note_ext[k : k + count] == note_ext[width - 1 : width - 1 + count]
        result = result + weights[k][None, :] * extended[k : k + count] * linked[:, None]
    return result


def conv_backward(extended, weights, note_ext):
    width = weights.shape[0]
    count = extended.shape[0] - width + 1
    result = jnp.zeros((count, extended.shape[1]), jnp.float32)
    for k in range(width):
        lag = width - 1 - k
        linked = note_ext[lag : lag + count] == note_ext[:count]
        result = result + weights[k][None, :] * extended[lag : lag + count] * linked[:, None]
    return result


def silu_slope(values):
    sigma = jax.nn.sigmoid(values)
    return sigma * (1.0 + values * (1.0 - sigma))


def chain_combine(earlier, later):
    return (earlier[0] * later[0], later[0][:, None, None] * earlier[1] + later[1])


def chain_in(value, keep, axis, direction):
    count = lax.axis_size(axis)
    packed = jnp.concatenate(
        [value.reshape(value.shape[0], -1), jnp.broadcast_to(keep[:, None], (keep.shape[0], 128))], axis=1
    )
    total = jnp.zeros_like(value)
    scale = jnp.ones_like(keep)
    for distance in range(1, count):
        arrived = shifted(packed, axis, direction * distance)
        part = arrived[:, : value[0].size].reshape(value.shape)
        total = total + scale[:, None, None] * part
        scale = scale * arrived[:, value[0].size]
    return total


def running_sum(values):
    length = values.shape[-1]
    upper = (jnp.arange(length)[:, None] <= jnp.arange(length)[None, :]).astype(values.dtype)
    return jnp.dot(values, upper, precision=precise, preferred_element_type=jnp.float32)


def chain_both(state, adjoint, keep, axis):
    count, mine = lax.axis_size(axis), lax.axis_index(axis)
    heads, size = state.shape[0], state[0].size
    tail = jnp.broadcast_to(keep[:, None], (heads, 128))
    later = jnp.concatenate([state.reshape(heads, size), tail], axis=1)
    earlier = jnp.concatenate([adjoint.reshape(heads, size), tail], axis=1)
    targets = jnp.arange(count)[:, None, None]
    outgoing = jnp.where(targets > mine, later[None], jnp.where(targets < mine, earlier[None], 0.0))
    arrived = lax.all_to_all(outgoing, axis, 0, 0, tiled=False)
    keeps = arrived[:, :, size]
    totals = []
    for order in (range(count - 1, -1, -1), range(count)):
        weights = [None] * count
        scale = jnp.ones_like(keep)
        for source in order:
            near = (source < mine) if order.step < 0 else (source > mine)
            weights[source] = jnp.where(near, scale, 0.0)
            scale = jnp.where(near, scale * keeps[source], scale)
        combined = jnp.sum(jnp.stack(weights)[:, :, None] * arrived, axis=0)
        totals.append(combined[:, :size].reshape(state.shape))
    return totals[0], totals[1]


def einsum(spec, *operands):
    return jnp.einsum(spec, *operands, precision=lax.Precision.HIGH, preferred_element_type=jnp.float32)


def block_forward_all(state, x_all, b_all, c_all, log_all, note_blocks, befores):
    cumul = running_sum(log_all)
    entry = jnp.exp(cumul) * (note_blocks == befores[:, None])
    leave = jnp.exp(cumul[..., -1:] - cumul) * (note_blocks == note_blocks[:, -1:])
    through = jnp.exp(cumul[..., -1]) * (note_blocks[:, -1] == befores)
    length = note_blocks.shape[1]
    lower = jnp.arange(length)[:, None] >= jnp.arange(length)[None, :]
    linked = lower & (note_blocks[:, :, None] == note_blocks[:, None, :])
    differences = cumul[..., :, None] - cumul[..., None, :]
    decay_matrix = jnp.exp(jnp.where(linked, differences, 0.0)) * linked
    scores = einsum("bin,bjn->bij", c_all, b_all) * decay_matrix
    output = einsum("hbij,hbjp->hbip", scores, x_all)
    chunk = einsum("hbjp,bjn->hbpn", x_all * leave[..., None], b_all)
    starts = []
    for block in range(note_blocks.shape[0]):
        starts.append(state)
        state = through[:, block, None, None] * state + chunk[:, block]
    output = output + entry[..., None] * einsum("bin,hbpn->hbip", c_all, jnp.stack(starts, axis=1))
    return (output, state)


def local(pre_x, pre_bc, conv_x, conv_bc, log_decay, lengths, grad_out):
    tok_rows = pre_x.shape[0]
    head_count = log_decay.shape[0]
    rim_width = K - 1
    block_count = tok_rows // BLOCK
    seq_start = lax.axis_index("seq") * tok_rows
    positions = seq_start + jnp.arange(-rim_width, tok_rows + rim_width)
    note_all = note_index(positions, lengths)
    note_ids = note_all[rim_width : rim_width + tok_rows]
    before_both = shifted(
        jnp.concatenate([pre_x[tok_rows - rim_width :], pre_bc[tok_rows - rim_width :]], axis=1), "seq", 1
    )
    before_x, before_bc = before_both[:, : pre_x.shape[1]], before_both[:, pre_x.shape[1] :]
    u_x = conv_forward(
        jnp.concatenate([before_x, pre_x]).astype(jnp.float32),
        conv_x,
        note_all[: tok_rows + rim_width],
    )
    u_bc = conv_forward(
        jnp.concatenate([before_bc, pre_bc]).astype(jnp.float32),
        conv_bc,
        note_all[: tok_rows + rim_width],
    )
    v_x = jax.nn.silu(u_x)
    v_bc = jax.nn.silu(u_bc)
    x_heads = v_x.reshape(block_count, BLOCK, head_count, P_SIZE).transpose(2, 0, 1, 3)
    b_blocks = v_bc[:, :N].reshape(block_count, BLOCK, N)
    c_blocks = v_bc[:, N:].reshape(block_count, BLOCK, N)
    log_blocks = log_decay.reshape(head_count, block_count, BLOCK)
    grad_heads = (
        grad_out.astype(jnp.float32)
        .reshape(block_count, BLOCK, head_count, P_SIZE)
        .transpose(2, 0, 1, 3)
    )
    note_blocks = note_ids.reshape(block_count, BLOCK)
    befores = jnp.concatenate([note_all[rim_width - 1 : rim_width], note_blocks[:-1, -1]])

    note_before = note_all[rim_width - 1]
    log_rows = log_decay.astype(jnp.float32)
    x_rows = v_x.reshape(tok_rows, head_count, P_SIZE)
    g_rows = grad_out.astype(jnp.float32).reshape(tok_rows, head_count, P_SIZE)
    block_cumul = running_sum(log_blocks)
    offsets = [jnp.zeros_like(block_cumul[:, 0, -1])]
    for block in range(block_count - 1):
        offsets.append(offsets[-1] + block_cumul[:, block, -1])
    shard_cumul = (block_cumul + jnp.stack(offsets, axis=1)[:, :, None]).reshape(head_count, tok_rows)
    keep = jnp.exp(shard_cumul[:, -1]) * (note_ids[-1] == note_before)
    leave_rows = jnp.exp(shard_cumul[:, -1:] - shard_cumul) * (note_ids == note_ids[-1])
    entry_rows = jnp.exp(shard_cumul) * (note_ids == note_before)
    local_state = jnp.einsum(
        "thp,ht,tn->hpn", x_rows, leave_rows, v_bc[:, :N], precision=lax.Precision.HIGH,
        preferred_element_type=jnp.float32,
    )
    local_adjoint = jnp.einsum(
        "thp,ht,tn->hpn", g_rows, entry_rows, v_bc[:, N:], precision=lax.Precision.HIGH,
        preferred_element_type=jnp.float32,
    )
    state_in, adjoint_in = chain_both(local_state, local_adjoint, keep, "seq")

    def local_forward(x_all, b_all, c_all, log_all):
        return block_forward_all(
            state_in, x_all, b_all, c_all, log_all, note_blocks, befores
        )

    _, pull = jax.vjp(local_forward, x_heads, b_blocks, c_blocks, log_blocks)
    grad_x_heads, grad_b, grad_c, grad_log = pull((grad_heads, adjoint_in))
    grad_log_decay = grad_log.reshape(head_count, tok_rows)
    grad_v_x = grad_x_heads.transpose(1, 2, 0, 3).reshape(tok_rows, head_count * P_SIZE)
    grad_v_bc = jnp.concatenate([grad_b.reshape(tok_rows, N), grad_c.reshape(tok_rows, N)], axis=1)
    grad_u_x = grad_v_x * silu_slope(u_x)
    grad_u_bc = grad_v_bc * silu_slope(u_bc)
    after_bc = shifted(grad_u_bc[:rim_width], "seq", -1)
    after_x = shifted(grad_u_x[:rim_width], "seq", -1)
    bulk_x = conv_backward(
        jnp.concatenate([grad_u_x, jnp.zeros_like(after_x)]), conv_x, note_all[rim_width:]
    )
    tail_x = conv_backward(
        jnp.concatenate([grad_u_x[tok_rows - rim_width :], after_x]),
        conv_x,
        note_all[tok_rows : tok_rows + 2 * rim_width],
    )
    grad_pre_x = jnp.concatenate([bulk_x[: tok_rows - rim_width], tail_x])
    bulk_bc = conv_backward(
        jnp.concatenate([grad_u_bc, jnp.zeros_like(after_bc)]), conv_bc, note_all[rim_width:]
    )
    tail_bc = conv_backward(
        jnp.concatenate([grad_u_bc[tok_rows - rim_width :], after_bc]),
        conv_bc,
        note_all[tok_rows : tok_rows + 2 * rim_width],
    )
    whole_bc = jnp.concatenate([bulk_bc[: tok_rows - rim_width], tail_bc])
    chips, cores = lax.axis_size("chip"), lax.axis_size("core")
    pieces = whole_bc.reshape(chips, cores, tok_rows // (chips * cores), whole_bc.shape[1])
    core = lax.axis_index("core")
    mine = lax.dynamic_index_in_dim(pieces, core, 1, keepdims=False)
    other = lax.dynamic_index_in_dim(pieces, 1 - core, 1, keepdims=False)
    pair_sum = mine + lax.ppermute(other, "core", [(0, 1), (1, 0)])
    grad_pre_bc = lax.all_to_all(pair_sum, "chip", 0, 0, tiled=False).sum(0)
    return (grad_pre_x, grad_pre_bc, grad_log_decay)


def solution(mesh):
    seq_size, head_size = mesh.shape["seq"], mesh.shape["head"]
    split = jax.sharding.Mesh(
        mesh.devices.reshape(seq_size, head_size // 2, 2), ("seq", "chip", "core")
    )
    head = ("chip", "core")
    placed = (
        P("seq", head),
        P("seq", None),
        P(None, head),
        P(),
        P(head, "seq"),
        P(),
        P("seq", head),
    )
    return jax.shard_map(
        local,
        mesh=split,
        in_specs=placed,
        out_specs=(P("seq", head), P(("seq",) + head, None), P(head, "seq")),
        check_vma=False,
    )
```

```python
import jax
import jax.numpy as jnp
from jax import lax
from jax.sharding import PartitionSpec as P

P_SIZE = 64
N = 128
K = 4
BLOCK = 256


precise = lax.Precision.HIGHEST


def shifted(value, axis, steps):
    count = lax.axis_size(axis)
    initial, last = (max(0, -steps), min(count, count - steps))
    return lax.ppermute(value, axis, [(source, source + steps) for source in range(initial, last)])


def entering(value, axis, join, neutral, backward):
    count, mine = (lax.axis_size(axis), lax.axis_index(axis))
    pieces = jax.tree.map(lambda part: lax.all_gather(part, axis), value)
    if backward:
        pieces = jax.tree.map(lambda part: part[::-1], pieces)
        mine = count - 1 - mine
    total = jax.tree.map(
        lambda part, zero: jnp.full_like(part, 0) + jnp.asarray(zero, part.dtype), value, neutral
    )

    def hop(position, total):
        longer = join(total, jax.tree.map(lambda part: part[position], pieces))
        return jax.tree.map(lambda new, old: jnp.where(position < mine, new, old), longer, total)

    return lax.fori_loop(0, count - 1, hop, total)


def matmul(left, right):
    return jnp.dot(left, right, precision=precise, preferred_element_type=jnp.float32)


def note_index(positions, lengths):
    starts = jnp.cumsum(lengths) - lengths
    hits = (positions[:, None] >= starts[None, :]).astype(jnp.int32)
    return jnp.sum(hits, axis=1) - 1


def block_edges(log_block, note_block, note_before):
    cumul = jnp.cumsum(log_block)
    entry = jnp.exp(cumul) * (note_block == note_before)
    leave = jnp.exp(cumul[-1] - cumul) * (note_block == note_block[-1])
    through = jnp.exp(cumul[-1]) * (note_block[-1] == note_before)
    return (cumul, entry, leave, through)


def block_forward(state, x_block, b_block, c_block, log_block, note_block, note_before):
    cumul, entry, leave, through = block_edges(log_block, note_block, note_before)
    length = note_block.shape[0]
    lower = jnp.arange(length)[:, None] >= jnp.arange(length)[None, :]
    linked = lower & (note_block[:, None] == note_block[None, :])
    decay_matrix = jnp.exp(jnp.where(linked, cumul[:, None] - cumul[None, :], 0.0)) * linked
    scores = matmul(c_block, b_block.T) * decay_matrix
    output = matmul(scores, x_block) + entry[:, None] * matmul(c_block, state.T)
    updated = through * state + matmul((x_block * leave[:, None]).T, b_block)
    return (output, updated)


def head_forward(state, x_head, b_blocks, c_blocks, log_head, note_blocks, befores):

    def head_advance(carry, block):
        output, updated = block_forward(carry, *block)
        return (updated, output)

    final, outputs = lax.scan(
        head_advance, state, (x_head, b_blocks, c_blocks, log_head, note_blocks, befores)
    )
    return (outputs, final)


def conv_forward(extended, weights, note_ext):
    width = weights.shape[0]
    count = extended.shape[0] - width + 1
    result = jnp.zeros((count, extended.shape[1]), jnp.float32)
    for k in range(width):
        linked = note_ext[k : k + count] == note_ext[width - 1 : width - 1 + count]
        result = result + weights[k][None, :] * extended[k : k + count] * linked[:, None]
    return result


def conv_backward(extended, weights, note_ext):
    width = weights.shape[0]
    count = extended.shape[0] - width + 1
    result = jnp.zeros((count, extended.shape[1]), jnp.float32)
    for k in range(width):
        lag = width - 1 - k
        linked = note_ext[lag : lag + count] == note_ext[:count]
        result = result + weights[k][None, :] * extended[lag : lag + count] * linked[:, None]
    return result


def silu_slope(values):
    sigma = jax.nn.sigmoid(values)
    return sigma * (1.0 + values * (1.0 - sigma))


def chain_combine(earlier, later):
    return (earlier[0] * later[0], later[0][:, None, None] * earlier[1] + later[1])


def chain_in(value, keep, axis, direction):
    count = lax.axis_size(axis)
    packed = jnp.concatenate(
        [value.reshape(value.shape[0], -1), jnp.broadcast_to(keep[:, None], (keep.shape[0], 128))], axis=1
    )
    total = jnp.zeros_like(value)
    scale = jnp.ones_like(keep)
    for distance in range(1, count):
        arrived = shifted(packed, axis, direction * distance)
        part = arrived[:, : value[0].size].reshape(value.shape)
        total = total + scale[:, None, None] * part
        scale = scale * arrived[:, value[0].size]
    return total


def running_sum(values):
    length = values.shape[-1]
    upper = (jnp.arange(length)[:, None] <= jnp.arange(length)[None, :]).astype(values.dtype)
    return jnp.dot(values, upper, precision=precise, preferred_element_type=jnp.float32)


def chain_both(state, adjoint, keep, axis):
    count, mine = lax.axis_size(axis), lax.axis_index(axis)
    heads, size = state.shape[0], state[0].size
    tail = jnp.broadcast_to(keep[:, None], (heads, 128))
    later = jnp.concatenate([state.reshape(heads, size), tail], axis=1)
    earlier = jnp.concatenate([adjoint.reshape(heads, size), tail], axis=1)
    targets = jnp.arange(count)[:, None, None]
    outgoing = jnp.where(targets > mine, later[None], jnp.where(targets < mine, earlier[None], 0.0))
    arrived = lax.all_to_all(outgoing, axis, 0, 0, tiled=False)
    keeps = arrived[:, :, size]
    totals = []
    for order in (range(count - 1, -1, -1), range(count)):
        weights = [None] * count
        scale = jnp.ones_like(keep)
        for source in order:
            near = (source < mine) if order.step < 0 else (source > mine)
            weights[source] = jnp.where(near, scale, 0.0)
            scale = jnp.where(near, scale * keeps[source], scale)
        combined = jnp.sum(jnp.stack(weights)[:, :, None] * arrived, axis=0)
        totals.append(combined[:, :size].reshape(state.shape))
    return totals[0], totals[1]


def einsum(spec, *operands):
    return jnp.einsum(spec, *operands, precision=lax.Precision.HIGH, preferred_element_type=jnp.float32)


def block_forward_all(state, x_all, b_all, c_all, log_all, note_blocks, befores):
    cumul = running_sum(log_all)
    entry = jnp.exp(cumul) * (note_blocks == befores[:, None])
    leave = jnp.exp(cumul[..., -1:] - cumul) * (note_blocks == note_blocks[:, -1:])
    through = jnp.exp(cumul[..., -1]) * (note_blocks[:, -1] == befores)
    length = note_blocks.shape[1]
    lower = jnp.arange(length)[:, None] >= jnp.arange(length)[None, :]
    linked = lower & (note_blocks[:, :, None] == note_blocks[:, None, :])
    differences = cumul[..., :, None] - cumul[..., None, :]
    decay_matrix = jnp.exp(jnp.where(linked, differences, 0.0)) * linked
    scores = einsum("bin,bjn->bij", c_all, b_all) * decay_matrix
    output = einsum("hbij,hbjp->hbip", scores, x_all)
    chunk = einsum("hbjp,bjn->hbpn", x_all * leave[..., None], b_all)
    starts = []
    for block in range(note_blocks.shape[0]):
        starts.append(state)
        state = through[:, block, None, None] * state + chunk[:, block]
    output = output + entry[..., None] * einsum("bin,hbpn->hbip", c_all, jnp.stack(starts, axis=1))
    return (output, state)


def local(pre_x, pre_bc, conv_x, conv_bc, log_decay, lengths, grad_out):
    tok_rows = pre_x.shape[0]
    head_count = log_decay.shape[0]
    rim_width = K - 1
    block_count = tok_rows // BLOCK
    seq_start = lax.axis_index("seq") * tok_rows
    positions = seq_start + jnp.arange(-rim_width, tok_rows + rim_width)
    note_all = note_index(positions, lengths)
    note_ids = note_all[rim_width : rim_width + tok_rows]
    before_both = shifted(
        jnp.concatenate([pre_x[tok_rows - rim_width :], pre_bc[tok_rows - rim_width :]], axis=1), "seq", 1
    )
    before_x, before_bc = before_both[:, : pre_x.shape[1]], before_both[:, pre_x.shape[1] :]
    u_x = conv_forward(
        jnp.concatenate([before_x, pre_x]).astype(jnp.float32),
        conv_x,
        note_all[: tok_rows + rim_width],
    )
    u_bc = conv_forward(
        jnp.concatenate([before_bc, pre_bc]).astype(jnp.float32),
        conv_bc,
        note_all[: tok_rows + rim_width],
    )
    v_x = jax.nn.silu(u_x)
    v_bc = jax.nn.silu(u_bc)
    x_heads = v_x.reshape(block_count, BLOCK, head_count, P_SIZE).transpose(2, 0, 1, 3)
    b_blocks = v_bc[:, :N].reshape(block_count, BLOCK, N)
    c_blocks = v_bc[:, N:].reshape(block_count, BLOCK, N)
    log_blocks = log_decay.reshape(head_count, block_count, BLOCK)
    grad_heads = (
        grad_out.astype(jnp.float32)
        .reshape(block_count, BLOCK, head_count, P_SIZE)
        .transpose(2, 0, 1, 3)
    )
    note_blocks = note_ids.reshape(block_count, BLOCK)
    befores = jnp.concatenate([note_all[rim_width - 1 : rim_width], note_blocks[:-1, -1]])

    note_before = note_all[rim_width - 1]
    log_rows = log_decay.astype(jnp.float32)
    x_rows = v_x.reshape(tok_rows, head_count, P_SIZE)
    g_rows = grad_out.astype(jnp.float32).reshape(tok_rows, head_count, P_SIZE)
    block_cumul = running_sum(log_blocks)
    offsets = [jnp.zeros_like(block_cumul[:, 0, -1])]
    for block in range(block_count - 1):
        offsets.append(offsets[-1] + block_cumul[:, block, -1])
    shard_cumul = (block_cumul + jnp.stack(offsets, axis=1)[:, :, None]).reshape(head_count, tok_rows)
    keep = jnp.exp(shard_cumul[:, -1]) * (note_ids[-1] == note_before)
    leave_rows = jnp.exp(shard_cumul[:, -1:] - shard_cumul) * (note_ids == note_ids[-1])
    entry_rows = jnp.exp(shard_cumul) * (note_ids == note_before)
    local_state = jnp.einsum(
        "thp,ht,tn->hpn", x_rows, leave_rows, v_bc[:, :N], precision=lax.Precision.HIGH,
        preferred_element_type=jnp.float32,
    )
    local_adjoint = jnp.einsum(
        "thp,ht,tn->hpn", g_rows, entry_rows, v_bc[:, N:], precision=lax.Precision.HIGH,
        preferred_element_type=jnp.float32,
    )
    state_in, adjoint_in = chain_both(local_state, local_adjoint, keep, "seq")

    def local_forward(x_all, b_all, c_all, log_all):
        return block_forward_all(
            state_in, x_all, b_all, c_all, log_all, note_blocks, befores
        )

    _, pull = jax.vjp(local_forward, x_heads, b_blocks, c_blocks, log_blocks)
    grad_x_heads, grad_b, grad_c, grad_log = pull((grad_heads, adjoint_in))
    grad_log_decay = grad_log.reshape(head_count, tok_rows)
    grad_v_x = grad_x_heads.transpose(1, 2, 0, 3).reshape(tok_rows, head_count * P_SIZE)
    grad_v_bc = jnp.concatenate([grad_b.reshape(tok_rows, N), grad_c.reshape(tok_rows, N)], axis=1)
    grad_u_x = grad_v_x * silu_slope(u_x)
    grad_u_bc = grad_v_bc * silu_slope(u_bc)
    after_bc = shifted(grad_u_bc[:rim_width], "seq", -1)
    after_x = shifted(grad_u_x[:rim_width], "seq", -1)
    grad_pre_x = conv_backward(jnp.concatenate([grad_u_x, after_x]), conv_x, note_all[rim_width:])
    bulk_bc = conv_backward(
        jnp.concatenate([grad_u_bc, jnp.zeros_like(after_bc)]), conv_bc, note_all[rim_width:]
    )
    rim_bc = conv_backward(
        jnp.concatenate([jnp.zeros_like(after_bc), after_bc]),
        conv_bc,
        note_all[tok_rows : tok_rows + 2 * rim_width],
    )
    chips, cores = lax.axis_size("chip"), lax.axis_size("core")
    share = tok_rows // (chips * cores)
    pieces = bulk_bc.reshape(chips, cores, share, bulk_bc.shape[1])
    core = lax.axis_index("core")
    mine = lax.dynamic_index_in_dim(pieces, core, 1, keepdims=False)
    other = lax.dynamic_index_in_dim(pieces, 1 - core, 1, keepdims=False)
    pair_sum = mine + lax.ppermute(other, "core", [(0, 1), (1, 0)])
    rim_pair = rim_bc + lax.ppermute(rim_bc, "core", [(source, cores - 1) for source in range(cores - 1)])
    rim_pair = jnp.where(core == cores - 1, rim_pair, 0.0)
    pair_sum = pair_sum.at[chips - 1, share - rim_width :].add(rim_pair)
    grad_pre_bc = lax.all_to_all(pair_sum, "chip", 0, 0, tiled=False).sum(0)
    return (grad_pre_x, grad_pre_bc, grad_log_decay)


def solution(mesh):
    seq_size, head_size = mesh.shape["seq"], mesh.shape["head"]
    split = jax.sharding.Mesh(
        mesh.devices.reshape(seq_size, head_size // 2, 2), ("seq", "chip", "core")
    )
    head = ("chip", "core")
    placed = (
        P("seq", head),
        P("seq", None),
        P(None, head),
        P(),
        P(head, "seq"),
        P(),
        P("seq", head),
    )
    return jax.shard_map(
        local,
        mesh=split,
        in_specs=placed,
        out_specs=(P("seq", head), P(("seq",) + head, None), P(head, "seq")),
        check_vma=False,
    )
```

```python
import jax
import jax.numpy as jnp
from jax import lax
from jax.sharding import PartitionSpec as P

P_SIZE = 64
N = 128
K = 4
BLOCK = 256


precise = lax.Precision.HIGHEST


def shifted(value, axis, steps):
    count = lax.axis_size(axis)
    initial, last = (max(0, -steps), min(count, count - steps))
    return lax.ppermute(value, axis, [(source, source + steps) for source in range(initial, last)])


def entering(value, axis, join, neutral, backward):
    count, mine = (lax.axis_size(axis), lax.axis_index(axis))
    pieces = jax.tree.map(lambda part: lax.all_gather(part, axis), value)
    if backward:
        pieces = jax.tree.map(lambda part: part[::-1], pieces)
        mine = count - 1 - mine
    total = jax.tree.map(
        lambda part, zero: jnp.full_like(part, 0) + jnp.asarray(zero, part.dtype), value, neutral
    )

    def hop(position, total):
        longer = join(total, jax.tree.map(lambda part: part[position], pieces))
        return jax.tree.map(lambda new, old: jnp.where(position < mine, new, old), longer, total)

    return lax.fori_loop(0, count - 1, hop, total)


def matmul(left, right):
    return jnp.dot(left, right, precision=precise, preferred_element_type=jnp.float32)


def note_index(positions, lengths):
    starts = jnp.cumsum(lengths) - lengths
    hits = (positions[:, None] >= starts[None, :]).astype(jnp.int32)
    return jnp.sum(hits, axis=1) - 1


def block_edges(log_block, note_block, note_before):
    cumul = jnp.cumsum(log_block)
    entry = jnp.exp(cumul) * (note_block == note_before)
    leave = jnp.exp(cumul[-1] - cumul) * (note_block == note_block[-1])
    through = jnp.exp(cumul[-1]) * (note_block[-1] == note_before)
    return (cumul, entry, leave, through)


def block_forward(state, x_block, b_block, c_block, log_block, note_block, note_before):
    cumul, entry, leave, through = block_edges(log_block, note_block, note_before)
    length = note_block.shape[0]
    lower = jnp.arange(length)[:, None] >= jnp.arange(length)[None, :]
    linked = lower & (note_block[:, None] == note_block[None, :])
    decay_matrix = jnp.exp(jnp.where(linked, cumul[:, None] - cumul[None, :], 0.0)) * linked
    scores = matmul(c_block, b_block.T) * decay_matrix
    output = matmul(scores, x_block) + entry[:, None] * matmul(c_block, state.T)
    updated = through * state + matmul((x_block * leave[:, None]).T, b_block)
    return (output, updated)


def head_forward(state, x_head, b_blocks, c_blocks, log_head, note_blocks, befores):

    def head_advance(carry, block):
        output, updated = block_forward(carry, *block)
        return (updated, output)

    final, outputs = lax.scan(
        head_advance, state, (x_head, b_blocks, c_blocks, log_head, note_blocks, befores)
    )
    return (outputs, final)


def conv_forward(extended, weights, note_ext):
    width = weights.shape[0]
    count = extended.shape[0] - width + 1
    result = jnp.zeros((count, extended.shape[1]), jnp.float32)
    for k in range(width):
        linked = note_ext[k : k + count] == note_ext[width - 1 : width - 1 + count]
        result = result + weights[k][None, :] * extended[k : k + count] * linked[:, None]
    return result


def conv_backward(extended, weights, note_ext):
    width = weights.shape[0]
    count = extended.shape[0] - width + 1
    result = jnp.zeros((count, extended.shape[1]), jnp.float32)
    for k in range(width):
        lag = width - 1 - k
        linked = note_ext[lag : lag + count] == note_ext[:count]
        result = result + weights[k][None, :] * extended[lag : lag + count] * linked[:, None]
    return result


def silu_slope(values):
    sigma = jax.nn.sigmoid(values)
    return sigma * (1.0 + values * (1.0 - sigma))


def chain_combine(earlier, later):
    return (earlier[0] * later[0], later[0][:, None, None] * earlier[1] + later[1])


def chain_in(value, keep, axis, direction):
    count = lax.axis_size(axis)
    packed = jnp.concatenate(
        [value.reshape(value.shape[0], -1), jnp.broadcast_to(keep[:, None], (keep.shape[0], 128))], axis=1
    )
    total = jnp.zeros_like(value)
    scale = jnp.ones_like(keep)
    for distance in range(1, count):
        arrived = shifted(packed, axis, direction * distance)
        part = arrived[:, : value[0].size].reshape(value.shape)
        total = total + scale[:, None, None] * part
        scale = scale * arrived[:, value[0].size]
    return total


def running_sum(values):
    length = values.shape[-1]
    upper = (jnp.arange(length)[:, None] <= jnp.arange(length)[None, :]).astype(values.dtype)
    return jnp.dot(values, upper, precision=precise, preferred_element_type=jnp.float32)


def chain_both(state, adjoint, keep, axis):
    count, mine = lax.axis_size(axis), lax.axis_index(axis)
    heads, size = state.shape[0], state[0].size
    tail = jnp.broadcast_to(keep[:, None], (heads, 128))
    later = jnp.concatenate([state.reshape(heads, size), tail], axis=1)
    earlier = jnp.concatenate([adjoint.reshape(heads, size), tail], axis=1)
    targets = jnp.arange(count)[:, None, None]
    outgoing = jnp.where(targets > mine, later[None], jnp.where(targets < mine, earlier[None], 0.0))
    arrived = lax.all_to_all(outgoing, axis, 0, 0, tiled=False)
    keeps = arrived[:, :, size]
    totals = []
    for order in (range(count - 1, -1, -1), range(count)):
        weights = [None] * count
        scale = jnp.ones_like(keep)
        for source in order:
            near = (source < mine) if order.step < 0 else (source > mine)
            weights[source] = jnp.where(near, scale, 0.0)
            scale = jnp.where(near, scale * keeps[source], scale)
        combined = jnp.sum(jnp.stack(weights)[:, :, None] * arrived, axis=0)
        totals.append(combined[:, :size].reshape(state.shape))
    return totals[0], totals[1]


def einsum(spec, *operands):
    return jnp.einsum(spec, *operands, precision=lax.Precision.HIGH, preferred_element_type=jnp.float32)


def block_forward_all(state, x_all, b_all, c_all, log_all, note_blocks, befores):
    cumul = running_sum(log_all)
    entry = jnp.exp(cumul) * (note_blocks == befores[:, None])
    leave = jnp.exp(cumul[..., -1:] - cumul) * (note_blocks == note_blocks[:, -1:])
    through = jnp.exp(cumul[..., -1]) * (note_blocks[:, -1] == befores)
    length = note_blocks.shape[1]
    lower = jnp.arange(length)[:, None] >= jnp.arange(length)[None, :]
    linked = lower & (note_blocks[:, :, None] == note_blocks[:, None, :])
    differences = cumul[..., :, None] - cumul[..., None, :]
    decay_matrix = jnp.exp(jnp.where(linked, differences, 0.0)) * linked
    scores = einsum("bin,bjn->bij", c_all, b_all) * decay_matrix
    output = einsum("hbij,hbjp->hbip", scores, x_all)
    chunk = einsum("hbjp,bjn->hbpn", x_all * leave[..., None], b_all)
    starts = []
    for block in range(note_blocks.shape[0]):
        starts.append(state)
        state = through[:, block, None, None] * state + chunk[:, block]
    output = output + entry[..., None] * einsum("bin,hbpn->hbip", c_all, jnp.stack(starts, axis=1))
    return (output, state)


def local(pre_x, pre_bc, conv_x, conv_bc, log_decay, lengths, grad_out):
    tok_rows = pre_x.shape[0]
    head_count = log_decay.shape[0]
    rim_width = K - 1
    block_count = tok_rows // BLOCK
    seq_start = lax.axis_index("seq") * tok_rows
    positions = seq_start + jnp.arange(-rim_width, tok_rows + rim_width)
    note_all = note_index(positions, lengths)
    note_ids = note_all[rim_width : rim_width + tok_rows]
    before_both = shifted(
        jnp.concatenate([pre_x[tok_rows - rim_width :], pre_bc[tok_rows - rim_width :]], axis=1), "seq", 1
    )
    before_x, before_bc = before_both[:, : pre_x.shape[1]], before_both[:, pre_x.shape[1] :]
    u_x = conv_forward(
        jnp.concatenate([before_x, pre_x]).astype(jnp.float32),
        conv_x,
        note_all[: tok_rows + rim_width],
    )
    u_bc = conv_forward(
        jnp.concatenate([before_bc, pre_bc]).astype(jnp.float32),
        conv_bc,
        note_all[: tok_rows + rim_width],
    )
    v_x = jax.nn.silu(u_x)
    v_bc = jax.nn.silu(u_bc)
    x_heads = v_x.reshape(block_count, BLOCK, head_count, P_SIZE).transpose(2, 0, 1, 3)
    b_blocks = v_bc[:, :N].reshape(block_count, BLOCK, N)
    c_blocks = v_bc[:, N:].reshape(block_count, BLOCK, N)
    log_blocks = log_decay.reshape(head_count, block_count, BLOCK)
    grad_heads = (
        grad_out.astype(jnp.float32)
        .reshape(block_count, BLOCK, head_count, P_SIZE)
        .transpose(2, 0, 1, 3)
    )
    note_blocks = note_ids.reshape(block_count, BLOCK)
    befores = jnp.concatenate([note_all[rim_width - 1 : rim_width], note_blocks[:-1, -1]])

    note_before = note_all[rim_width - 1]
    log_rows = log_decay.astype(jnp.float32)
    x_rows = v_x.reshape(tok_rows, head_count, P_SIZE)
    g_rows = grad_out.astype(jnp.float32).reshape(tok_rows, head_count, P_SIZE)
    block_cumul = running_sum(log_blocks)
    offsets = [jnp.zeros_like(block_cumul[:, 0, -1])]
    for block in range(block_count - 1):
        offsets.append(offsets[-1] + block_cumul[:, block, -1])
    shard_cumul = (block_cumul + jnp.stack(offsets, axis=1)[:, :, None]).reshape(head_count, tok_rows)
    keep = jnp.exp(shard_cumul[:, -1]) * (note_ids[-1] == note_before)
    leave_rows = jnp.exp(shard_cumul[:, -1:] - shard_cumul) * (note_ids == note_ids[-1])
    entry_rows = jnp.exp(shard_cumul) * (note_ids == note_before)
    local_state = jnp.einsum(
        "thp,ht,tn->hpn", x_rows, leave_rows, v_bc[:, :N], precision=lax.Precision.HIGH,
        preferred_element_type=jnp.float32,
    )
    local_adjoint = jnp.einsum(
        "thp,ht,tn->hpn", g_rows, entry_rows, v_bc[:, N:], precision=lax.Precision.HIGH,
        preferred_element_type=jnp.float32,
    )
    state_in, adjoint_in = chain_both(local_state, local_adjoint, keep, "seq")

    def local_forward(x_all, b_all, c_all, log_all):
        return block_forward_all(
            state_in, x_all, b_all, c_all, log_all, note_blocks, befores
        )

    _, pull = jax.vjp(local_forward, x_heads, b_blocks, c_blocks, log_blocks)
    grad_x_heads, grad_b, grad_c, grad_log = pull((grad_heads, adjoint_in))
    grad_log_decay = grad_log.reshape(head_count, tok_rows)
    grad_v_x = grad_x_heads.transpose(1, 2, 0, 3).reshape(tok_rows, head_count * P_SIZE)
    grad_v_bc = jnp.concatenate([grad_b.reshape(tok_rows, N), grad_c.reshape(tok_rows, N)], axis=1)
    grad_u_x = grad_v_x * silu_slope(u_x)
    grad_u_bc = grad_v_bc * silu_slope(u_bc)
    after_bc = shifted(grad_u_bc[:rim_width], "seq", -1)
    after_x = shifted(grad_u_x[:rim_width], "seq", -1)
    grad_pre_x = conv_backward(jnp.concatenate([grad_u_x, after_x]), conv_x, note_all[rim_width:])
    bulk_bc = conv_backward(
        jnp.concatenate([grad_u_bc, jnp.zeros_like(after_bc)]), conv_bc, note_all[rim_width:]
    )
    tail_bc = conv_backward(
        jnp.concatenate([grad_u_bc[tok_rows - rim_width :], after_bc]),
        conv_bc,
        note_all[tok_rows : tok_rows + 2 * rim_width],
    )
    whole_bc = lax.dynamic_update_slice_in_dim(bulk_bc, tail_bc, tok_rows - rim_width, 0)
    chips, cores = lax.axis_size("chip"), lax.axis_size("core")
    pieces = whole_bc.reshape(chips, cores, tok_rows // (chips * cores), whole_bc.shape[1])
    core = lax.axis_index("core")
    mine = lax.dynamic_index_in_dim(pieces, core, 1, keepdims=False)
    other = lax.dynamic_index_in_dim(pieces, 1 - core, 1, keepdims=False)
    pair_sum = mine + lax.ppermute(other, "core", [(0, 1), (1, 0)])
    grad_pre_bc = lax.all_to_all(pair_sum, "chip", 0, 0, tiled=False).sum(0)
    return (grad_pre_x, grad_pre_bc, grad_log_decay)


def solution(mesh):
    seq_size, head_size = mesh.shape["seq"], mesh.shape["head"]
    split = jax.sharding.Mesh(
        mesh.devices.reshape(seq_size, head_size // 2, 2), ("seq", "chip", "core")
    )
    head = ("chip", "core")
    placed = (
        P("seq", head),
        P("seq", None),
        P(None, head),
        P(),
        P(head, "seq"),
        P(),
        P("seq", head),
    )
    return jax.shard_map(
        local,
        mesh=split,
        in_specs=placed,
        out_specs=(P("seq", head), P(("seq",) + head, None), P(head, "seq")),
        check_vma=False,
    )
```

```python
import jax
import jax.numpy as jnp
from jax import lax
from jax.sharding import PartitionSpec as P

P_SIZE = 64
N = 128
K = 4
BLOCK = 256


precise = lax.Precision.HIGHEST


def shifted(value, axis, steps):
    count = lax.axis_size(axis)
    initial, last = (max(0, -steps), min(count, count - steps))
    return lax.ppermute(value, axis, [(source, source + steps) for source in range(initial, last)])


def entering(value, axis, join, neutral, backward):
    count, mine = (lax.axis_size(axis), lax.axis_index(axis))
    pieces = jax.tree.map(lambda part: lax.all_gather(part, axis), value)
    if backward:
        pieces = jax.tree.map(lambda part: part[::-1], pieces)
        mine = count - 1 - mine
    total = jax.tree.map(
        lambda part, zero: jnp.full_like(part, 0) + jnp.asarray(zero, part.dtype), value, neutral
    )

    def hop(position, total):
        longer = join(total, jax.tree.map(lambda part: part[position], pieces))
        return jax.tree.map(lambda new, old: jnp.where(position < mine, new, old), longer, total)

    return lax.fori_loop(0, count - 1, hop, total)


def matmul(left, right):
    return jnp.dot(left, right, precision=precise, preferred_element_type=jnp.float32)


def note_index(positions, lengths):
    starts = jnp.cumsum(lengths) - lengths
    hits = (positions[:, None] >= starts[None, :]).astype(jnp.int32)
    return jnp.sum(hits, axis=1) - 1


def block_edges(log_block, note_block, note_before):
    cumul = jnp.cumsum(log_block)
    entry = jnp.exp(cumul) * (note_block == note_before)
    leave = jnp.exp(cumul[-1] - cumul) * (note_block == note_block[-1])
    through = jnp.exp(cumul[-1]) * (note_block[-1] == note_before)
    return (cumul, entry, leave, through)


def block_forward(state, x_block, b_block, c_block, log_block, note_block, note_before):
    cumul, entry, leave, through = block_edges(log_block, note_block, note_before)
    length = note_block.shape[0]
    lower = jnp.arange(length)[:, None] >= jnp.arange(length)[None, :]
    linked = lower & (note_block[:, None] == note_block[None, :])
    decay_matrix = jnp.exp(jnp.where(linked, cumul[:, None] - cumul[None, :], 0.0)) * linked
    scores = matmul(c_block, b_block.T) * decay_matrix
    output = matmul(scores, x_block) + entry[:, None] * matmul(c_block, state.T)
    updated = through * state + matmul((x_block * leave[:, None]).T, b_block)
    return (output, updated)


def head_forward(state, x_head, b_blocks, c_blocks, log_head, note_blocks, befores):

    def head_advance(carry, block):
        output, updated = block_forward(carry, *block)
        return (updated, output)

    final, outputs = lax.scan(
        head_advance, state, (x_head, b_blocks, c_blocks, log_head, note_blocks, befores)
    )
    return (outputs, final)


def conv_forward(extended, weights, note_ext):
    width = weights.shape[0]
    count = extended.shape[0] - width + 1
    result = jnp.zeros((count, extended.shape[1]), jnp.float32)
    for k in range(width):
        linked = note_ext[k : k + count] == note_ext[width - 1 : width - 1 + count]
        result = result + weights[k][None, :] * extended[k : k + count] * linked[:, None]
    return result


def conv_backward(extended, weights, note_ext):
    width = weights.shape[0]
    count = extended.shape[0] - width + 1
    result = jnp.zeros((count, extended.shape[1]), jnp.float32)
    for k in range(width):
        lag = width - 1 - k
        linked = note_ext[lag : lag + count] == note_ext[:count]
        result = result + weights[k][None, :] * extended[lag : lag + count] * linked[:, None]
    return result


def silu_slope(values):
    sigma = jax.nn.sigmoid(values)
    return sigma * (1.0 + values * (1.0 - sigma))


def chain_combine(earlier, later):
    return (earlier[0] * later[0], later[0][:, None, None] * earlier[1] + later[1])


def chain_in(value, keep, axis, direction):
    count = lax.axis_size(axis)
    packed = jnp.concatenate(
        [value.reshape(value.shape[0], -1), jnp.broadcast_to(keep[:, None], (keep.shape[0], 128))], axis=1
    )
    total = jnp.zeros_like(value)
    scale = jnp.ones_like(keep)
    for distance in range(1, count):
        arrived = shifted(packed, axis, direction * distance)
        part = arrived[:, : value[0].size].reshape(value.shape)
        total = total + scale[:, None, None] * part
        scale = scale * arrived[:, value[0].size]
    return total


def running_sum(values):
    length = values.shape[-1]
    upper = (jnp.arange(length)[:, None] <= jnp.arange(length)[None, :]).astype(values.dtype)
    return jnp.dot(values, upper, precision=precise, preferred_element_type=jnp.float32)


def chain_both(state, adjoint, keep, axis):
    count, mine = lax.axis_size(axis), lax.axis_index(axis)
    heads, size = state.shape[0], state[0].size
    tail = jnp.broadcast_to(keep[:, None], (heads, 128))
    later = jnp.concatenate([state.reshape(heads, size), tail], axis=1)
    earlier = jnp.concatenate([adjoint.reshape(heads, size), tail], axis=1)
    targets = jnp.arange(count)[:, None, None]
    outgoing = jnp.where(targets > mine, later[None], jnp.where(targets < mine, earlier[None], 0.0))
    arrived = lax.all_to_all(outgoing, axis, 0, 0, tiled=False)
    keeps = arrived[:, :, size]
    totals = []
    for order in (range(count - 1, -1, -1), range(count)):
        weights = [None] * count
        scale = jnp.ones_like(keep)
        for source in order:
            near = (source < mine) if order.step < 0 else (source > mine)
            weights[source] = jnp.where(near, scale, 0.0)
            scale = jnp.where(near, scale * keeps[source], scale)
        combined = jnp.sum(jnp.stack(weights)[:, :, None] * arrived, axis=0)
        totals.append(combined[:, :size].reshape(state.shape))
    return totals[0], totals[1]


def einsum(spec, *operands):
    return jnp.einsum(spec, *operands, precision=lax.Precision.HIGH, preferred_element_type=jnp.float32)


def block_forward_all(state, x_all, b_all, c_all, log_all, note_blocks, befores):
    cumul = running_sum(log_all)
    entry = jnp.exp(cumul) * (note_blocks == befores[:, None])
    leave = jnp.exp(cumul[..., -1:] - cumul) * (note_blocks == note_blocks[:, -1:])
    through = jnp.exp(cumul[..., -1]) * (note_blocks[:, -1] == befores)
    length = note_blocks.shape[1]
    lower = jnp.arange(length)[:, None] >= jnp.arange(length)[None, :]
    linked = lower & (note_blocks[:, :, None] == note_blocks[:, None, :])
    differences = cumul[..., :, None] - cumul[..., None, :]
    decay_matrix = jnp.exp(jnp.where(linked, differences, 0.0)) * linked
    scores = einsum("bin,bjn->bij", c_all, b_all) * decay_matrix
    output = einsum("hbij,hbjp->hbip", scores, x_all)
    chunk = einsum("hbjp,bjn->hbpn", x_all * leave[..., None], b_all)
    starts = []
    for block in range(note_blocks.shape[0]):
        starts.append(state)
        state = through[:, block, None, None] * state + chunk[:, block]
    output = output + entry[..., None] * einsum("bin,hbpn->hbip", c_all, jnp.stack(starts, axis=1))
    return (output, state)


def local(pre_x, pre_bc, conv_x, conv_bc, log_decay, lengths, grad_out):
    tok_rows = pre_x.shape[0]
    head_count = log_decay.shape[0]
    rim_width = K - 1
    block_count = tok_rows // BLOCK
    seq_start = lax.axis_index("seq") * tok_rows
    positions = seq_start + jnp.arange(-rim_width, tok_rows + rim_width)
    note_all = note_index(positions, lengths)
    note_ids = note_all[rim_width : rim_width + tok_rows]
    before_both = shifted(
        jnp.concatenate([pre_x[tok_rows - rim_width :], pre_bc[tok_rows - rim_width :]], axis=1), "seq", 1
    )
    before_x, before_bc = before_both[:, : pre_x.shape[1]], before_both[:, pre_x.shape[1] :]
    u_x = conv_forward(
        jnp.concatenate([before_x, pre_x]).astype(jnp.float32),
        conv_x,
        note_all[: tok_rows + rim_width],
    )
    u_bc = conv_forward(
        jnp.concatenate([before_bc, pre_bc]).astype(jnp.float32),
        conv_bc,
        note_all[: tok_rows + rim_width],
    )
    v_x = jax.nn.silu(u_x)
    v_bc = jax.nn.silu(u_bc)
    x_heads = v_x.reshape(block_count, BLOCK, head_count, P_SIZE).transpose(2, 0, 1, 3)
    b_blocks = v_bc[:, :N].reshape(block_count, BLOCK, N)
    c_blocks = v_bc[:, N:].reshape(block_count, BLOCK, N)
    log_blocks = log_decay.reshape(head_count, block_count, BLOCK)
    grad_heads = (
        grad_out.astype(jnp.float32)
        .reshape(block_count, BLOCK, head_count, P_SIZE)
        .transpose(2, 0, 1, 3)
    )
    note_blocks = note_ids.reshape(block_count, BLOCK)
    befores = jnp.concatenate([note_all[rim_width - 1 : rim_width], note_blocks[:-1, -1]])

    note_before = note_all[rim_width - 1]
    log_rows = log_decay.astype(jnp.float32)
    x_rows = v_x.reshape(tok_rows, head_count, P_SIZE)
    g_rows = grad_out.astype(jnp.float32).reshape(tok_rows, head_count, P_SIZE)
    block_cumul = running_sum(log_blocks)
    offsets = [jnp.zeros_like(block_cumul[:, 0, -1])]
    for block in range(block_count - 1):
        offsets.append(offsets[-1] + block_cumul[:, block, -1])
    shard_cumul = (block_cumul + jnp.stack(offsets, axis=1)[:, :, None]).reshape(head_count, tok_rows)
    keep = jnp.exp(shard_cumul[:, -1]) * (note_ids[-1] == note_before)
    leave_rows = jnp.exp(shard_cumul[:, -1:] - shard_cumul) * (note_ids == note_ids[-1])
    entry_rows = jnp.exp(shard_cumul) * (note_ids == note_before)
    local_state = jnp.einsum(
        "thp,ht,tn->hpn", x_rows, leave_rows, v_bc[:, :N], precision=lax.Precision.HIGH,
        preferred_element_type=jnp.float32,
    )
    local_adjoint = jnp.einsum(
        "thp,ht,tn->hpn", g_rows, entry_rows, v_bc[:, N:], precision=lax.Precision.HIGH,
        preferred_element_type=jnp.float32,
    )
    state_in, adjoint_in = chain_both(local_state, local_adjoint, keep, "seq")

    def local_forward(x_all, b_all, c_all, log_all):
        return block_forward_all(
            state_in, x_all, b_all, c_all, log_all, note_blocks, befores
        )

    _, pull = jax.vjp(local_forward, x_heads, b_blocks, c_blocks, log_blocks)
    grad_x_heads, grad_b, grad_c, grad_log = pull((grad_heads, adjoint_in))
    grad_log_decay = grad_log.reshape(head_count, tok_rows)
    grad_v_x = grad_x_heads.transpose(1, 2, 0, 3).reshape(tok_rows, head_count * P_SIZE)
    grad_v_bc = jnp.concatenate([grad_b.reshape(tok_rows, N), grad_c.reshape(tok_rows, N)], axis=1)
    grad_u_x = grad_v_x * silu_slope(u_x)
    grad_u_bc = grad_v_bc * silu_slope(u_bc)
    after_bc = shifted(grad_u_bc[:rim_width], "seq", -1)
    after_x = shifted(grad_u_x[:rim_width], "seq", -1)
    grad_pre_x = conv_backward(jnp.concatenate([grad_u_x, after_x]), conv_x, note_all[rim_width:])
    bulk_bc = conv_backward(
        jnp.concatenate([grad_u_bc, jnp.zeros_like(after_bc)]), conv_bc, note_all[rim_width:]
    )
    tail_bc = conv_backward(
        jnp.concatenate([grad_u_bc[tok_rows - rim_width :], after_bc]),
        conv_bc,
        note_all[tok_rows : tok_rows + 2 * rim_width],
    )
    whole_bc = jnp.concatenate([bulk_bc[: tok_rows - rim_width], tail_bc])
    chips, cores = lax.axis_size("chip"), lax.axis_size("core")
    pieces = whole_bc.reshape(chips, cores, tok_rows // (chips * cores), whole_bc.shape[1])
    core = lax.axis_index("core")
    mine = jnp.where(core == 0, pieces[:, 0], pieces[:, 1])
    other = jnp.where(core == 0, pieces[:, 1], pieces[:, 0])
    pair_sum = mine + lax.ppermute(other, "core", [(0, 1), (1, 0)])
    grad_pre_bc = lax.all_to_all(pair_sum, "chip", 0, 0, tiled=False).sum(0)
    return (grad_pre_x, grad_pre_bc, grad_log_decay)


def solution(mesh):
    seq_size, head_size = mesh.shape["seq"], mesh.shape["head"]
    split = jax.sharding.Mesh(
        mesh.devices.reshape(seq_size, head_size // 2, 2), ("seq", "chip", "core")
    )
    head = ("chip", "core")
    placed = (
        P("seq", head),
        P("seq", None),
        P(None, head),
        P(),
        P(head, "seq"),
        P(),
        P("seq", head),
    )
    return jax.shard_map(
        local,
        mesh=split,
        in_specs=placed,
        out_specs=(P("seq", head), P(("seq",) + head, None), P(head, "seq")),
        check_vma=False,
    )
```
